32 devices in a mesh: dp: 8 (over z, x), fsdp: 4 (over y, core).
Axes of the slice: x: 2, y: 2, z: 4, core: 2. Of those that a mesh axis runs over, the one named last changes fastest.
Arguments:
- tokens: bfloat16 [64, 1200, 512], P(('dp', 'fsdp')), may hold values from -6 to 6
- known_flags: int32 [64, 1200], P(('dp', 'fsdp')), may hold values 0 or 1
- query_proj: bfloat16 [512, 512], P('fsdp'), may hold values from -0.25 to 0.25
- query_bias: bfloat16 [512], P('fsdp'), may hold values from -3 to 3
- key_proj: bfloat16 [512, 512], P('fsdp'), may hold values from -0.25 to 0.25
- value_proj: bfloat16 [512, 512], P('fsdp'), may hold values from -0.25 to 0.25
- value_bias: bfloat16 [512], P('fsdp'), may hold values from -3 to 3
- out_proj: bfloat16 [512, 512], P('fsdp'), may hold values from -4 to 4
- out_bias: bfloat16 [512], P('fsdp'), may hold values from -3 to 3
- gain_first: bfloat16 [512], P('fsdp'), may hold values from 0.5 to 1.5
- shift_first: bfloat16 [512], P('fsdp'), may hold values from -3 to 3
- up_proj: bfloat16 [512, 512], P('fsdp'), may hold values from -0.25 to 0.25
- up_bias: bfloat16 [512], P('fsdp'), may hold values from -3 to 3
- down_proj: bfloat16 [512, 512], P('fsdp'), may hold values from -0.25 to 0.25
- down_bias: bfloat16 [512], P('fsdp'), may hold values from -3 to 3
- gain_second: bfloat16 [512], P('fsdp'), may hold values from 0.5 to 1.5
- shift_second: bfloat16 [512], P('fsdp'), may hold values from -3 to 3
- cotangent: bfloat16 [64, 1200, 512], P(('dp', 'fsdp')), may hold values from -6 to 6
Outputs:
- result: bfloat16 [64, 1200, 512], P(('dp', 'fsdp'))
- tokens_grad: bfloat16 [64, 1200, 512], P(('dp', 'fsdp'))
- query_proj_grad: float32 [512, 512], P('fsdp')
- query_bias_grad: float32 [512], P('fsdp')
- key_proj_grad: float32 [512, 512], P('fsdp')
- value_proj_grad: float32 [512, 512], P('fsdp')
- value_bias_grad: float32 [512], P('fsdp')
- out_proj_grad: float32 [512, 512], P('fsdp')
- out_bias_grad: float32 [512], P('fsdp')
- gain_first_grad: float32 [512], P('fsdp')
- shift_first_grad: float32 [512], P('fsdp')
- up_proj_grad: float32 [512, 512], P('fsdp')
- up_bias_grad: float32 [512], P('fsdp')
- down_proj_grad: float32 [512, 512], P('fsdp')
- down_bias_grad: float32 [512], P('fsdp')
- gain_second_grad: float32 [512], P('fsdp')
- shift_second_grad: float32 [512], P('fsdp')
The draws below stay inside these ranges and needn't reach their ends.
All inputs are finite; a program needn't handle non-finite values. No bound on the sum of `known_flags` on one device may be relied on, other than what follows from the above.
Results may differ from the reference program's by a relative error of at most 0.014.
Values may be sent and summed in bfloat16 or wider, within the bound.
No kernel may reach another device: no remote copies, remote signals or barrier semaphores. Data moves between devices by JAX's collectives and lax.ppermute only.
A program may use at most 128 MiB of HBM per device.

```python
import jax
import jax.numpy as jnp
from jax import lax

D = 512
H = 8
HD = 64
FF = 512
GENES = 1200
CELLS = 64


def place_ends(values, stream_key, smallest, top_value):
    extent = values.shape
    place = [jax.random.randint(jax.random.fold_in(stream_key, axis), (), 0, extent[axis]) for axis in range(len(extent))]
    values = values.at[tuple(place)].set(smallest)
    longest = extent.index(max(extent))
    place[longest] = (place[longest] + 1) % extent[longest]
    return values.at[tuple(place)].set(top_value)


def spiked(drawn, stream_key, source, target, parts, factor):
    owner, partner = [(jnp.arange(drawn.shape[axis_at]) // (drawn.shape[axis_at] // parts)).reshape([-1 if axis == axis_at else 1 for axis in range(drawn.ndim)]) for axis_at in (source, target)]
    chosen = jax.random.permutation(stream_key, parts)[partner]
    strong = (owner == chosen) | (owner == (partner + parts // 2) % parts)
    return jnp.where(strong, factor * drawn, drawn)


def block_scale(own_key, dims, cuts, low, high):
    def one(axis_at, blocks):
        steps = jax.random.uniform(jax.random.fold_in(jax.random.fold_in(own_key, 6), axis_at), (blocks,), jnp.float32, low / len(cuts), high / len(cuts))
        return jnp.repeat(jnp.exp(steps), dims[axis_at] // blocks).reshape((-1,) + (1,) * (len(dims) - axis_at - 1))

    level = one(*cuts[0])
    for cut in cuts[1:]:
        level = level * one(*cut)
    return level


def noise(rng, dims, spread, reach, split=(), held_as=jnp.bfloat16):
    entries = jax.random.normal(rng, dims, jnp.float32) * spread
    if len(split) > 0:
        entries = block_scale(rng, dims, split, -0.22, 0.18) * entries
    return jnp.clip(entries, min=-reach, max=reach).astype(held_as)


def noise_with(own_key, extent, deviation, limit, pieces, heavy, dtype=jnp.bfloat16):
    drawn = deviation * jax.random.normal(own_key, extent, jnp.float32)
    if pieces:
        drawn = drawn * block_scale(own_key, extent, pieces, -0.22, 0.18)
    return jnp.clip(spiked(drawn, jax.random.fold_in(own_key, 3), *heavy), -limit, limit).astype(dtype)


def setup_inputs(seed: int = 0) -> dict:
    arg_keys = jax.random.split(jax.random.key(seed), 19)
    tokens = noise(arg_keys[0], (CELLS, GENES, D), 1.0, 6.0, ((0, 32),))
    known_flags = place_ends((jax.random.randint(arg_keys[1], (CELLS, GENES), 0, 2) < 1).astype(jnp.int32), jax.random.fold_in(arg_keys[1], 1), 0, 1)
    query_proj = noise(arg_keys[2], (D, D), D ** -0.5, 0.25, ((0, 4),))
    query_bias = noise(arg_keys[3], (D,), 0.5, 3.0, ((0, 4),))
    key_proj = noise(arg_keys[4], (D, D), D ** -0.5, 0.25, ((0, 4),))
    value_proj = noise(arg_keys[5], (D, D), D ** -0.5, 0.25, ((0, 4),))
    value_bias = noise(arg_keys[6], (D,), 0.5, 3.0, ((0, 4),))
    out_proj = noise(arg_keys[7], (D, D), 2 ** -0.5, 4.0, ((0, 4),))
    out_bias = noise(arg_keys[8], (D,), 0.5, 3.0, ((0, 4),))
    gain_first = jnp.clip(0.5 + 1.0 * jax.random.uniform(arg_keys[9], (D,), jnp.float32) ** block_scale(arg_keys[9], (D,), ((0, 4),), -0.2, 0.2), 0.5, 1.5).astype(jnp.bfloat16)
    shift_first = noise(arg_keys[10], (D,), 0.5, 3.0, ((0, 4),))
    up_proj = noise(arg_keys[11], (D, FF), D ** -0.5, 0.25, ((0, 4),))
    up_bias = noise(arg_keys[12], (FF,), 0.5, 3.0, ((0, 4),))
    down_proj = noise(arg_keys[13], (FF, D), FF ** -0.5, 0.25, ((0, 4),))
    down_bias = noise(arg_keys[14], (D,), 0.5, 3.0, ((0, 4),))
    gain_second = jnp.clip(0.5 + 1.0 * jax.random.uniform(arg_keys[15], (D,), jnp.float32) ** block_scale(arg_keys[15], (D,), ((0, 4),), -0.2, 0.2), 0.5, 1.5).astype(jnp.bfloat16)
    shift_second = noise(arg_keys[16], (D,), 0.5, 3.0, ((0, 4),))
    cotangent = noise_with(arg_keys[17], (CELLS, GENES, D), 1.0, 6.0, ((0, 32),), (0, 2, 32, 2.75))
    return dict(tokens=tokens, known_flags=known_flags, query_proj=query_proj, query_bias=query_bias, key_proj=key_proj, value_proj=value_proj, value_bias=value_bias, out_proj=out_proj, out_bias=out_bias, gain_first=gain_first, shift_first=shift_first, up_proj=up_proj, up_bias=up_bias, down_proj=down_proj, down_bias=down_bias, gain_second=gain_second, shift_second=shift_second, cotangent=cotangent)


@jax.custom_vjp
def low(v):
    return lax.optimization_barrier(v.astype(jnp.bfloat16)).astype(jnp.float32)

@jax.custom_vjp
def low_back(v):
    return v

def low_keep(v):
    return (low(v), None)

def low_pass(kept, grad):
    return (grad,)

def back_keep(v):
    return (v, None)

def back_low(kept, grad):
    return (low(grad),)
low.defvjp(low_keep, low_pass)
low_back.defvjp(back_keep, back_low)
NORM_EPSILON = 1e-05
MASK_FILL = -1e+30

def norm_rows(rows_in, gain, shift):
    row_mean = lax.optimization_barrier(jnp.mean(rows_in, axis=-1, keepdims=True))
    centred = rows_in - row_mean
    row_var = lax.optimization_barrier(jnp.mean(centred * centred, axis=-1, keepdims=True))
    return centred * lax.rsqrt(row_var + NORM_EPSILON) * gain + shift

def matmul(left, right):
    return jnp.dot(left, right, precision=lax.Precision.HIGHEST)

def cell_layer(weights_all, cell_rows, known_row):
    query_proj, query_bias, key_proj, value_proj, value_bias, out_proj, out_bias, gain_first, shift_first, up_proj, up_bias, down_proj, down_bias, gain_second, shift_second = weights_all
    queries = low(low_back(matmul(cell_rows, query_proj) + query_bias))
    keys_all = low(low_back(matmul(cell_rows, key_proj)))
    values_all = low(low_back(matmul(cell_rows, value_proj) + value_bias))
    head_query = queries.reshape(GENES, H, HD)
    head_keys = keys_all.reshape(GENES, H, HD)
    head_values = values_all.reshape(GENES, H, HD)
    raw_scores = jnp.einsum('qhd,khd->hqk', head_query, head_keys, precision=lax.Precision.HIGHEST)
    scores = low_back(raw_scores) * HD ** (-0.5)
    places = jnp.arange(GENES)
    allowed = (known_row[None, :] > 0) | (places[:, None] == places[None, :])
    scores = jnp.where(allowed[None, :, :], scores, MASK_FILL)
    attn_prob = jax.nn.softmax(scores, axis=-1)
    attended = jnp.einsum('hqk,khd->qhd', low(attn_prob), head_values, precision=lax.Precision.HIGHEST)
    attended = low(low_back(attended.reshape(GENES, D)))
    attn_out = low_back(matmul(attended, out_proj) + out_bias)
    first_norm = norm_rows(cell_rows + attn_out, gain_first, shift_first)
    pre_act = low_back(matmul(low(first_norm), up_proj) + up_bias)
    activated = low(jax.nn.gelu(pre_act, approximate=False))
    ff_out = low_back(matmul(activated, down_proj) + down_bias)
    return norm_rows(first_norm + ff_out, gain_second, shift_second)

def reference(tokens, known_flags, query_proj, query_bias, key_proj, value_proj, value_bias, out_proj, out_bias, gain_first, shift_first, up_proj, up_bias, down_proj, down_bias, gain_second, shift_second, cotangent):
    weights_all = tuple((p.astype(jnp.float32) for p in (query_proj, query_bias, key_proj, value_proj, value_bias, out_proj, out_bias, gain_first, shift_first, up_proj, up_bias, down_proj, down_bias, gain_second, shift_second)))
    cell_input = tokens.astype(jnp.float32)

    def forward(cells_in, weights_in):
        one_cell = jax.checkpoint(lambda cell_rows, known_row: cell_layer(weights_in, cell_rows, known_row))

        def scan_step(carry, items):
            return (carry, one_cell(items[0], items[1]))
        carry_end, stacked = lax.scan(scan_step, jnp.zeros((), jnp.float32), (cells_in, known_flags))
        return stacked
    result, pull_back = jax.vjp(forward, cell_input, weights_all)
    grad_cells, grads = pull_back(cotangent.astype(jnp.float32))
    return (result.astype(jnp.bfloat16), grad_cells.astype(jnp.bfloat16), grads[0], grads[1], grads[2], grads[3], grads[4], grads[5], grads[6], grads[7], grads[8], grads[9], grads[10], grads[11], grads[12], grads[13], grads[14])
```

```python
import functools

import jax
import jax.numpy as jnp
from jax import lax
from jax.experimental import pallas as pl
from jax.experimental.pallas import tpu as pltpu
from jax.sharding import PartitionSpec as P

H = 8
HD = 64
SCALE = HD ** (-0.5)
NORM_EPSILON = 1e-05
MASK_FILL = -1e30

CHUNK = 336
ROWS = 480
ONES = 16
LANES = 128

F32 = jnp.float32
BF16 = jnp.bfloat16
MEBI = 1 << 20


def dot(left, right, left_dim=1, right_dim=0):
    return lax.dot_general(
        left, right, (((left_dim,), (right_dim,)), ((), ())), preferred_element_type=F32
    )


def chunk_rows(chunk):
    return pl.ds(pl.multiple_of(chunk * CHUNK, 16), CHUNK)


def pair_rows(pair, offset=0, size=LANES):
    return pl.ds(pl.multiple_of(pair * LANES + offset, HD), size)


def chunk_count(known):
    return (known + CHUNK - 1) // CHUNK


def gather_kernel(known_ref, flags_ref, x_ref, xc_ref, xt_ref, pos_ref):
    known = known_ref[pl.program_id(0)]
    length = x_ref.shape[1]
    flagged = flags_ref[0] > 0
    before = lax.broadcasted_iota(jnp.int32, (length, length), 0)
    after = lax.broadcasted_iota(jnp.int32, (length, length), 1)
    upper = jnp.where(before <= after, 1.0, 0.0).astype(BF16)
    marks = jnp.broadcast_to(jnp.where(flagged, 1.0, 0.0), (16, length)).astype(BF16)
    place = dot(marks, upper)[0:1, :].astype(jnp.int32) - 1
    place = jnp.where(flagged, place, -1)
    pos_ref[0] = place

    def one_chunk(chunk, carry):
        target = chunk * CHUNK + lax.broadcasted_iota(jnp.int32, (CHUNK, length), 0)
        target = jnp.minimum(target, known - 1)
        chosen = jnp.where(place == target, 1.0, 0.0).astype(BF16)
        xc_ref[0, chunk_rows(chunk), :] = dot(chosen, x_ref[0]).astype(BF16)
        return carry

    lax.fori_loop(0, chunk_count(known), one_chunk, 0)
    width = x_ref.shape[2]
    xt_ref[0, 0:width, :] = x_ref[0].T
    xt_ref[0, width:, :] = jnp.ones((ONES, length), BF16)


def gather_known(known, flags, x):
    cells, length, width = x.shape
    padded = -(-length // CHUNK) * CHUNK
    one = lambda *shape: pl.BlockSpec((1,) + shape, lambda i, known: (i, 0, 0))
    return pl.pallas_call(
        gather_kernel,
        out_shape=(
            jax.ShapeDtypeStruct((cells, padded, width), BF16),
            jax.ShapeDtypeStruct((cells, width + ONES, length), BF16),
            jax.ShapeDtypeStruct((cells, 1, length), jnp.int32),
        ),
        grid_spec=pltpu.PrefetchScalarGridSpec(
            num_scalar_prefetch=1,
            grid=(cells,),
            in_specs=[one(1, length), one(length, width)],
            out_specs=[one(padded, width), one(width + ONES, length), one(1, length)],
        ),
        compiler_params=pltpu.CompilerParams(vmem_limit_bytes=60 * MEBI),
        name="gather_known",
    )(known, flags, x)


def attend_kernel(
    known_ref, xt_ref, xc_ref, pos_ref, wq_ref, wk_ref, wv_ref, bq_ref, bv_ref, bv_row_ref,
    qt_ref, kt_ref, vt_ref, kc_ref, vc_ref, ot_ref, o_ref, lse_ref,
    vct, qz, top, acc,
):
    known = known_ref[pl.program_id(0)]
    width, length = qt_ref.shape[1], qt_ref.shape[2]
    pairs = width // LANES
    steps = chunk_count(known)
    hidden = pos_ref[0] < 0

    xt = xt_ref[0, 0:width, :]
    qt_ref[0] = (dot(wq_ref[...], xt, 0, 0) + bq_ref[...]).astype(BF16)
    kt_ref[0] = dot(wk_ref[...], xt, 0, 0).astype(BF16)
    vt_ref[0] = (dot(wv_ref[...], xt, 0, 0) + bv_ref[...]).astype(BF16)

    def project(chunk, carry):
        rows = chunk_rows(chunk)
        xc = xc_ref[0, rows, :]
        keys = dot(xc, wk_ref[...]).astype(BF16)
        values = dot(xc, wv_ref[...]) + bv_row_ref[...]
        for pair in range(pairs):
            cols = slice(pair * LANES, (pair + 1) * LANES)
            kc_ref[0, pair, rows, :] = keys[:, cols]
            vc_ref[0, pair, rows, :] = values[:, cols].astype(BF16)
        row = chunk * CHUNK + lax.broadcasted_iota(jnp.int32, (CHUNK, width), 0)
        held = jnp.where(row < known, values, 0.0).astype(BF16).T
        row = chunk * CHUNK + lax.broadcasted_iota(jnp.int32, (16, CHUNK), 1)
        valid = jnp.where(row < known, 1.0, 0.0).astype(BF16)
        for head in range(width // HD):
            vct[chunk, head, 0:HD, :] = held[head * HD : (head + 1) * HD, :]
            vct[chunk, head, HD:, :] = valid
        return carry

    lax.fori_loop(0, steps, project, 0)

    def one_pair(pair, carry):
        low = lax.broadcasted_iota(jnp.int32, (LANES, length), 0) < HD
        scaled = qt_ref[0, pair_rows(pair), :].astype(F32) * SCALE
        qz[0] = jnp.where(low, scaled, 0.0).astype(BF16)
        qz[1] = jnp.where(low, 0.0, scaled).astype(BF16)
        for side in range(2):
            rows = pair_rows(pair, side * HD, HD)
            own = jnp.sum(
                qt_ref[0, rows, :].astype(F32) * kt_ref[0, rows, :].astype(F32),
                axis=0,
                keepdims=True,
            )
            top[side] = jnp.where(hidden, own * SCALE, MASK_FILL)
            acc[side, 0:HD, :] = jnp.where(hidden, vt_ref[0, rows, :].astype(F32), 0.0)
            acc[side, HD:, :] = jnp.broadcast_to(jnp.where(hidden, 1.0, 0.0), (16, length))

        def one_chunk(chunk, carry):
            keys = kc_ref[0, pair, chunk_rows(chunk), :]
            for side in range(2):
                scores = dot(keys, qz[side])
                peak = jnp.maximum(top[side], jnp.max(scores, axis=0, keepdims=True))
                probs = jnp.exp(scores - peak).astype(BF16)
                fade = jnp.exp(top[side] - peak)
                acc[side] = acc[side] * fade + dot(vct[chunk, 2 * pair + side], probs)
                top[side] = peak
            return carry

        lax.fori_loop(0, steps, one_chunk, 0)
        for side in range(2):
            total = acc[side, HD : HD + 1, :]
            ot_ref[0, pair_rows(pair, side * HD, HD), :] = (acc[side, 0:HD, :] / total).astype(BF16)
            lse_ref[0, 2 * pair + side] = top[side] + jnp.log(total)
        return carry

    lax.fori_loop(0, pairs, one_pair, 0)
    o_ref[0] = ot_ref[0].T


def attend(known, xt, xc, pos, wq, wk, wv, bq, bv, bv_row):
    cells, length = xt.shape[0], xt.shape[2]
    width = xt.shape[1] - ONES
    padded = xc.shape[1]
    pairs = width // LANES
    one = lambda *shape: pl.BlockSpec((1,) + shape, lambda i, known: (i,) + (0,) * len(shape))
    full = lambda *shape: pl.BlockSpec(shape, lambda i, known: (0,) * len(shape))
    turned = jax.ShapeDtypeStruct((cells, width, length), BF16)
    packed = jax.ShapeDtypeStruct((cells, pairs, padded, LANES), BF16)
    return pl.pallas_call(
        attend_kernel,
        out_shape=(
            turned, turned, turned, packed, packed, turned,
            jax.ShapeDtypeStruct((cells, length, width), BF16),
            jax.ShapeDtypeStruct((cells, H, 1, length), F32),
        ),
        grid_spec=pltpu.PrefetchScalarGridSpec(
            num_scalar_prefetch=1,
            grid=(cells,),
            in_specs=[
                one(width + ONES, length), one(padded, width), one(1, length),
                full(width, width), full(width, width), full(width, width),
                full(width, 1), full(width, 1), full(1, width),
            ],
            out_specs=[
                one(width, length), one(width, length), one(width, length),
                one(pairs, padded, LANES), one(pairs, padded, LANES),
                one(width, length), one(length, width), one(H, 1, length),
            ],
            scratch_shapes=[
                pltpu.VMEM((padded // CHUNK, H, HD + 16, CHUNK), BF16),
                pltpu.VMEM((2, LANES, length), BF16),
                pltpu.VMEM((2, 1, length), F32),
                pltpu.VMEM((2, HD + 16, length), F32),
            ],
        ),
        compiler_params=pltpu.CompilerParams(vmem_limit_bytes=60 * MEBI),
        name="attend",
    )(known, xt, xc, pos, wq, wk, wv, bq, bv, bv_row)


def row_mean(rows):
    return jnp.mean(rows, axis=-1, keepdims=True)


def normalize(rows):
    centred = rows - row_mean(rows)
    scale = lax.rsqrt(row_mean(centred * centred) + NORM_EPSILON)
    return centred * scale, scale


def norm_back(grad, normed, scale):
    return scale * (grad - row_mean(grad) - normed * row_mean(grad * normed))


def column_sum(rows):
    return jnp.sum(rows, axis=0, keepdims=True)


def middle_kernel(
    x_ref, o_ref, cot_ref, wo_ref, wu_ref, wd_ref, vec_ref,
    result_ref, dhid_ref, datt_ref, go_ref, gu_ref, gd_ref, gvec_ref,
):
    @pl.when(pl.program_id(0) == 0)
    def _():
        go_ref[...] = jnp.zeros_like(go_ref)
        gu_ref[...] = jnp.zeros_like(gu_ref)
        gd_ref[...] = jnp.zeros_like(gd_ref)
        gvec_ref[...] = jnp.zeros_like(gvec_ref)

    out_bias, gain_one, shift_one = vec_ref[0:1, :], vec_ref[1:2, :], vec_ref[2:3, :]
    up_bias, down_bias = vec_ref[3:4, :], vec_ref[4:5, :]
    gain_two, shift_two = vec_ref[5:6, :], vec_ref[6:7, :]
    attended = o_ref[...]
    first_in = x_ref[...].astype(F32) + (dot(attended, wo_ref[...]) + out_bias)
    norm_one, scale_one = normalize(first_in)
    first_norm = norm_one * gain_one + shift_one
    first_low = first_norm.astype(BF16)
    pre_act = dot(first_low, wu_ref[...]) + up_bias
    below = 0.5 * (1.0 + lax.erf(pre_act * (0.5**0.5)))
    activated = (pre_act * below).astype(BF16)
    slope = below + pre_act * (jnp.exp(-0.5 * pre_act * pre_act) * 0.3989422804014327)
    second_in = first_norm + (dot(activated, wd_ref[...]) + down_bias)
    norm_two, scale_two = normalize(second_in)
    result_ref[...] = (norm_two * gain_two + shift_two).astype(BF16)

    dy = cot_ref[...].astype(F32)
    d_second = norm_back(dy * gain_two, norm_two, scale_two)
    d_ff = d_second.astype(BF16)
    gd_ref[...] += dot(activated, d_ff, 0, 0)
    d_pre = (dot(d_ff, wd_ref[...], 1, 1) * slope).astype(BF16)
    gu_ref[...] += dot(first_low, d_pre, 0, 0)
    d_first = d_second + dot(d_pre, wu_ref[...], 1, 1)
    d_hidden = norm_back(d_first * gain_one, norm_one, scale_one)
    d_attn = d_hidden.astype(BF16)
    go_ref[...] += dot(attended, d_attn, 0, 0)
    dhid_ref[...] = d_attn
    datt_ref[...] = dot(d_attn, wo_ref[...], 1, 1).astype(BF16)
    gvec_ref[0:1, :] += column_sum(d_attn.astype(F32))
    gvec_ref[1:2, :] += column_sum(d_first * norm_one)
    gvec_ref[2:3, :] += column_sum(d_first)
    gvec_ref[3:4, :] += column_sum(d_pre.astype(F32))
    gvec_ref[4:5, :] += column_sum(d_ff.astype(F32))
    gvec_ref[5:6, :] += column_sum(dy * norm_two)
    gvec_ref[6:7, :] += column_sum(dy)


def middle(x, o, cot, wo, wu, wd, vectors):
    rows, width = x.shape
    step = ROWS if rows % ROWS == 0 else rows
    block = pl.BlockSpec((step, width), lambda i: (i, 0))
    full = lambda *shape: pl.BlockSpec(shape, lambda i: (0,) * len(shape))
    low = jax.ShapeDtypeStruct((rows, width), BF16)
    square = jax.ShapeDtypeStruct((width, width), F32)
    return pl.pallas_call(
        middle_kernel,
        out_shape=(low, low, low, square, square, square, jax.ShapeDtypeStruct((8, width), F32)),
        grid=(rows // step,),
        in_specs=[block, block, block] + [full(width, width)] * 3 + [full(8, width)],
        out_specs=[block, block, block] + [full(width, width)] * 3 + [full(8, width)],
        compiler_params=pltpu.CompilerParams(vmem_limit_bytes=60 * MEBI),
        name="middle",
    )(x, o, cot, wo, wu, wd, vectors)


def back_kernel(
    known_ref, pos_ref, xt_ref, qt_ref, kt_ref, vt_ref, kc_ref, vc_ref, ot_ref, lse_ref,
    datt_ref, dhid_ref, wq_ref, wk_ref, wv_ref,
    tg_ref, gq_ref, gk_ref, gv_ref, gvec_ref,
    dot_t, hot, kct, qz, oz, dqa, dkv, delta, dt,
):
    @pl.when(pl.program_id(0) == 0)
    def _():
        gq_ref[...] = jnp.zeros_like(gq_ref)
        gk_ref[...] = jnp.zeros_like(gk_ref)
        gv_ref[...] = jnp.zeros_like(gv_ref)
        gvec_ref[...] = jnp.zeros_like(gvec_ref)

    known = known_ref[pl.program_id(0)]
    width, length = qt_ref.shape[1], qt_ref.shape[2]
    pairs = width // LANES
    steps = chunk_count(known)
    place = pos_ref[0]
    hidden = place < 0
    dot_t[...] = datt_ref[0].T

    def prepare(chunk, carry):
        row = chunk * CHUNK + lax.broadcasted_iota(jnp.int32, (CHUNK, length), 0)
        hot[chunk] = jnp.where(place == row, 1.0, 0.0).astype(BF16)
        row = chunk * CHUNK + lax.broadcasted_iota(jnp.int32, (CHUNK, LANES), 0)
        for pair in range(pairs):
            keys = kc_ref[0, pair, chunk_rows(chunk), :].astype(F32)
            keys = jnp.where(row < known, keys, 0.0).astype(BF16)
            kct[chunk, pair * LANES : (pair + 1) * LANES, :] = keys.T
        return carry

    lax.fori_loop(0, steps, prepare, 0)

    def one_pair(pair, carry):
        low = lax.broadcasted_iota(jnp.int32, (LANES, length), 0) < HD
        scaled = qt_ref[0, pair_rows(pair), :].astype(F32) * SCALE
        qz[0] = jnp.where(low, scaled, 0.0).astype(BF16)
        qz[1] = jnp.where(low, 0.0, scaled).astype(BF16)
        grads = dot_t[pair_rows(pair), :].astype(F32)
        oz[0] = jnp.where(low, grads, 0.0).astype(BF16)
        oz[1] = jnp.where(low, 0.0, grads).astype(BF16)
        for side in range(2):
            rows = pair_rows(pair, side * HD, HD)
            base = side * HD
            query = qt_ref[0, rows, :].astype(F32) * SCALE
            key = kt_ref[0, rows, :].astype(F32)
            grad = dot_t[rows, :].astype(F32)
            delta_row = jnp.sum(grad * ot_ref[0, rows, :].astype(F32), axis=0, keepdims=True)
            delta[side] = delta_row
            own = jnp.sum(query * key, axis=0, keepdims=True)
            prob = jnp.exp(jnp.where(hidden, own, MASK_FILL) - lse_ref[0, 2 * pair + side])
            own_grad = jnp.sum(grad * vt_ref[0, rows, :].astype(F32), axis=0, keepdims=True)
            back = (prob * (own_grad - delta_row)).astype(BF16).astype(F32)
            dqa[base : base + HD, :] = back * key
            dkv[base : base + HD, :] = back * query
            dkv[LANES + base : LANES + base + HD, :] = prob.astype(BF16).astype(F32) * grad

        def one_chunk(chunk, carry):
            rows = chunk_rows(chunk)
            keys = kc_ref[0, pair, rows, :]
            values = vc_ref[0, pair, rows, :]
            d_keys = jnp.zeros((CHUNK, LANES), F32)
            d_values = jnp.zeros((CHUNK, LANES), F32)
            for side in range(2):
                base = side * HD
                probs = jnp.exp(dot(keys, qz[side]) - lse_ref[0, 2 * pair + side])
                d_scores = (probs * (dot(values, oz[side]) - delta[side])).astype(BF16)
                d_values += dot(probs.astype(BF16), oz[side], 1, 1)
                d_keys += dot(d_scores, qz[side], 1, 1)
                head = kct[chunk, pair_rows(pair, base, HD), :]
                dqa[base : base + HD, :] += dot(head, d_scores)
            both = jnp.concatenate([d_keys, d_values], axis=1).astype(BF16)
            dkv[...] += dot(both, hot[chunk], 0, 0)
            return carry

        lax.fori_loop(0, steps, one_chunk, 0)
        dt[pair_rows(pair), :] = (dqa[...] * SCALE).astype(BF16)
        dt[pl.ds(pl.multiple_of(width + pair * LANES, LANES), LANES), :] = dkv[0:LANES, :].astype(BF16)
        dt[pl.ds(pl.multiple_of(2 * width + pair * LANES, LANES), LANES), :] = dkv[LANES:, :].astype(BF16)
        return carry

    lax.fori_loop(0, pairs, one_pair, 0)

    xt = xt_ref[0]
    for which, grad_ref in enumerate((gq_ref, gk_ref, gv_ref)):
        part = dot(xt, dt[which * width : (which + 1) * width, :], 1, 1)
        grad_ref[...] += part[0:width, :]
        if which != 1:
            gvec_ref[which : which + 1, :] += part[width : width + 1, :]
    back = (
        dot(wq_ref[...], dt[0:width, :])
        + dot(wk_ref[...], dt[width : 2 * width, :])
        + dot(wv_ref[...], dt[2 * width :, :])
    )
    tg_ref[0] = (back.T + dhid_ref[0].astype(F32)).astype(BF16)


def attend_back(known, pos, xt, qt, kt, vt, kc, vc, ot, lse, datt, dhid, wq, wk, wv):
    cells, width, length = qt.shape
    pairs, padded = kc.shape[1], kc.shape[2]
    one = lambda *shape: pl.BlockSpec((1,) + shape, lambda i, known: (i,) + (0,) * len(shape))
    full = lambda *shape: pl.BlockSpec(shape, lambda i, known: (0,) * len(shape))
    turned = one(width, length)
    square = jax.ShapeDtypeStruct((width, width), F32)
    return pl.pallas_call(
        back_kernel,
        out_shape=(
            jax.ShapeDtypeStruct((cells, length, width), BF16),
            square, square, square, jax.ShapeDtypeStruct((8, width), F32),
        ),
        grid_spec=pltpu.PrefetchScalarGridSpec(
            num_scalar_prefetch=1,
            grid=(cells,),
            in_specs=[
                one(1, length), one(width + ONES, length), turned, turned, turned,
                one(pairs, padded, LANES), one(pairs, padded, LANES), turned, one(H, 1, length),
                one(length, width), one(length, width),
                full(width, width), full(width, width), full(width, width),
            ],
            out_specs=[one(length, width)] + [full(width, width)] * 3 + [full(8, width)],
            scratch_shapes=[
                pltpu.VMEM((width, length), BF16),
                pltpu.VMEM((padded // CHUNK, CHUNK, length), BF16),
                pltpu.VMEM((padded // CHUNK, width, CHUNK), BF16),
                pltpu.VMEM((2, LANES, length), BF16),
                pltpu.VMEM((2, LANES, length), BF16),
                pltpu.VMEM((LANES, length), F32),
                pltpu.VMEM((2 * LANES, length), F32),
                pltpu.VMEM((2, 1, length), F32),
                pltpu.VMEM((3 * width, length), BF16),
            ],
        ),
        compiler_params=pltpu.CompilerParams(vmem_limit_bytes=60 * MEBI),
        name="attend_back",
    )(known, pos, xt, qt, kt, vt, kc, vc, ot, lse, datt, dhid, wq, wk, wv)


def layer(tokens, known_flags, cotangent, squares, vectors):
    wq, wk, wv, wo, wu, wd = squares
    bq, bv, bo, g1, s1, bu, bd, g2, s2 = [v.astype(F32) for v in vectors]
    cells, length, width = tokens.shape
    known = jnp.sum((known_flags > 0).astype(jnp.int32), axis=1)
    xc, xt, pos = gather_known(known, known_flags.reshape(cells, 1, length), tokens)
    qt, kt, vt, kc, vc, ot, o, lse = attend(
        known, xt, xc, pos, wq, wk, wv, bq.reshape(-1, 1), bv.reshape(-1, 1), bv.reshape(1, -1)
    )
    flat = lambda a: a.reshape(cells * length, width)
    rows = jnp.stack([bo, g1, s1, bu, bd, g2, s2, jnp.zeros_like(bo)])
    result, dhid, datt, go, gu, gd, gmid = middle(
        flat(tokens), flat(o), flat(cotangent), wo, wu, wd, rows
    )
    cube = lambda a: a.reshape(cells, length, width)
    tg, gq, gk, gv, gatt = attend_back(
        known, pos, xt, qt, kt, vt, kc, vc, ot, lse, cube(datt), cube(dhid), wq, wk, wv
    )
    return cube(result), tg, (gq, gk, gv, go, gu, gd), (
        gatt[0], gatt[2], gmid[0], gmid[1], gmid[2], gmid[3], gmid[4], gmid[5], gmid[6]
    )


SQUARES = (2, 4, 5, 7, 11, 13)
VECTORS = (3, 6, 8, 9, 10, 12, 14, 15, 16)


def body(*args):
    squares = [lax.all_gather(args[i], "fsdp", axis=0, tiled=True) for i in SQUARES]
    vectors = [lax.all_gather(args[i], "fsdp", axis=0, tiled=True) for i in VECTORS]
    result, tg, gs, gv = layer(args[0], args[1], args[17], squares, vectors)
    out = {}
    for i, g in list(zip(SQUARES, gs)) + list(zip(VECTORS, gv)):
        out[i] = lax.psum(lax.psum_scatter(g, "fsdp", scatter_dimension=0, tiled=True), "dp")
    return (result, tg) + tuple(out[i] for i in range(2, 17))


def solution(mesh):
    cells = P(("dp", "fsdp"), None, None)
    specs = tuple(P("fsdp", None) if i in SQUARES else P("fsdp") for i in range(2, 17))
    return jax.shard_map(
        body,
        mesh=mesh,
        in_specs=(cells, P(("dp", "fsdp"), None)) + specs + (cells,),
        out_specs=(cells, cells) + specs,
        check_vma=False,
    )
```

```python
import functools

import jax
import jax.numpy as jnp
from jax import lax
from jax.experimental import pallas as pl
from jax.experimental.pallas import tpu as pltpu
from jax.sharding import PartitionSpec as P

H = 8
HD = 64
SCALE = HD ** (-0.5)
NORM_EPSILON = 1e-05
MASK_FILL = -1e30
SAFE_SCORE = 50.0

CHUNK = 672
ROWS = 480
ONES = 16
EXTRA = 16
LANES = 128
TRIPLE = 3 * LANES
GROUPS = ((0, 2), (2, 2))

F32 = jnp.float32
BF16 = jnp.bfloat16
VMEM_LIMIT = 60 << 20

SQUARES = (2, 4, 5, 7, 11, 13)
VECTORS = (3, 6, 8, 9, 10, 12, 14, 15, 16)
MIDDLE_VECTORS = 7


def dot(left, right, left_dim=1, right_dim=0):
    return lax.dot_general(
        left, right, (((left_dim,), (right_dim,)), ((), ())), preferred_element_type=F32
    )


def params():
    return pltpu.CompilerParams(vmem_limit_bytes=VMEM_LIMIT)


def cost(flops, moved):
    return pl.CostEstimate(flops=int(flops), bytes_accessed=int(moved), transcendentals=0)


def offsets(shards):
    held, mask = [0], shards // 2
    while mask:
        held = held + [offset ^ mask for offset in held]
        mask //= 2
    return held


def gather_kernel(scalars_ref, flags_ref, x_ref, xc_ref, xt_ref, pos_ref):
    known = scalars_ref[pl.program_id(0)]
    length, width = x_ref.shape[1], x_ref.shape[2]
    flagged = flags_ref[0] > 0
    before = lax.broadcasted_iota(jnp.int32, (length, length), 0)
    after = lax.broadcasted_iota(jnp.int32, (length, length), 1)
    upper = jnp.where(before <= after, 1.0, 0.0).astype(BF16)
    marks = jnp.broadcast_to(jnp.where(flagged, 1.0, 0.0), (16, length)).astype(BF16)
    place = dot(marks, upper)[0:1, :].astype(jnp.int32) - 1
    place = jnp.where(flagged, place, -1)
    pos_ref[0] = place

    for chunk in range(xc_ref.shape[1] // CHUNK):

        @pl.when(chunk * CHUNK < known)
        def _():
            target = chunk * CHUNK + lax.broadcasted_iota(jnp.int32, (CHUNK, length), 0)
            target = jnp.minimum(target, known - 1)
            chosen = jnp.where(place == target, 1.0, 0.0).astype(BF16)
            xc_ref[0, chunk * CHUNK : (chunk + 1) * CHUNK, :] = dot(chosen, x_ref[0]).astype(BF16)

    xt_ref[0, 0:width, :] = x_ref[0].T
    xt_ref[0, width:, :] = jnp.ones((ONES, length), BF16)


def gather_known(scalars, flags, x):
    cells, length, width = x.shape
    padded = -(-length // CHUNK) * CHUNK
    one = lambda *shape: pl.BlockSpec((1,) + shape, lambda i, s: (i, 0, 0))
    return pl.pallas_call(
        gather_kernel,
        out_shape=(
            jax.ShapeDtypeStruct((cells, padded, width), BF16),
            jax.ShapeDtypeStruct((cells, width + ONES, length), BF16),
            jax.ShapeDtypeStruct((cells, 1, length), jnp.int32),
        ),
        grid_spec=pltpu.PrefetchScalarGridSpec(
            num_scalar_prefetch=1,
            grid=(cells,),
            in_specs=[one(1, length), one(length, width)],
            out_specs=[one(padded, width), one(width + ONES, length), one(1, length)],
        ),
        compiler_params=params(),
        cost_estimate=cost(cells * 2e9, cells * 6e6),
        name="gather_known",
    )(scalars, flags, x)


def as_column(row):
    return jnp.broadcast_to(row, (LANES, LANES)).T[:, 0:1]


def attend_kernel(*refs, held, cells):
    scalars_ref, refs = refs[0], refs[1:]
    pieces, refs = refs[: len(held)], refs[len(held) :]
    (
        xt_ref, xc_ref, pos_ref,
        w_ref, vec_ref, qkv_ref, kct_ref, vc_ref, e_ref, more_ref, top_ref, ot_ref, o_ref, lse_ref,
        bias, qz, vct, top, acc, fast, spill,
    ) = refs
    cell, pair = pl.program_id(0), pl.program_id(1)
    known = scalars_ref[cell]
    me = scalars_ref[cells]
    width, length = w_ref.shape[0], xt_ref.shape[2]
    pairs = width // LANES
    block = width // len(held)

    @pl.when((cell == 0) & (pair == 0))
    def _():
        for offset, piece in zip(held, pieces):
            owner = me ^ offset
            rows = pl.ds(pl.multiple_of(owner * block, block), block)
            for which in range(3):
                for p in range(pairs):
                    col = p * TRIPLE + which * LANES
                    w_ref[rows, col : col + LANES] = piece[
                        which * block : (which + 1) * block, p * LANES : (p + 1) * LANES
                    ]
            vec_ref[:, rows] = piece[3 * block :, 0:block].astype(F32)
        for p in range(pairs):
            cols = slice(p * LANES, (p + 1) * LANES)
            bias[p, :, 0:1] = as_column(vec_ref[0:1, cols])
            bias[p, :, 1:2] = as_column(vec_ref[1:2, cols])

    weights = w_ref[:, pl.ds(pl.multiple_of(pair * TRIPLE, LANES), TRIPLE)]
    hidden = pos_ref[0] < 0
    turned = dot(weights, xt_ref[0, 0:width, :], 0, 0)
    queries = (turned[0:LANES, :] + bias[pair, :, 0:1]).astype(BF16)
    keys = turned[LANES : 2 * LANES, :].astype(BF16)
    values = (turned[2 * LANES :, :] + bias[pair, :, 1:2]).astype(BF16)
    qkv_ref[0, 0, 0:LANES, :] = queries
    qkv_ref[0, 0, LANES : 2 * LANES, :] = keys
    qkv_ref[0, 0, 2 * LANES :, :] = values
    low = lax.broadcasted_iota(jnp.int32, (LANES, length), 0) < HD
    scaled = queries.astype(F32) * SCALE
    qz[0] = jnp.where(low, scaled, 0.0).astype(BF16)
    qz[1] = jnp.where(low, 0.0, scaled).astype(BF16)
    keys = keys.astype(F32)
    values = values.astype(F32)
    for side in range(2):
        rows = slice(side * HD, (side + 1) * HD)
        q, k = scaled[rows, :], keys[rows, :]
        own = jnp.sum(q * k, axis=0, keepdims=True)
        longest_q = jnp.max(jnp.sum(q * q, axis=0, keepdims=True))
        longest_k = jnp.max(jnp.sum(k * k, axis=0, keepdims=True))
        safe = longest_q * longest_k < SAFE_SCORE * SAFE_SCORE
        fast[side] = safe.astype(jnp.int32)
        top[side] = jnp.where(safe, 0.0, jnp.where(hidden, own, MASK_FILL))
        weight = jnp.exp(jnp.where(safe, own, 0.0))
        weight = jnp.where(hidden, weight, 0.0).astype(BF16).astype(F32)
        acc[side, 0:HD, :] = weight * values[rows, :]
        acc[side, HD:, :] = jnp.broadcast_to(weight, (EXTRA, length))
    both = (fast[0] + fast[1]) == 2
    value_bias = vec_ref[1:2, pl.ds(pl.multiple_of(pair * LANES, LANES), LANES)]

    def one_chunk(chunk, exps):
        rows = pl.ds(pl.multiple_of(chunk * CHUNK, 16), CHUNK)
        packed = dot(xc_ref[0, rows, :], weights[:, LANES:])
        keys = packed[:, 0:LANES]
        values = packed[:, LANES:] + value_bias
        row = chunk * CHUNK + lax.broadcasted_iota(jnp.int32, (CHUNK, LANES), 0)
        valid = row < known
        kct_ref[0, 0, chunk] = jnp.where(valid, keys, 0.0).T.astype(BF16)
        values_t = jnp.where(valid, values, 0.0).T.astype(BF16)
        keys = keys.astype(BF16)
        vc_ref[0, 0, rows, :] = values.astype(BF16)
        row = chunk * CHUNK + lax.broadcasted_iota(jnp.int32, (EXTRA, CHUNK), 1)
        counted = jnp.where(row < known, 1.0, 0.0).astype(BF16)
        for side in range(2):
            vct[side, 0:HD, :] = values_t[side * HD : (side + 1) * HD, :]
            vct[side, HD:, :] = counted

        @pl.when(both)
        def _():
            for side in range(2):
                probs = jnp.exp(dot(keys, qz[side])).astype(BF16)
                exps[side] = probs
                acc[side] += dot(vct[side], probs)
                top_ref[0, 0, chunk, side] = top[side]

        @pl.when(jnp.logical_not(both))
        def _():
            for side in range(2):
                scores = dot(keys, qz[side])
                peak = jnp.maximum(top[side], jnp.max(scores, axis=0, keepdims=True))
                probs = jnp.exp(scores - peak).astype(BF16)
                exps[side] = probs
                acc[side] = acc[side] * jnp.exp(top[side] - peak) + dot(vct[side], probs)
                top[side] = peak
                top_ref[0, 0, chunk, side] = peak

    @pl.when(known > 0)
    def _():
        one_chunk(0, e_ref.at[0, 0])

    def later_chunk(chunk, carry):
        one_chunk(chunk, spill)
        pltpu.sync_copy(spill, more_ref.at[cell, pair, chunk - 1])
        return carry

    lax.fori_loop(1, (known + CHUNK - 1) // CHUNK, later_chunk, 0)

    for side in range(2):
        total = acc[side, HD : HD + 1, :]
        ot_ref[0, side * HD : (side + 1) * HD, :] = (acc[side, 0:HD, :] / total).astype(BF16)
        lse_ref[0, side] = top[side] + jnp.log(total)
    o_ref[0] = ot_ref[0].T


def attend(scalars, held, pieces, xt, xc, pos):
    cells, length = xt.shape[0], xt.shape[2]
    width = xt.shape[1] - ONES
    padded = xc.shape[1]
    pairs = width // LANES
    chunks = padded // CHUNK
    full = lambda *shape: pl.BlockSpec(shape, lambda c, p, s: (0,) * len(shape))
    shape = jax.ShapeDtypeStruct
    return pl.pallas_call(
        functools.partial(attend_kernel, held=held, cells=cells),
        out_shape=(
            shape((width, 3 * width), BF16),
            shape((EXTRA, width), F32),
            shape((cells, pairs, TRIPLE, length), BF16),
            shape((cells, pairs, chunks, LANES, CHUNK), BF16),
            shape((cells, pairs, padded, LANES), BF16),
            shape((cells, pairs, 2, CHUNK, length), BF16),
            shape((cells, pairs, max(chunks - 1, 1), 2, CHUNK, length), BF16),
            shape((cells, pairs, chunks, 2, 1, length), F32),
            shape((cells, width, length), BF16),
            shape((cells, length, width), BF16),
            shape((cells, H, 1, length), F32),
        ),
        grid_spec=pltpu.PrefetchScalarGridSpec(
            num_scalar_prefetch=1,
            grid=(cells, pairs),
            in_specs=[full(*piece.shape) for piece in pieces]
            + [
                pl.BlockSpec((1, width + ONES, length), lambda c, p, s: (c, 0, 0)),
                pl.BlockSpec((1, padded, width), lambda c, p, s: (c, 0, 0)),
                pl.BlockSpec((1, 1, length), lambda c, p, s: (c, 0, 0)),
            ],
            out_specs=[
                full(width, 3 * width),
                full(EXTRA, width),
                pl.BlockSpec((1, 1, TRIPLE, length), lambda c, p, s: (c, p, 0, 0)),
                pl.BlockSpec((1, 1, chunks, LANES, CHUNK), lambda c, p, s: (c, p, 0, 0, 0)),
                pl.BlockSpec((1, 1, padded, LANES), lambda c, p, s: (c, p, 0, 0)),
                pl.BlockSpec((1, 1, 2, CHUNK, length), lambda c, p, s: (c, p, 0, 0, 0)),
                pl.BlockSpec(memory_space=pl.ANY),
                pl.BlockSpec((1, 1, chunks, 2, 1, length), lambda c, p, s: (c, p, 0, 0, 0, 0)),
                pl.BlockSpec((1, LANES, length), lambda c, p, s: (c, p, 0)),
                pl.BlockSpec((1, length, LANES), lambda c, p, s: (c, 0, p)),
                pl.BlockSpec((1, 2, 1, length), lambda c, p, s: (c, p, 0, 0)),
            ],
            scratch_shapes=[
                pltpu.VMEM((pairs, LANES, 8), F32),
                pltpu.VMEM((2, LANES, length), BF16),
                pltpu.VMEM((2, HD + EXTRA, CHUNK), BF16),
                pltpu.VMEM((2, 1, length), F32),
                pltpu.VMEM((2, HD + EXTRA, length), F32),
                pltpu.SMEM((2,), jnp.int32),
                pltpu.VMEM((2, CHUNK, length), BF16),
            ],
        ),
        compiler_params=params(),
        cost_estimate=cost(cells * 1e10, cells * 2.5e7),
        name="attend",
    )(scalars, *pieces, xt, xc, pos)


def row_mean(rows):
    return jnp.mean(rows, axis=-1, keepdims=True)


def normalize(rows):
    centred = rows - row_mean(rows)
    scale = lax.rsqrt(row_mean(centred * centred) + NORM_EPSILON)
    return centred * scale, scale


def norm_back(grad, normed, scale):
    return scale * (grad - row_mean(grad) - normed * row_mean(grad * normed))


def column_sum(rows):
    return jnp.sum(rows, axis=0, keepdims=True)


def middle_kernel(*refs, held, cells):
    scalars_ref, refs = refs[0], refs[1:]
    pieces, refs = refs[: len(held)], refs[len(held) :]
    (
        x_ref, o_ref, cot_ref, vec_ref,
        result_ref, dhid_ref, datt_ref, keep_ref, send_ref,
        w, go, gu, gd, gvec,
    ) = refs
    me = scalars_ref[cells]
    width = x_ref.shape[1]
    block = width // len(held)

    @pl.when(pl.program_id(0) == 0)
    def _():
        for offset, piece in zip(held, pieces):
            rows = pl.ds(pl.multiple_of((me ^ offset) * block, block), block)
            for which in range(3):
                w[which, rows, :] = piece[which * block : (which + 1) * block, :]
        go[...] = jnp.zeros_like(go)
        gu[...] = jnp.zeros_like(gu)
        gd[...] = jnp.zeros_like(gd)
        gvec[...] = jnp.zeros_like(gvec)

    out_bias, gain_one, shift_one, up_bias, down_bias, gain_two, shift_two = (
        vec_ref[2 + i : 3 + i, :] for i in range(MIDDLE_VECTORS)
    )
    attended = o_ref[...]
    first_in = x_ref[...].astype(F32) + (dot(attended, w[0]) + out_bias)
    norm_one, scale_one = normalize(first_in)
    first_norm = norm_one * gain_one + shift_one
    first_low = first_norm.astype(BF16)
    pre_act = dot(first_low, w[1]) + up_bias
    below = 0.5 * (1.0 + lax.erf(pre_act * (0.5**0.5)))
    activated = (pre_act * below).astype(BF16)
    slope = below + pre_act * (jnp.exp(-0.5 * pre_act * pre_act) * 0.3989422804014327)
    second_in = first_norm + (dot(activated, w[2]) + down_bias)
    norm_two, scale_two = normalize(second_in)
    result_ref[...] = (norm_two * gain_two + shift_two).astype(BF16)

    dy = cot_ref[...].astype(F32)
    d_second = norm_back(dy * gain_two, norm_two, scale_two)
    d_ff = d_second.astype(BF16)
    gd[...] += dot(activated, d_ff, 0, 0)
    d_pre = (dot(d_ff, w[2], 1, 1) * slope).astype(BF16)
    gu[...] += dot(first_low, d_pre, 0, 0)
    d_first = d_second + dot(d_pre, w[1], 1, 1)
    d_hidden = norm_back(d_first * gain_one, norm_one, scale_one)
    d_attn = d_hidden.astype(BF16)
    go[...] += dot(attended, d_attn, 0, 0)
    dhid_ref[...] = d_attn
    datt_ref[...] = dot(d_attn, w[0], 1, 1).astype(BF16)
    gvec[0:1, :] += column_sum(d_attn.astype(F32))
    gvec[1:2, :] += column_sum(d_first * norm_one)
    gvec[2:3, :] += column_sum(d_first)
    gvec[3:4, :] += column_sum(d_pre.astype(F32))
    gvec[4:5, :] += column_sum(d_ff.astype(F32))
    gvec[5:6, :] += column_sum(dy * norm_two)
    gvec[6:7, :] += column_sum(dy)

    @pl.when(pl.program_id(0) == pl.num_programs(0) - 1)
    def _():
        for offset in range(len(held)):
            target = (keep_ref, send_ref)[offset % 2].at[offset // 2]
            rows = pl.ds(pl.multiple_of((me ^ offset) * block, block), block)
            for which, grad in enumerate((go, gu, gd)):
                cols = slice(which * width, (which + 1) * width)
                target[0:block, cols] = grad[rows, :].astype(BF16)
            target[block:, :] = jnp.zeros((EXTRA, 3 * width), BF16)
            target[block:, 0:block] = gvec[:, rows].astype(BF16)


def middle(scalars, held, pieces, x, o, cot, vec, cells):
    rows, width = x.shape
    step = ROWS if rows % ROWS == 0 else rows
    block = pl.BlockSpec((step, width), lambda i, s: (i, 0))
    full = lambda *shape: pl.BlockSpec(shape, lambda i, s: (0,) * len(shape))
    low = jax.ShapeDtypeStruct((rows, width), BF16)
    half = (len(held) // 2, width // len(held) + EXTRA, 3 * width)
    return pl.pallas_call(
        functools.partial(middle_kernel, held=held, cells=cells),
        out_shape=(low, low, low, jax.ShapeDtypeStruct(half, BF16), jax.ShapeDtypeStruct(half, BF16)),
        grid_spec=pltpu.PrefetchScalarGridSpec(
            num_scalar_prefetch=1,
            grid=(rows // step,),
            in_specs=[full(*piece.shape) for piece in pieces] + [block, block, block, full(EXTRA, width)],
            out_specs=[block, block, block, full(*half), full(*half)],
            scratch_shapes=[
                pltpu.VMEM((3, width, width), BF16),
                pltpu.VMEM((width, width), F32),
                pltpu.VMEM((width, width), F32),
                pltpu.VMEM((width, width), F32),
                pltpu.VMEM((EXTRA, width), F32),
            ],
        ),
        compiler_params=params(),
        cost_estimate=cost(rows * 5e6, rows * 8e3),
        name="middle",
    )(scalars, *pieces, x, o, cot, vec)


def back_kernel(
    scalars_ref, pos_ref, xt_ref, qkv_ref, kct_ref, vc_ref, e_ref, more_ref, top_ref, ot_ref, lse_ref,
    datt_ref,
    dt_ref, keep_ref, send_ref,
    hot, qz, og, dqa, dkv, delta, grad, spill,
    *, shards, cells, first_pair,
):
    pair, cell = pl.program_id(0), pl.program_id(1)
    known = scalars_ref[cell]
    me = scalars_ref[cells]
    width, length = xt_ref.shape[1] - ONES, xt_ref.shape[2]
    block = width // shards
    steps = (known + CHUNK - 1) // CHUNK
    place = pos_ref[0]
    hidden = place < 0

    @pl.when(pair == 0)
    def _():
        def mark(chunk, carry):
            row = chunk * CHUNK + lax.broadcasted_iota(jnp.int32, (CHUNK, length), 0)
            hot[cell, chunk] = jnp.where(place == row, 1.0, 0.0).astype(BF16)
            return carry

        lax.fori_loop(0, steps, mark, 0)

    low = lax.broadcasted_iota(jnp.int32, (LANES, length), 0) < HD
    queries = qkv_ref[0, 0, 0:LANES, :].astype(F32) * SCALE
    qz[0] = jnp.where(low, queries, 0.0).astype(BF16)
    qz[1] = jnp.where(low, 0.0, queries).astype(BF16)
    turned = datt_ref[0].T
    og[...] = turned
    turned = turned.astype(F32)
    for side in range(2):
        rows = slice(side * HD, (side + 1) * HD)
        query, grads = queries[rows, :], turned[rows, :]
        key = qkv_ref[0, 0, LANES + side * HD : LANES + (side + 1) * HD, :].astype(F32)
        value = qkv_ref[0, 0, 2 * LANES + side * HD : 2 * LANES + (side + 1) * HD, :].astype(F32)
        delta_row = jnp.sum(grads * ot_ref[0, rows, :].astype(F32), axis=0, keepdims=True)
        delta[side] = delta_row
        own = jnp.sum(query * key, axis=0, keepdims=True)
        prob = jnp.exp(jnp.where(hidden, own, MASK_FILL) - lse_ref[0, side])
        own_grad = jnp.sum(grads * value, axis=0, keepdims=True)
        back = (prob * (own_grad - delta_row)).astype(BF16).astype(F32)
        dqa[rows, :] = back * key
        dkv[rows, :] = back * query
        dkv[LANES + side * HD : LANES + (side + 1) * HD, :] = prob.astype(BF16).astype(F32) * grads

    def one_chunk(chunk, exps):
        values = vc_ref[0, 0, pl.ds(pl.multiple_of(chunk * CHUNK, 16), CHUNK), :]
        d_keys = jnp.zeros((CHUNK, LANES), F32)
        d_values = jnp.zeros((CHUNK, LANES), F32)
        for side in range(2):
            rows = slice(side * HD, (side + 1) * HD)
            share = jnp.exp(top_ref[0, 0, chunk, side] - lse_ref[0, side])
            mine = low if side == 0 else jnp.logical_not(low)
            oz = jnp.where(mine, og[...].astype(F32) * share, 0.0).astype(BF16)
            probs = exps[side]
            d_scores = (probs.astype(F32) * (dot(values, oz) - delta[side] * share)).astype(BF16)
            d_values += dot(probs, oz, 1, 1)
            d_keys += dot(d_scores, qz[side], 1, 1)
            dqa[rows, :] += dot(kct_ref[0, 0, chunk, rows, :], d_scores)
        joined = jnp.concatenate([d_keys, d_values], axis=1).astype(BF16)
        dkv[...] += dot(joined, hot[cell, chunk], 0, 0)

    @pl.when(known > 0)
    def _():
        one_chunk(0, e_ref.at[0, 0])

    def later_chunk(chunk, carry):
        pltpu.sync_copy(more_ref.at[cell, first_pair + pair, chunk - 1], spill)
        one_chunk(chunk, spill)
        return carry

    lax.fori_loop(1, steps, later_chunk, 0)

    dt_ref[0, 0, 0:LANES, :] = (dqa[...] * SCALE).astype(BF16)
    dt_ref[0, 0, LANES:, :] = dkv[...].astype(BF16)
    term = dot(xt_ref[0], dt_ref[0, 0], 1, 1)

    @pl.when(cell == 0)
    def _():
        grad[...] = term

    @pl.when(cell > 0)
    def _():
        grad[...] += term

    @pl.when(cell == cells - 1)
    def _():
        for offset in range(shards):
            owner = me ^ offset
            target = (keep_ref, send_ref)[offset % 2].at[0, offset // 2]
            rows = pl.ds(pl.multiple_of(owner * block, block), block)
            target[0:block, :] = grad[rows, :].astype(BF16)
            ours = jnp.where(owner == first_pair + pair, 1.0, 0.0)
            target[block:, :] = (grad[width:, :] * ours).astype(BF16)


def attend_back(group, shards, scalars, pos, xt, qkv, kct, vc, e, more, top, ot, lse, datt):
    first, count = group
    cells, length = xt.shape[0], xt.shape[2]
    width = xt.shape[1] - ONES
    padded = vc.shape[2]
    chunks = padded // CHUNK
    half = (count, shards // 2, width // shards + EXTRA, TRIPLE)
    part = pl.BlockSpec((1,) + half[1:], lambda p, c, s: (p, 0, 0, 0))
    shape = jax.ShapeDtypeStruct
    return pl.pallas_call(
        functools.partial(back_kernel, shards=shards, cells=cells, first_pair=first),
        out_shape=(shape((cells, count, TRIPLE, length), BF16), shape(half, BF16), shape(half, BF16)),
        grid_spec=pltpu.PrefetchScalarGridSpec(
            num_scalar_prefetch=1,
            grid=(count, cells),
            in_specs=[
                pl.BlockSpec((1, 1, length), lambda p, c, s: (c, 0, 0)),
                pl.BlockSpec((1, width + ONES, length), lambda p, c, s: (c, 0, 0)),
                pl.BlockSpec((1, 1, TRIPLE, length), lambda p, c, s: (c, first + p, 0, 0)),
                pl.BlockSpec((1, 1, chunks, LANES, CHUNK), lambda p, c, s: (c, first + p, 0, 0, 0)),
                pl.BlockSpec((1, 1, padded, LANES), lambda p, c, s: (c, first + p, 0, 0)),
                pl.BlockSpec((1, 1, 2, CHUNK, length), lambda p, c, s: (c, first + p, 0, 0, 0)),
                pl.BlockSpec(memory_space=pl.ANY),
                pl.BlockSpec((1, 1, chunks, 2, 1, length), lambda p, c, s: (c, first + p, 0, 0, 0, 0)),
                pl.BlockSpec((1, LANES, length), lambda p, c, s: (c, first + p, 0)),
                pl.BlockSpec((1, 2, 1, length), lambda p, c, s: (c, first + p, 0, 0)),
                pl.BlockSpec((1, length, LANES), lambda p, c, s: (c, 0, first + p)),
            ],
            out_specs=[
                pl.BlockSpec((1, 1, TRIPLE, length), lambda p, c, s: (c, p, 0, 0)),
                part,
                part,
            ],
            scratch_shapes=[
                pltpu.VMEM((cells, chunks, CHUNK, length), BF16),
                pltpu.VMEM((2, LANES, length), BF16),
                pltpu.VMEM((LANES, length), BF16),
                pltpu.VMEM((LANES, length), F32),
                pltpu.VMEM((2 * LANES, length), F32),
                pltpu.VMEM((2, 1, length), F32),
                pltpu.VMEM((width + ONES, TRIPLE), F32),
                pltpu.VMEM((2, CHUNK, length), BF16),
            ],
        ),
        compiler_params=params(),
        cost_estimate=cost(cells * count * 6e9, cells * count * 7e6),
        name="attend_back",
    )(scalars, pos, xt, qkv, kct, vc, e, more, top, ot, lse, datt)


def input_kernel(w_ref, dhid_ref, *refs):
    parts, out_ref = refs[:-1], refs[-1]
    back, col = None, 0
    for part in parts:
        rows = part.shape[1]
        term = dot(w_ref[:, col : col + rows], part[0])
        back = term if back is None else back + term
        col += rows
    out_ref[0] = (back.T + dhid_ref[0].astype(F32)).astype(BF16)


def input_grad(w, dhid, parts):
    cells, length, width = dhid.shape
    parts = [part.reshape(cells, -1, length) for part in parts]
    block = pl.BlockSpec((1, length, width), lambda i: (i, 0, 0))
    return pl.pallas_call(
        input_kernel,
        out_shape=jax.ShapeDtypeStruct(dhid.shape, BF16),
        grid=(cells,),
        in_specs=[pl.BlockSpec(w.shape, lambda i: (0, 0)), block]
        + [pl.BlockSpec((1,) + part.shape[1:], lambda i: (i, 0, 0)) for part in parts],
        out_specs=block,
        compiler_params=params(),
        cost_estimate=cost(cells * 2e9, cells * 8e6),
        name="input_grad",
    )(w, dhid, *parts)


def swap(values, axis, mask):
    size = lax.axis_size(axis)
    return lax.ppermute(values, axis, [(i, i ^ mask) for i in range(size)])


def masks(axis):
    found, mask = [], 1
    while mask < lax.axis_size(axis):
        found.append(mask)
        mask *= 2
    return found


def gather_pieces(own):
    held = [own]
    for mask in reversed(masks("fsdp")):
        held = held + [swap(piece, "fsdp", mask) for piece in held]
    return held


def plus(left, right):
    return left.astype(F32) + right.astype(F32)


def reduce_parts(keep, send, dim):
    for mask in masks("fsdp"):
        if mask > 1:
            keep, send = (lax.slice_in_dim(total, i, total.shape[dim], 2, dim) for i in (0, 1))
        total = plus(keep, swap(send, "fsdp", mask)).astype(BF16)
    total = jnp.squeeze(total, dim)
    for mask in masks("dp"):
        total = plus(total.astype(BF16), swap(total.astype(BF16), "dp", mask))
    return total.astype(F32)


def body(*args):
    tokens, known_flags, cotangent = args[0], args[1], args[17]
    cells, length, width = tokens.shape
    shards = lax.axis_size("fsdp")
    block = width // shards
    held = offsets(shards)

    vectors = jnp.stack([args[i] for i in VECTORS])
    vectors = jnp.pad(vectors, ((0, EXTRA - len(VECTORS)), (0, width - block)))
    early = gather_pieces(jnp.concatenate([args[i] for i in SQUARES[:3]] + [vectors]))
    own = jnp.concatenate([args[i] for i in SQUARES[3:]])
    late = [own] + [swap(own, "fsdp", offset) for offset in held[1:]]

    known = jnp.sum((known_flags > 0).astype(jnp.int32), axis=1)
    scalars = jnp.concatenate([known, lax.axis_index("fsdp").astype(jnp.int32)[None]])
    xc, xt, pos = gather_known(scalars, known_flags.reshape(cells, 1, length), tokens)
    w, vec, qkv, kct, vc, e, more, top, ot, o, lse = attend(scalars, held, early, xt, xc, pos)
    flat = lambda a: a.reshape(cells * length, width)
    result, dhid, datt, keep, send = middle(
        scalars, held, late, flat(tokens), flat(o), flat(cotangent), vec, cells
    )
    middle_grads = reduce_parts(keep, send, 0)
    cube = lambda a: a.reshape(cells, length, width)
    parts, pair_grads = [], []
    for group in GROUPS:
        dt, keep, send = attend_back(
            group, shards, scalars, pos, xt, qkv, kct, vc, e, more, top, ot, lse, cube(datt)
        )
        parts.append(dt)
        pair_grads.append(reduce_parts(keep, send, 1))
    tokens_grad = input_grad(w, cube(dhid), parts)

    pair_grads = jnp.concatenate(pair_grads)
    pick = lambda which: pair_grads[:, :, which * LANES : (which + 1) * LANES]
    out = {}
    for which, i in enumerate(SQUARES[:3]):
        out[i] = pick(which)[:, 0:block].transpose(1, 0, 2).reshape(block, width)
        out[i + 1] = jnp.sum(pick(which)[:, block], axis=0)
    for which, i in enumerate(SQUARES[3:]):
        out[i] = middle_grads[0:block, which * width : (which + 1) * width]
    out[6] = jnp.sum(pick(2)[:, block], axis=0)
    out[4] = pick(1)[:, 0:block].transpose(1, 0, 2).reshape(block, width)
    out[5] = pick(2)[:, 0:block].transpose(1, 0, 2).reshape(block, width)
    for row, i in enumerate(VECTORS[2:]):
        out[i] = middle_grads[block + row, 0:block]
    return (cube(result), tokens_grad) + tuple(out[i] for i in range(2, 17))


def solution(mesh):
    cells = P(("dp", "fsdp"), None, None)
    specs = tuple(P("fsdp", None) if i in SQUARES else P("fsdp") for i in range(2, 17))
    return jax.shard_map(
        body,
        mesh=mesh,
        in_specs=(cells, P(("dp", "fsdp"), None)) + specs + (cells,),
        out_specs=(cells, cells) + specs,
        check_vma=False,
    )
```

```python
import functools

import jax
import jax.numpy as jnp
from jax import lax
from jax.experimental import pallas as pl
from jax.experimental.pallas import tpu as pltpu
from jax.sharding import PartitionSpec as P

H = 8
HD = 64
SCALE = HD ** (-0.5)
NORM_EPSILON = 1e-05
MASK_FILL = -1e30
SAFE_SCORE = 50.0

CHUNK = 672
ROWS = 480
SPLITS = 1
STAGES = 7
ONES = 16
EXTRA = 16
LANES = 128
CUT = 512
LOG2E = 1.4426950408889634
TRIPLE = 3 * LANES
GROUPS = ((0, 2), (2, 2))

F32 = jnp.float32
BF16 = jnp.bfloat16
VMEM_LIMIT = 60 << 20

SQUARES = (2, 4, 5, 7, 11, 13)
VECTORS = (3, 6, 8, 9, 10, 12, 14, 15, 16)
MIDDLE_VECTORS = 7


def dot(left, right, left_dim=1, right_dim=0):
    return lax.dot_general(
        left, right, (((left_dim,), (right_dim,)), ((), ())), preferred_element_type=F32
    )


def params():
    return pltpu.CompilerParams(vmem_limit_bytes=VMEM_LIMIT)


def cost(flops, moved):
    return pl.CostEstimate(flops=int(flops), bytes_accessed=int(moved), transcendentals=0)


def offsets(shards):
    held, mask = [0], shards // 2
    while mask:
        held = held + [offset ^ mask for offset in held]
        mask //= 2
    return held


def pack_kernel(*refs):
    flags_ref, squares, vectors = refs[0], refs[1:7], refs[7:16]
    early_ref, late_ref, scalars_ref = refs[16:]
    block = squares[0].shape[0]
    for i in range(3):
        early_ref[i * block : (i + 1) * block, :] = squares[i][...]
        late_ref[i * block : (i + 1) * block, :] = squares[3 + i][...]
    rows = [vector[...].astype(F32).reshape(1, -1) for vector in vectors]
    rows = jnp.concatenate(rows + [jnp.zeros((EXTRA - len(rows), block), F32)], axis=0)
    early_ref[3 * block :, :] = jnp.zeros((EXTRA, early_ref.shape[1]), BF16)
    early_ref[3 * block :, 0:block] = rows.astype(BF16)
    flagged = jnp.where(flags_ref[...] > 0, 1.0, 0.0)
    cells = flags_ref.shape[0]
    for cell in range(cells):
        scalars_ref[cell] = jnp.sum(flagged[cell : cell + 1, :]).astype(jnp.int32)
    scalars_ref[cells] = lax.axis_index("fsdp")


def pack(flags, squares, vectors):
    block, width = squares[0].shape
    cells = flags.shape[0]
    vmem = pl.BlockSpec(memory_space=pltpu.VMEM)
    return pl.pallas_call(
        pack_kernel,
        out_shape=(
            jax.ShapeDtypeStruct((3 * block + EXTRA, width), BF16),
            jax.ShapeDtypeStruct((3 * block, width), BF16),
            jax.ShapeDtypeStruct((cells + 1,), jnp.int32),
        ),
        in_specs=[vmem] * 16,
        out_specs=[vmem, vmem, pl.BlockSpec(memory_space=pltpu.SMEM)],
        compiler_params=params(),
        name="pack",
    )(flags, *squares, *vectors)


def gather_kernel(scalars_ref, flags_ref, x_ref, xc_ref, xt_ref, pos_ref):
    known = scalars_ref[pl.program_id(0)]
    length, width = x_ref.shape[1], x_ref.shape[2]
    flagged = flags_ref[pl.ds(pl.program_id(0), 1), :] > 0
    before = lax.broadcasted_iota(jnp.int32, (length, length), 0)
    after = lax.broadcasted_iota(jnp.int32, (length, length), 1)
    upper = jnp.where(before <= after, 1.0, 0.0).astype(BF16)
    marks = jnp.broadcast_to(jnp.where(flagged, 1.0, 0.0), (16, length)).astype(BF16)
    place = dot(marks, upper)[0:1, :].astype(jnp.int32) - 1
    place = jnp.where(flagged, place, -1)
    pos_ref[0] = place

    for chunk in range(xc_ref.shape[1] // CHUNK):

        @pl.when((chunk == 0) | (chunk * CHUNK < known))
        def _():
            target = chunk * CHUNK + lax.broadcasted_iota(jnp.int32, (CHUNK, length), 0)
            target = jnp.where(known > 0, jnp.minimum(target, known - 1), -2)
            chosen = jnp.where(place == target, 1.0, 0.0).astype(BF16)
            xc_ref[0, chunk * CHUNK : (chunk + 1) * CHUNK, :] = dot(chosen, x_ref[0]).astype(BF16)

    xt_ref[0, 0:width, :] = x_ref[0].T
    xt_ref[0, width:, :] = jnp.ones((ONES, length), BF16)


def gather_known(scalars, flags, x):
    cells, length, width = x.shape
    padded = -(-length // CHUNK) * CHUNK
    one = lambda *shape: pl.BlockSpec((1,) + shape, lambda i, s: (i, 0, 0))
    return pl.pallas_call(
        gather_kernel,
        out_shape=(
            jax.ShapeDtypeStruct((cells, padded, width), BF16),
            jax.ShapeDtypeStruct((cells, width + ONES, length), BF16),
            jax.ShapeDtypeStruct((cells, 1, length), jnp.int32),
        ),
        grid_spec=pltpu.PrefetchScalarGridSpec(
            num_scalar_prefetch=1,
            grid=(cells,),
            in_specs=[pl.BlockSpec(flags.shape, lambda i, s: (0, 0)), one(length, width)],
            out_specs=[one(padded, width), one(width + ONES, length), one(1, length)],
        ),
        compiler_params=params(),
        cost_estimate=cost(cells * 2e9, cells * 6e6),
        name="gather_known",
    )(scalars, flags, x)


def as_column(row):
    return jnp.broadcast_to(row, (LANES, LANES)).T[:, 0:1]


def attend_kernel(*refs, held, cells):
    scalars_ref, refs = refs[0], refs[1:]
    pieces, refs = refs[: len(held)], refs[len(held) :]
    (
        xt_ref, xc_ref, pos_ref,
        w_ref, vec_ref, qkv_ref, kct_ref, vc_ref, e_ref, more_ref, top_ref, ot_ref, o_ref, lse_ref, own_ref,
        bias, qz, kc, vct, top, own, acc, spill,
    ) = refs
    cell, pair = pl.program_id(0), pl.program_id(1)
    known = scalars_ref[cell]
    me = scalars_ref[cells]
    width, length = w_ref.shape[0], xt_ref.shape[2]
    pairs = width // LANES
    block = width // len(held)

    @pl.when((cell == 0) & (pair == 0))
    def _():
        for offset, piece in zip(held, pieces):
            owner = me ^ offset
            rows = pl.ds(pl.multiple_of(owner * block, block), block)
            for which in range(3):
                for p in range(pairs):
                    col = p * TRIPLE + which * LANES
                    w_ref[rows, col : col + LANES] = piece[
                        which * block : (which + 1) * block, p * LANES : (p + 1) * LANES
                    ]
            vec_ref[:, rows] = piece[3 * block :, 0:block].astype(F32)
        qz[...] = jnp.zeros_like(qz)
        for p in range(pairs):
            cols = slice(p * LANES, (p + 1) * LANES)
            bias[p, :, 0:1] = as_column(vec_ref[0:1, cols])
            bias[p, :, 1:2] = as_column(vec_ref[1:2, cols])

    col = pl.multiple_of(pair * TRIPLE, LANES)
    part = lambda first, count: w_ref[:, pl.ds(col + first * LANES, count * LANES)]
    hidden = pos_ref[0] < 0
    steps = (known + CHUNK - 1) // CHUNK
    value_bias = vec_ref[1:2, pl.ds(pl.multiple_of(pair * LANES, LANES), LANES)]
    tokens = xt_ref[0, 0:width, :]
    heads = [slice(side * HD, (side + 1) * HD) for side in range(2)]
    cuts = [slice(start, min(start + CUT, length)) for start in range(0, length, CUT)]

    def project(chunk):
        rows = pl.ds(pl.multiple_of(chunk * CHUNK, 16), CHUNK)
        packed = dot(xc_ref[0, rows, :], part(1, 2))
        yield
        row = chunk * CHUNK + lax.broadcasted_iota(jnp.int32, (CHUNK, LANES), 0)
        keys = packed[:, 0:LANES]
        kc[...] = keys.astype(BF16)
        kct_ref[0, 0, chunk] = jnp.where(row < known, keys, 0.0).astype(BF16).T
        yield
        values = packed[:, LANES:] + value_bias
        vc_ref[0, 0, rows, :] = values.astype(BF16)
        values = jnp.where(row < known, values, 0.0).astype(BF16).T
        counted = chunk * CHUNK + lax.broadcasted_iota(jnp.int32, (EXTRA, CHUNK), 1)
        counted = jnp.where(counted < known, 1.0, 0.0).astype(BF16)
        for side in range(2):
            vct[side, 0:HD, :] = values[heads[side], :]
            vct[side, HD:, :] = counted
        yield

    def begin(side, shifted):
        weight = jnp.ones((1, length), F32) if shifted else jnp.exp(own[side])
        weight = jnp.where(hidden, weight, 0.0).astype(BF16).astype(F32)
        top[side] = jnp.where(hidden, own[side], MASK_FILL) if shifted else jnp.zeros((1, length), F32)
        return weight

    def own_values(side):
        return qkv_ref[0, 0, 2 * LANES + side * HD : 2 * LANES + (side + 1) * HD, :].astype(F32)

    def measure(side):
        q = qkv_ref[0, 0, heads[side], :].astype(F32)
        k = qkv_ref[0, 0, LANES + side * HD : LANES + (side + 1) * HD, :].astype(F32)
        own[side] = jnp.sum(q * k, axis=0, keepdims=True) * SCALE
        longest_q = jnp.max(jnp.sum(q * q, axis=0, keepdims=True))
        longest_k = jnp.max(jnp.sum(k * k, axis=0, keepdims=True))
        return longest_q * longest_k < (SAFE_SCORE / SCALE) * (SAFE_SCORE / SCALE)

    def conclude(side):
        total = acc[side, HD : HD + 1, :]
        ot_ref[0, heads[side], :] = (acc[side, 0:HD, :] * (1.0 / total)).astype(BF16)
        lse_ref[0, side] = top[side] + jnp.log(total)
        own_ref[0, side] = own[side]

    first = project(0)
    next(first)
    turned = dot(part(0, 1), tokens, 0, 0)
    next(first)
    queries = (turned + bias[pair, :, 0:1]).astype(BF16)
    turned = dot(part(1, 1), tokens, 0, 0)
    qkv_ref[0, 0, 0:LANES, :] = queries
    for side in range(2):
        qz[side, heads[side], :] = queries[heads[side], :]
    next(first)
    qkv_ref[0, 0, LANES : 2 * LANES, :] = turned.astype(BF16)
    turned = dot(part(2, 1), tokens, 0, 0)
    weights = []
    safe = None
    for side in range(2):
        for cut in cuts:
            scores = dot(kc[...], qz[side, :, cut])
            e_ref[0, 0, side, :, cut] = jnp.exp2(scores * (SCALE * LOG2E)).astype(BF16)
            if side == 0 and cut is cuts[0]:
                qkv_ref[0, 0, 2 * LANES :, :] = (turned + bias[pair, :, 1:2]).astype(BF16)
            if cut is cuts[1]:
                bounded = measure(side)
                safe = bounded if safe is None else safe & bounded
                weights.append(begin(side, False))
        total = dot(vct[side], e_ref[0, 0, side])
        acc[side, 0:HD, :] = total[0:HD, :] + weights[side] * own_values(side)
        acc[side, HD:, :] = total[HD:, :] + weights[side]
    for side in range(2):
        conclude(side)
        top_ref[0, 0, 0, side] = top[side]
    o_ref[0] = ot_ref[0].T

    def weigh(chunk, side, exps, shifted):
        scores = dot(kc[...], qz[side]) * SCALE
        if shifted:
            peak = jnp.maximum(top[side], jnp.max(scores, axis=0, keepdims=True))
            peak = jnp.where(known > 0, peak, top[side])
            scores = jnp.minimum(scores - peak, 0.0)
        probs = jnp.exp(scores).astype(BF16)
        exps[side] = probs
        if shifted:
            acc[side] = acc[side] * jnp.exp(top[side] - peak) + dot(vct[side], probs)
            top[side] = peak
        else:
            acc[side] += dot(vct[side], probs)
        top_ref[0, 0, chunk, side] = top[side]

    @pl.when(jnp.logical_not(safe))
    def _():
        for side in range(2):
            weight = begin(side, True)
            acc[side, 0:HD, :] = weight * own_values(side)
            acc[side, HD:, :] = jnp.broadcast_to(weight, (EXTRA, length))
            weigh(0, side, e_ref.at[0, 0], True)

    def later_chunk(chunk, carry):
        for _ in project(chunk):
            pass

        @pl.when(safe)
        def _():
            for side in range(2):
                weigh(chunk, side, spill, False)

        @pl.when(jnp.logical_not(safe))
        def _():
            for side in range(2):
                weigh(chunk, side, spill, True)

        pltpu.sync_copy(spill, more_ref.at[cell, pair, chunk - 1])
        return carry

    lax.fori_loop(1, steps, later_chunk, 0)

    @pl.when(jnp.logical_not(safe) | (steps > 1))
    def _():
        for side in range(2):
            conclude(side)
        o_ref[0] = ot_ref[0].T


def attend(scalars, held, pieces, xt, xc, pos):
    cells, length = xt.shape[0], xt.shape[2]
    width = xt.shape[1] - ONES
    padded = xc.shape[1]
    pairs = width // LANES
    chunks = padded // CHUNK
    full = lambda *shape: pl.BlockSpec(shape, lambda c, p, s: (0,) * len(shape))
    shape = jax.ShapeDtypeStruct
    return pl.pallas_call(
        functools.partial(attend_kernel, held=held, cells=cells),
        out_shape=(
            shape((width, 3 * width), BF16),
            shape((EXTRA, width), F32),
            shape((cells, pairs, TRIPLE, length), BF16),
            shape((cells, pairs, chunks, LANES, CHUNK), BF16),
            shape((cells, pairs, padded, LANES), BF16),
            shape((cells, pairs, 2, CHUNK, length), BF16),
            shape((cells, pairs, max(chunks - 1, 1), 2, CHUNK, length), BF16),
            shape((cells, pairs, chunks, 2, 1, length), F32),
            shape((cells, width, length), BF16),
            shape((cells, length, width), BF16),
            shape((cells, H, 1, length), F32),
            shape((cells, H, 1, length), F32),
        ),
        grid_spec=pltpu.PrefetchScalarGridSpec(
            num_scalar_prefetch=1,
            grid=(cells, pairs),
            in_specs=[full(*piece.shape) for piece in pieces]
            + [
                pl.BlockSpec((1, width + ONES, length), lambda c, p, s: (c, 0, 0)),
                pl.BlockSpec((1, padded, width), lambda c, p, s: (c, 0, 0)),
                pl.BlockSpec((1, 1, length), lambda c, p, s: (c, 0, 0)),
            ],
            out_specs=[
                full(width, 3 * width),
                full(EXTRA, width),
                pl.BlockSpec((1, 1, TRIPLE, length), lambda c, p, s: (c, p, 0, 0)),
                pl.BlockSpec((1, 1, chunks, LANES, CHUNK), lambda c, p, s: (c, p, 0, 0, 0)),
                pl.BlockSpec((1, 1, padded, LANES), lambda c, p, s: (c, p, 0, 0)),
                pl.BlockSpec((1, 1, 2, CHUNK, length), lambda c, p, s: (c, p, 0, 0, 0)),
                pl.BlockSpec(memory_space=pl.ANY),
                pl.BlockSpec((1, 1, chunks, 2, 1, length), lambda c, p, s: (c, p, 0, 0, 0, 0)),
                pl.BlockSpec((1, LANES, length), lambda c, p, s: (c, p, 0)),
                pl.BlockSpec((1, length, LANES), lambda c, p, s: (c, 0, p)),
                pl.BlockSpec((1, 2, 1, length), lambda c, p, s: (c, p, 0, 0)),
                pl.BlockSpec((1, 2, 1, length), lambda c, p, s: (c, p, 0, 0)),
            ],
            scratch_shapes=[
                pltpu.VMEM((pairs, LANES, 8), F32),
                pltpu.VMEM((2, LANES, length), BF16),
                pltpu.VMEM((CHUNK, LANES), BF16),
                pltpu.VMEM((2, HD + EXTRA, CHUNK), BF16),
                pltpu.VMEM((2, 1, length), F32),
                pltpu.VMEM((2, 1, length), F32),
                pltpu.VMEM((2, HD + EXTRA, length), F32),
                pltpu.VMEM((2, CHUNK, length), BF16),
            ],
        ),
        compiler_params=params(),
        cost_estimate=cost(cells * 1e10, cells * 2.5e7),
        name="attend",
    )(scalars, *pieces, xt, xc, pos)


def row_mean(rows):
    return jnp.mean(rows, axis=-1, keepdims=True)


def normalize(rows):
    centred = rows - row_mean(rows)
    scale = lax.rsqrt(row_mean(centred * centred) + NORM_EPSILON)
    return centred * scale, scale


def norm_back(grad, normed, scale):
    return scale * (grad - row_mean(grad) - normed * row_mean(grad * normed))


def column_sum(rows):
    return jnp.sum(rows, axis=0, keepdims=True)


def middle_kernel(*refs, held, cells):
    scalars_ref, refs = refs[0], refs[1:]
    pieces, refs = refs[: len(held)], refs[len(held) :]
    (
        x_ref, o_ref, cot_ref, vec_ref,
        result_ref, dhid_ref, datt_ref, keep_ref, send_ref,
        w, go, gu, gd, gvec,
    ) = refs
    me = scalars_ref[cells]
    width = x_ref.shape[1]
    block = width // len(held)

    @pl.when(pl.program_id(0) == 0)
    def _():
        for offset, piece in zip(held, pieces):
            rows = pl.ds(pl.multiple_of((me ^ offset) * block, block), block)
            for which in range(3):
                w[which, rows, :] = piece[which * block : (which + 1) * block, :]
        go[...] = jnp.zeros_like(go)
        gu[...] = jnp.zeros_like(gu)
        gd[...] = jnp.zeros_like(gd)
        gvec[...] = jnp.zeros_like(gvec)

    def stages(rows):
        out_bias, gain_one, shift_one, up_bias, down_bias, gain_two, shift_two = (
            vec_ref[2 + i : 3 + i, :] for i in range(MIDDLE_VECTORS)
        )
        attended = o_ref[rows, :]
        product = dot(attended, w[0])
        yield
        norm_one, scale_one = normalize(x_ref[rows, :].astype(F32) + (product + out_bias))
        first_norm = norm_one * gain_one + shift_one
        first_low = first_norm.astype(BF16)
        product = dot(first_low, w[1])
        yield
        pre_act = product + up_bias
        below = 0.5 * (1.0 + lax.erf(pre_act * (0.5**0.5)))
        activated = (pre_act * below).astype(BF16)
        product = dot(activated, w[2])
        slope = below + pre_act * (jnp.exp(-0.5 * pre_act * pre_act) * 0.3989422804014327)
        yield
        norm_two, scale_two = normalize(first_norm + (product + down_bias))
        result_ref[rows, :] = (norm_two * gain_two + shift_two).astype(BF16)
        dy = cot_ref[rows, :].astype(F32)
        d_second = norm_back(dy * gain_two, norm_two, scale_two)
        d_ff = d_second.astype(BF16)
        product = dot(d_ff, w[2], 1, 1)
        gvec[4:5, :] += column_sum(d_ff.astype(F32))
        gvec[5:6, :] += column_sum(dy * norm_two)
        gvec[6:7, :] += column_sum(dy)
        yield
        d_pre = (product * slope).astype(BF16)
        product = dot(d_pre, w[1], 1, 1)
        gd[...] += dot(activated, d_ff, 0, 0)
        gvec[3:4, :] += column_sum(d_pre.astype(F32))
        yield
        d_first = d_second + product
        d_hidden = norm_back(d_first * gain_one, norm_one, scale_one)
        d_attn = d_hidden.astype(BF16)
        dhid_ref[rows, :] = d_attn
        product = dot(d_attn, w[0], 1, 1)
        gu[...] += dot(first_low, d_pre, 0, 0)
        gvec[0:1, :] += column_sum(d_attn.astype(F32))
        gvec[1:2, :] += column_sum(d_first * norm_one)
        gvec[2:3, :] += column_sum(d_first)
        yield
        datt_ref[rows, :] = product.astype(BF16)
        go[...] += dot(attended, d_attn, 0, 0)
        yield

    step = x_ref.shape[0] // SPLITS
    live = [stages(slice(i * step, (i + 1) * step)) for i in range(SPLITS)]
    for turn in range(STAGES + SPLITS - 1):
        for i, part in enumerate(live):
            if 0 <= turn - i < STAGES:
                next(part)

    @pl.when(pl.program_id(0) == pl.num_programs(0) - 1)
    def _():
        for offset in range(len(held)):
            target = (keep_ref, send_ref)[offset % 2].at[offset // 2]
            rows = pl.ds(pl.multiple_of((me ^ offset) * block, block), block)
            for which, grad in enumerate((go, gu, gd)):
                cols = slice(which * width, (which + 1) * width)
                target[0:block, cols] = grad[rows, :].astype(BF16)
            target[block:, :] = jnp.zeros((EXTRA, 3 * width), BF16)
            target[block:, 0:block] = gvec[:, rows].astype(BF16)


def middle(scalars, held, pieces, x, o, cot, vec, cells):
    rows, width = x.shape
    step = ROWS if rows % ROWS == 0 else rows
    block = pl.BlockSpec((step, width), lambda i, s: (i, 0))
    full = lambda *shape: pl.BlockSpec(shape, lambda i, s: (0,) * len(shape))
    low = jax.ShapeDtypeStruct((rows, width), BF16)
    half = (len(held) // 2, width // len(held) + EXTRA, 3 * width)
    return pl.pallas_call(
        functools.partial(middle_kernel, held=held, cells=cells),
        out_shape=(low, low, low, jax.ShapeDtypeStruct(half, BF16), jax.ShapeDtypeStruct(half, BF16)),
        grid_spec=pltpu.PrefetchScalarGridSpec(
            num_scalar_prefetch=1,
            grid=(rows // step,),
            in_specs=[full(*piece.shape) for piece in pieces] + [block, block, block, full(EXTRA, width)],
            out_specs=[block, block, block, full(*half), full(*half)],
            scratch_shapes=[
                pltpu.VMEM((3, width, width), BF16),
                pltpu.VMEM((width, width), F32),
                pltpu.VMEM((width, width), F32),
                pltpu.VMEM((width, width), F32),
                pltpu.VMEM((EXTRA, width), F32),
            ],
        ),
        compiler_params=params(),
        cost_estimate=cost(rows * 5e6, rows * 8e3),
        name="middle",
    )(scalars, *pieces, x, o, cot, vec)


def back_kernel(
    scalars_ref, pos_ref, xt_ref, qkv_ref, kct_ref, vc_ref, e_ref, more_ref, top_ref, ot_ref, lse_ref,
    own_ref, datt_ref,
    dt_ref, keep_ref, send_ref,
    hot, oz, og, ds, joined, dqa, dkv, self_q, self_kv, delta, grad, term, spill,
    *, shards, cells, first_pair,
):
    pair, cell = pl.program_id(0), pl.program_id(1)
    known = scalars_ref[cell]
    me = scalars_ref[cells]
    width, length = xt_ref.shape[1] - ONES, xt_ref.shape[2]
    block = width // shards
    steps = (known + CHUNK - 1) // CHUNK
    place = pos_ref[0]
    hidden = place < 0

    @pl.when(pair == 0)
    def _():
        hot[cell, 0] = jnp.where(
            place == lax.broadcasted_iota(jnp.int32, (CHUNK, length), 0), 1.0, 0.0
        ).astype(BF16)

        def mark(chunk, carry):
            row = chunk * CHUNK + lax.broadcasted_iota(jnp.int32, (CHUNK, length), 0)
            hot[cell, chunk] = jnp.where(place == row, 1.0, 0.0).astype(BF16)
            return carry

        lax.fori_loop(1, steps, mark, 0)

    heads = [slice(side * HD, (side + 1) * HD) for side in range(2)]
    cuts = [slice(start, min(start + CUT, length)) for start in range(0, length, CUT)]
    queries = qkv_ref.at[0, 0, 0:LANES]

    @pl.when((pair == 0) & (cell == 0))
    def _():
        oz[...] = jnp.zeros_like(oz)

    og[...] = datt_ref[0].T

    def share(chunk, side):
        return jnp.exp(top_ref[0, 0, chunk, side] - lse_ref[0, side])

    def outset(side):
        rows = heads[side]
        grads = og[rows, :].astype(F32)
        query = queries[rows, :].astype(F32) * SCALE
        key = qkv_ref[0, 0, LANES + side * HD : LANES + (side + 1) * HD, :].astype(F32)
        value = qkv_ref[0, 0, 2 * LANES + side * HD : 2 * LANES + (side + 1) * HD, :].astype(F32)
        prob = jnp.exp(jnp.where(hidden, own_ref[0, side], MASK_FILL) - lse_ref[0, side])
        own_grad = jnp.sum(grads * value, axis=0, keepdims=True)
        back = (prob * (own_grad - delta[side])).astype(BF16).astype(F32)
        self_q[rows, :] = back * key
        self_kv[rows, :] = back * query
        self_kv[LANES + side * HD : LANES + (side + 1) * HD, :] = prob.astype(BF16).astype(F32) * grads

    def score_grads(chunk, side, exps, values, cut, scaled):
        part = dot(values, oz[side, :, cut]) - scaled[:, cut]
        ds[side, :, cut] = (exps[side, :, cut].astype(F32) * part).astype(BF16)

    def spread(chunk, side, part):
        scaled = share(chunk, side)
        oz[side, heads[side], :] = (og[heads[side], :].astype(F32) * scaled).astype(BF16)
        return delta[side] * scaled

    def close(q_part, kv_part):
        dt_ref[0, 0, 0:LANES, :] = ((q_part + self_q[...]) * SCALE).astype(BF16)
        dt_ref[0, 0, LANES:, :] = (kv_part + self_kv[...]).astype(BF16)
        term[...] = dot(xt_ref[0], dt_ref[0, 0], 1, 1)

    exps = e_ref.at[0, 0]
    values = vc_ref[0, 0, 0:CHUNK, :]
    for side in range(2):
        rows = heads[side]
        delta[side] = jnp.sum(
            og[rows, :].astype(F32) * ot_ref[0, rows, :].astype(F32), axis=0, keepdims=True
        )
    scaled = [spread(0, side, None) for side in range(2)]
    for cut in cuts:
        score_grads(0, 0, exps, values, cut, scaled[0])
    d_values = dot(exps[0], oz[0], 1, 1)
    outset(0)
    for cut in cuts:
        score_grads(0, 1, exps, values, cut, scaled[1])
    d_keys = dot(ds[0], queries[...], 1, 1)
    outset(1)
    d_values += dot(exps[1], oz[1], 1, 1)
    lanes = lax.broadcasted_iota(jnp.int32, (CHUNK, LANES), 1) < HD
    joined[:, LANES:] = d_values.astype(BF16)
    dqa[0:HD, :] = dot(kct_ref[0, 0, 0, 0:HD, :], ds[0])
    d_keys = jnp.where(lanes, d_keys, dot(ds[1], queries[...], 1, 1)) * SCALE
    dqa[HD:, :] = dot(kct_ref[0, 0, 0, HD:, :], ds[1])
    joined[:, 0:LANES] = d_keys.astype(BF16)
    dkv[...] = dot(joined[...], hot[cell, 0], 0, 0)
    close(dqa[...], dkv[...])

    def later_chunk(chunk, carry):
        pltpu.sync_copy(more_ref.at[cell, first_pair + pair, chunk - 1], spill)
        values = vc_ref[0, 0, pl.ds(pl.multiple_of(chunk * CHUNK, 16), CHUNK), :]
        d_values = jnp.zeros((CHUNK, LANES), F32)
        for side in range(2):
            scaled = spread(chunk, side, None)
            for cut in cuts:
                score_grads(chunk, side, spill, values, cut, scaled)
            d_values += dot(spill[side], oz[side], 1, 1)
            dqa[heads[side], :] += dot(kct_ref[0, 0, chunk, heads[side], :], ds[side])
        d_keys = jnp.where(lanes, dot(ds[0], queries[...], 1, 1), dot(ds[1], queries[...], 1, 1)) * SCALE
        joined[:, 0:LANES] = d_keys.astype(BF16)
        joined[:, LANES:] = d_values.astype(BF16)
        dkv[...] += dot(joined[...], hot[cell, chunk], 0, 0)
        return carry

    @pl.when(steps > 1)
    def _():
        lax.fori_loop(1, steps, later_chunk, 0)
        close(dqa[...], dkv[...])

    @pl.when(cell == 0)
    def _():
        grad[...] = term[...]

    @pl.when(cell > 0)
    def _():
        grad[...] += term[...]

    @pl.when(cell == cells - 1)
    def _():
        for offset in range(shards):
            owner = me ^ offset
            target = (keep_ref, send_ref)[offset % 2].at[offset // 2, 0]
            rows = pl.ds(pl.multiple_of(owner * block, block), block)
            target[0:block, :] = grad[rows, :].astype(BF16)
            ours = jnp.where(owner == first_pair + pair, 1.0, 0.0)
            target[block:, :] = (grad[width:, :] * ours).astype(BF16)


def attend_back(group, shards, scalars, pos, xt, qkv, kct, vc, e, more, top, ot, lse, own, datt):
    first, count = group
    cells, length = xt.shape[0], xt.shape[2]
    width = xt.shape[1] - ONES
    padded = vc.shape[2]
    chunks = padded // CHUNK
    half = (shards // 2, count, width // shards + EXTRA, TRIPLE)
    part = pl.BlockSpec((shards // 2, 1) + half[2:], lambda p, c, s: (0, p, 0, 0))
    shape = jax.ShapeDtypeStruct
    return pl.pallas_call(
        functools.partial(back_kernel, shards=shards, cells=cells, first_pair=first),
        out_shape=(shape((cells, count, TRIPLE, length), BF16), shape(half, BF16), shape(half, BF16)),
        grid_spec=pltpu.PrefetchScalarGridSpec(
            num_scalar_prefetch=1,
            grid=(count, cells),
            in_specs=[
                pl.BlockSpec((1, 1, length), lambda p, c, s: (c, 0, 0)),
                pl.BlockSpec((1, width + ONES, length), lambda p, c, s: (c, 0, 0)),
                pl.BlockSpec((1, 1, TRIPLE, length), lambda p, c, s: (c, first + p, 0, 0)),
                pl.BlockSpec((1, 1, chunks, LANES, CHUNK), lambda p, c, s: (c, first + p, 0, 0, 0)),
                pl.BlockSpec((1, 1, padded, LANES), lambda p, c, s: (c, first + p, 0, 0)),
                pl.BlockSpec((1, 1, 2, CHUNK, length), lambda p, c, s: (c, first + p, 0, 0, 0)),
                pl.BlockSpec(memory_space=pl.ANY),
                pl.BlockSpec((1, 1, chunks, 2, 1, length), lambda p, c, s: (c, first + p, 0, 0, 0, 0)),
                pl.BlockSpec((1, LANES, length), lambda p, c, s: (c, first + p, 0)),
                pl.BlockSpec((1, 2, 1, length), lambda p, c, s: (c, first + p, 0, 0)),
                pl.BlockSpec((1, 2, 1, length), lambda p, c, s: (c, first + p, 0, 0)),
                pl.BlockSpec((1, length, LANES), lambda p, c, s: (c, 0, first + p)),
            ],
            out_specs=[
                pl.BlockSpec((1, 1, TRIPLE, length), lambda p, c, s: (c, p, 0, 0)),
                part,
                part,
            ],
            scratch_shapes=[
                pltpu.VMEM((cells, chunks, CHUNK, length), BF16),
                pltpu.VMEM((2, LANES, length), BF16),
                pltpu.VMEM((LANES, length), BF16),
                pltpu.VMEM((2, CHUNK, length), BF16),
                pltpu.VMEM((CHUNK, 2 * LANES), BF16),
                pltpu.VMEM((LANES, length), F32),
                pltpu.VMEM((2 * LANES, length), F32),
                pltpu.VMEM((LANES, length), F32),
                pltpu.VMEM((2 * LANES, length), F32),
                pltpu.VMEM((2, 1, length), F32),
                pltpu.VMEM((width + ONES, TRIPLE), F32),
                pltpu.VMEM((width + ONES, TRIPLE), F32),
                pltpu.VMEM((2, CHUNK, length), BF16),
            ],
        ),
        compiler_params=params(),
        cost_estimate=cost(cells * count * 6e9, cells * count * 7e6),
        name="attend_back",
    )(scalars, pos, xt, qkv, kct, vc, e, more, top, ot, lse, own, datt)


def input_kernel(w_ref, dhid_ref, *refs):
    parts, out_ref = refs[:-1], refs[-1]
    back, col = None, 0
    for part in parts:
        rows = part.shape[1]
        term = dot(w_ref[:, col : col + rows], part[0])
        back = term if back is None else back + term
        col += rows
    out_ref[0] = (back.T + dhid_ref[0].astype(F32)).astype(BF16)


def input_grad(w, dhid, parts):
    cells, length, width = dhid.shape
    parts = [part.reshape(cells, -1, length) for part in parts]
    block = pl.BlockSpec((1, length, width), lambda i: (i, 0, 0))
    return pl.pallas_call(
        input_kernel,
        out_shape=jax.ShapeDtypeStruct(dhid.shape, BF16),
        grid=(cells,),
        in_specs=[pl.BlockSpec(w.shape, lambda i: (0, 0)), block]
        + [pl.BlockSpec((1,) + part.shape[1:], lambda i: (i, 0, 0)) for part in parts],
        out_specs=block,
        compiler_params=params(),
        cost_estimate=cost(cells * 2e9, cells * 8e6),
        name="input_grad",
    )(w, dhid, *parts)


def finish_kernel(*refs):
    terms, halves, outs = refs[:2], refs[2:-15], refs[-15:]
    block, width = outs[0].shape
    for which in range(3):
        cols = slice(which * width, (which + 1) * width)
        outs[3 + which][...] = terms[0][0:block, cols].astype(F32) + terms[1][0:block, cols].astype(F32)
    rows = terms[0][block:, 0:block].astype(F32) + terms[1][block:, 0:block].astype(F32)
    for row in range(MIDDLE_VECTORS):
        outs[8 + row][...] = rows[row : row + 1, :].reshape(block)

    def write(order):
        biases = [jnp.zeros((1, LANES), F32), jnp.zeros((1, LANES), F32)]
        pair = 0
        for group in range(0, len(halves), 2):
            for part in [halves[group + i] for i in order]:
                for p in range(part.shape[0]):
                    for which in range(3):
                        cols = slice(which * LANES, (which + 1) * LANES)
                        outs[which][:, pair * LANES : (pair + 1) * LANES] = part[p, 0:block, cols].astype(F32)
                    biases[0] += part[p, block : block + 1, 0:LANES].astype(F32)
                    biases[1] += part[p, block : block + 1, 2 * LANES :].astype(F32)
                    pair += 1
        outs[6][...] = biases[0].reshape(block)
        outs[7][...] = biases[1].reshape(block)

    low = lax.axis_index("dp") % 2 == 0

    @pl.when(low)
    def _():
        write((0, 1))

    @pl.when(jnp.logical_not(low))
    def _():
        write((1, 0))


def finish(parts, block, width):
    vmem = pl.BlockSpec(memory_space=pltpu.VMEM)
    return pl.pallas_call(
        finish_kernel,
        out_shape=(jax.ShapeDtypeStruct((block, width), F32),) * 6 + (jax.ShapeDtypeStruct((block,), F32),) * 9,
        in_specs=[vmem] * len(parts),
        out_specs=[vmem] * 15,
        compiler_params=params(),
        name="finish",
    )(*parts)


def swap(values, axis, mask):
    size = lax.axis_size(axis)
    return lax.ppermute(values, axis, [(i, i ^ mask) for i in range(size)])


def masks(axis):
    found, mask = [], 1
    while mask < lax.axis_size(axis):
        found.append(mask)
        mask *= 2
    return found


def after(value, *others):
    return lax.optimization_barrier((value,) + others)[0]


def gather_pieces(own, beside):
    held = [own]
    for mask in reversed(masks("fsdp")):
        held = held + [swap(piece, "fsdp", mask) for piece in held]
        held = held[:1] + [after(piece, beside) for piece in held[1:]]
    return held


def plus(left, right):
    return left.astype(F32) + right.astype(F32)


class Reduction:
    def __init__(self, keep, send, half_dim=None):
        self.keep, self.send = keep, send
        self.half_dim = half_dim
        order = masks("dp") if half_dim is not None else reversed(masks("dp"))
        self.plan = [("fsdp", mask) for mask in masks("fsdp")] + [("dp", mask) for mask in order]
        self.low = (lax.axis_index("dp") % 2) == 0

    def pair(self):
        return self.keep, self.send

    def start(self, pair=None):
        if self.plan:
            self.keep, self.send = pair or self.pair()
            self.arrived = swap(self.send, *self.plan[0])

    def arrive(self):
        self.plan = self.plan[1:]
        if not self.plan:
            return
        total = plus(self.keep, self.arrived).astype(BF16)
        axis, mask = self.plan[0]
        if axis == "fsdp":
            self.keep, self.send = total[0::2], total[1::2]
        elif mask == 1 and self.half_dim is not None:
            first, second = jnp.split(total, 2, self.half_dim)
            self.keep = jnp.where(self.low, first, second)
            self.send = jnp.where(self.low, second, first)
        else:
            self.keep = self.send = total

    def finish(self):
        while self.plan:
            self.start()
            self.arrive()
        if self.half_dim is None:
            return self.keep[0], self.arrived[0]
        mine = plus(self.keep, self.arrived).astype(BF16)[0]
        if lax.axis_size("dp") == 1:
            return jnp.split(mine, 2, self.half_dim - 1)
        return mine, swap(mine, "dp", 1)


def body(*args):
    tokens, known_flags, cotangent = args[0], args[1], args[17]
    cells, length, width = tokens.shape
    shards = lax.axis_size("fsdp")
    block = width // shards
    held = offsets(shards)

    early, late, scalars = pack(known_flags, [args[i] for i in SQUARES], [args[i] for i in VECTORS])
    xc, xt, pos = gather_known(scalars, known_flags, tokens)
    early = gather_pieces(early, xt)
    late = after(late, *early[:2])
    late = [late] + [swap(late, "fsdp", offset) for offset in held[1:]]
    w, vec, qkv, kct, vc, e, more, top, ot, o, lse, own = attend(scalars, held, early, xt, xc, pos)
    flat = lambda a: a.reshape(cells * length, width)
    result, dhid, datt, keep, send = middle(
        scalars, held, late, flat(tokens), flat(o), flat(cotangent), vec, cells
    )
    cube = lambda a: a.reshape(cells, length, width)
    chains = [Reduction(keep, send)]

    def boundary(value):
        for chain in chains[:-1]:
            chain.arrive()
        newest = chains[-1]
        pairs = lax.optimization_barrier([chain.pair() for chain in chains])
        for chain, (chain.keep, chain.send) in zip(chains, pairs):
            pass
        newest.start()
        newest.arrive()
        value, pairs = lax.optimization_barrier((value, [chain.pair() for chain in chains]))
        for chain, pair in zip(chains, pairs):
            chain.start(pair)
        return value

    parts = []
    for group in GROUPS:
        dt, keep, send = attend_back(
            group, shards, boundary(scalars), pos, xt, qkv, kct, vc, e, more, top, ot, lse, own, cube(datt)
        )
        parts.append(dt)
        chains.append(Reduction(keep, send, 1))
    tokens_grad = input_grad(boundary(w), cube(dhid), parts)
    tokens_grad, arrived = lax.optimization_barrier((tokens_grad, [chain.arrived for chain in chains]))
    for chain, chain.arrived in zip(chains, arrived):
        chain.arrive()
    newest = chains[-1]
    newest.start()
    newest.arrive()
    chains[0].send = after(chains[0].send, newest.send)
    halves = [half for chain in chains for half in chain.finish()]
    summed = finish(halves, block, width)
    out = dict(zip(SQUARES + VECTORS, summed))
    return (cube(result), tokens_grad) + tuple(out[i] for i in range(2, 17))


def solution(mesh):
    cells = P(("dp", "fsdp"), None, None)
    specs = tuple(P("fsdp", None) if i in SQUARES else P("fsdp") for i in range(2, 17))
    return jax.shard_map(
        body,
        mesh=mesh,
        in_specs=(cells, P(("dp", "fsdp"), None)) + specs + (cells,),
        out_specs=(cells, cells) + specs,
        check_vma=False,
    )
```

```python
import functools

import jax
import jax.numpy as jnp
from jax import lax
from jax.experimental import pallas as pl
from jax.experimental.pallas import tpu as pltpu
from jax.sharding import PartitionSpec as P

H = 8
HD = 64
SCALE = HD ** (-0.5)
NORM_EPSILON = 1e-05
MASK_FILL = -1e30
SAFE_SCORE = 50.0

CHUNK = 672
ROWS = 480
SPLITS = 1
STAGES = 7
ONES = 16
EXTRA = 16
LANES = 128
CUT = 512
LOG2E = 1.4426950408889634
TRIPLE = 3 * LANES
GROUPS = ((0, 2), (2, 2))

F32 = jnp.float32
BF16 = jnp.bfloat16

SQUARES = (2, 4, 5, 7, 11, 13)
VECTORS = (3, 6, 8, 9, 10, 12, 14, 15, 16)
MIDDLE_VECTORS = 7


def dot(left, right, left_dim=1, right_dim=0):
    return lax.dot_general(
        left, right, (((left_dim,), (right_dim,)), ((), ())), preferred_element_type=F32
    )


def params(mebibytes):
    return pltpu.CompilerParams(vmem_limit_bytes=mebibytes << 20)


def cost(flops, moved):
    return pl.CostEstimate(flops=int(flops), bytes_accessed=int(moved), transcendentals=0)


def offsets(shards):
    held, mask = [0], shards // 2
    while mask:
        held = held + [offset ^ mask for offset in held]
        mask //= 2
    return held


def pack_kernel(*refs):
    flags_ref, squares, vectors = refs[0], refs[1:7], refs[7:16]
    early_ref, late_ref, scalars_ref = refs[16:]
    block = squares[0].shape[0]
    for i in range(3):
        early_ref[i * block : (i + 1) * block, :] = squares[i][...]
        late_ref[i * block : (i + 1) * block, :] = squares[3 + i][...]
    rows = [vector[...].astype(F32).reshape(1, -1) for vector in vectors]
    rows = jnp.concatenate(rows + [jnp.zeros((EXTRA - len(rows), block), F32)], axis=0)
    early_ref[3 * block :, :] = jnp.zeros((EXTRA, early_ref.shape[1]), BF16)
    early_ref[3 * block :, 0:block] = rows.astype(BF16)
    flagged = jnp.where(flags_ref[...] > 0, 1.0, 0.0)
    cells = flags_ref.shape[0]
    for cell in range(cells):
        scalars_ref[cell] = jnp.sum(flagged[cell : cell + 1, :]).astype(jnp.int32)
    scalars_ref[cells] = lax.axis_index("fsdp")


def pack(flags, squares, vectors):
    block, width = squares[0].shape
    cells = flags.shape[0]
    vmem = pl.BlockSpec(memory_space=pltpu.VMEM)
    return pl.pallas_call(
        pack_kernel,
        out_shape=(
            jax.ShapeDtypeStruct((3 * block + EXTRA, width), BF16),
            jax.ShapeDtypeStruct((3 * block, width), BF16),
            jax.ShapeDtypeStruct((cells + 1,), jnp.int32),
        ),
        in_specs=[vmem] * 16,
        out_specs=[vmem, vmem, pl.BlockSpec(memory_space=pltpu.SMEM)],
        compiler_params=params(60),
        name="pack",
    )(flags, *squares, *vectors)


def gather_kernel(scalars_ref, flags_ref, x_ref, xc_ref, xt_ref, pos_ref):
    known = scalars_ref[pl.program_id(0)]
    length, width = x_ref.shape[1], x_ref.shape[2]
    flagged = flags_ref[pl.ds(pl.program_id(0), 1), :] > 0
    before = lax.broadcasted_iota(jnp.int32, (length, length), 0)
    after = lax.broadcasted_iota(jnp.int32, (length, length), 1)
    upper = jnp.where(before <= after, 1.0, 0.0).astype(BF16)
    marks = jnp.broadcast_to(jnp.where(flagged, 1.0, 0.0), (16, length)).astype(BF16)
    place = dot(marks, upper)[0:1, :].astype(jnp.int32) - 1
    place = jnp.where(flagged, place, -1)
    pos_ref[0] = place

    for chunk in range(xc_ref.shape[1] // CHUNK):

        @pl.when((chunk == 0) | (chunk * CHUNK < known))
        def _():
            target = chunk * CHUNK + lax.broadcasted_iota(jnp.int32, (CHUNK, length), 0)
            target = jnp.where(known > 0, jnp.minimum(target, known - 1), -2)
            chosen = jnp.where(place == target, 1.0, 0.0).astype(BF16)
            xc_ref[0, chunk * CHUNK : (chunk + 1) * CHUNK, :] = dot(chosen, x_ref[0]).astype(BF16)

    xt_ref[0, 0:width, :] = x_ref[0].T
    xt_ref[0, width:, :] = jnp.ones((ONES, length), BF16)


def gather_known(scalars, flags, x):
    cells, length, width = x.shape
    padded = -(-length // CHUNK) * CHUNK
    one = lambda *shape: pl.BlockSpec((1,) + shape, lambda i, s: (i, 0, 0))
    return pl.pallas_call(
        gather_kernel,
        out_shape=(
            jax.ShapeDtypeStruct((cells, padded, width), BF16),
            jax.ShapeDtypeStruct((cells, width + ONES, length), BF16),
            jax.ShapeDtypeStruct((cells, 1, length), jnp.int32),
        ),
        grid_spec=pltpu.PrefetchScalarGridSpec(
            num_scalar_prefetch=1,
            grid=(cells,),
            in_specs=[pl.BlockSpec(flags.shape, lambda i, s: (0, 0)), one(length, width)],
            out_specs=[one(padded, width), one(width + ONES, length), one(1, length)],
        ),
        compiler_params=params(60),
        cost_estimate=cost(cells * 2e9, cells * 6e6),
        name="gather_known",
    )(scalars, flags, x)


def as_column(row):
    return jnp.broadcast_to(row, (LANES, LANES)).T[:, 0:1]


def attend_kernel(*refs, held, cells):
    scalars_ref, refs = refs[0], refs[1:]
    pieces, refs = refs[: len(held)], refs[len(held) :]
    (
        xt_ref, xc_ref, pos_ref,
        w_ref, vec_ref, qkv_ref, kct_ref, vc_ref, e_ref, more_ref, top_ref, ot_ref, o_ref, lse_ref, own_ref,
        bias, qz, kc, vct, top, own, acc, spill,
    ) = refs
    cell, pair = pl.program_id(0), pl.program_id(1)
    known = scalars_ref[cell]
    me = scalars_ref[cells]
    width, length = w_ref.shape[0], xt_ref.shape[2]
    pairs = width // LANES
    block = width // len(held)

    @pl.when((cell == 0) & (pair == 0))
    def _():
        for offset, piece in zip(held, pieces):
            owner = me ^ offset
            rows = pl.ds(pl.multiple_of(owner * block, block), block)
            for which in range(3):
                for p in range(pairs):
                    col = p * TRIPLE + which * LANES
                    w_ref[rows, col : col + LANES] = piece[
                        which * block : (which + 1) * block, p * LANES : (p + 1) * LANES
                    ]
            vec_ref[:, rows] = piece[3 * block :, 0:block].astype(F32)
        qz[...] = jnp.zeros_like(qz)
        for p in range(pairs):
            cols = slice(p * LANES, (p + 1) * LANES)
            bias[p, :, 0:1] = as_column(vec_ref[0:1, cols])
            bias[p, :, 1:2] = as_column(vec_ref[1:2, cols])

    col = pl.multiple_of(pair * TRIPLE, LANES)
    part = lambda first, count: w_ref[:, pl.ds(col + first * LANES, count * LANES)]
    hidden = pos_ref[0] < 0
    steps = (known + CHUNK - 1) // CHUNK
    value_bias = vec_ref[1:2, pl.ds(pl.multiple_of(pair * LANES, LANES), LANES)]
    tokens = xt_ref[0, 0:width, :]
    heads = [slice(side * HD, (side + 1) * HD) for side in range(2)]
    cuts = [slice(start, min(start + CUT, length)) for start in range(0, length, CUT)]

    def project(chunk):
        rows = pl.ds(pl.multiple_of(chunk * CHUNK, 16), CHUNK)
        packed = dot(xc_ref[0, rows, :], part(1, 2))
        yield
        row = chunk * CHUNK + lax.broadcasted_iota(jnp.int32, (CHUNK, LANES), 0)
        keys = packed[:, 0:LANES]
        kc[...] = keys.astype(BF16)
        kct_ref[0, 0, chunk] = jnp.where(row < known, keys, 0.0).astype(BF16).T
        yield
        values = packed[:, LANES:] + value_bias
        vc_ref[0, 0, rows, :] = values.astype(BF16)
        values = jnp.where(row < known, values, 0.0).astype(BF16).T
        counted = chunk * CHUNK + lax.broadcasted_iota(jnp.int32, (EXTRA, CHUNK), 1)
        counted = jnp.where(counted < known, 1.0, 0.0).astype(BF16)
        for side in range(2):
            vct[side, 0:HD, :] = values[heads[side], :]
            vct[side, HD:, :] = counted
        yield

    def begin(side, shifted):
        weight = jnp.ones((1, length), F32) if shifted else jnp.exp(own[side])
        weight = jnp.where(hidden, weight, 0.0).astype(BF16).astype(F32)
        top[side] = jnp.where(hidden, own[side], MASK_FILL) if shifted else jnp.zeros((1, length), F32)
        return weight

    def own_values(side):
        return qkv_ref[0, 0, 2 * LANES + side * HD : 2 * LANES + (side + 1) * HD, :].astype(F32)

    def measure(side):
        q = qkv_ref[0, 0, heads[side], :].astype(F32)
        k = qkv_ref[0, 0, LANES + side * HD : LANES + (side + 1) * HD, :].astype(F32)
        own[side] = jnp.sum(q * k, axis=0, keepdims=True) * SCALE
        longest_q = jnp.max(jnp.sum(q * q, axis=0, keepdims=True))
        longest_k = jnp.max(jnp.sum(k * k, axis=0, keepdims=True))
        return longest_q * longest_k < (SAFE_SCORE / SCALE) * (SAFE_SCORE / SCALE)

    def conclude(side):
        total = acc[side, HD : HD + 1, :]
        ot_ref[0, heads[side], :] = (acc[side, 0:HD, :] * (1.0 / total)).astype(BF16)
        lse_ref[0, side] = top[side] + jnp.log(total)
        own_ref[0, side] = own[side]

    first = project(0)
    next(first)
    turned = dot(part(0, 1), tokens, 0, 0)
    next(first)
    queries = (turned + bias[pair, :, 0:1]).astype(BF16)
    turned = dot(part(1, 1), tokens, 0, 0)
    qkv_ref[0, 0, 0:LANES, :] = queries
    for side in range(2):
        qz[side, heads[side], :] = queries[heads[side], :]
    next(first)
    qkv_ref[0, 0, LANES : 2 * LANES, :] = turned.astype(BF16)
    turned = dot(part(2, 1), tokens, 0, 0)
    weights = []
    safe = None
    for side in range(2):
        for cut in cuts:
            scores = dot(kc[...], qz[side, :, cut])
            e_ref[0, 0, side, :, cut] = jnp.exp2(scores * (SCALE * LOG2E)).astype(BF16)
            if side == 0 and cut is cuts[0]:
                qkv_ref[0, 0, 2 * LANES :, :] = (turned + bias[pair, :, 1:2]).astype(BF16)
            if cut is cuts[1]:
                bounded = measure(side)
                safe = bounded if safe is None else safe & bounded
                weights.append(begin(side, False))
        total = dot(vct[side], e_ref[0, 0, side])
        acc[side, 0:HD, :] = total[0:HD, :] + weights[side] * own_values(side)
        acc[side, HD:, :] = total[HD:, :] + weights[side]
    for side in range(2):
        conclude(side)
        top_ref[0, 0, 0, side] = top[side]
    o_ref[0] = ot_ref[0].T

    def weigh(chunk, side, exps, shifted):
        scores = dot(kc[...], qz[side]) * SCALE
        if shifted:
            peak = jnp.maximum(top[side], jnp.max(scores, axis=0, keepdims=True))
            peak = jnp.where(known > 0, peak, top[side])
            scores = jnp.minimum(scores - peak, 0.0)
        probs = jnp.exp(scores).astype(BF16)
        exps[side] = probs
        if shifted:
            acc[side] = acc[side] * jnp.exp(top[side] - peak) + dot(vct[side], probs)
            top[side] = peak
        else:
            acc[side] += dot(vct[side], probs)
        top_ref[0, 0, chunk, side] = top[side]

    @pl.when(jnp.logical_not(safe))
    def _():
        for side in range(2):
            weight = begin(side, True)
            acc[side, 0:HD, :] = weight * own_values(side)
            acc[side, HD:, :] = jnp.broadcast_to(weight, (EXTRA, length))
            weigh(0, side, e_ref.at[0, 0], True)

    def later_chunk(chunk, carry):
        for _ in project(chunk):
            pass

        @pl.when(safe)
        def _():
            for side in range(2):
                weigh(chunk, side, spill, False)

        @pl.when(jnp.logical_not(safe))
        def _():
            for side in range(2):
                weigh(chunk, side, spill, True)

        pltpu.sync_copy(spill, more_ref.at[cell, pair, chunk - 1])
        return carry

    lax.fori_loop(1, steps, later_chunk, 0)

    @pl.when(jnp.logical_not(safe) | (steps > 1))
    def _():
        for side in range(2):
            conclude(side)
        o_ref[0] = ot_ref[0].T


def attend(scalars, held, pieces, xt, xc, pos):
    cells, length = xt.shape[0], xt.shape[2]
    width = xt.shape[1] - ONES
    padded = xc.shape[1]
    pairs = width // LANES
    chunks = padded // CHUNK
    full = lambda *shape: pl.BlockSpec(shape, lambda c, p, s: (0,) * len(shape))
    shape = jax.ShapeDtypeStruct
    return pl.pallas_call(
        functools.partial(attend_kernel, held=held, cells=cells),
        out_shape=(
            shape((width, 3 * width), BF16),
            shape((EXTRA, width), F32),
            shape((cells, pairs, TRIPLE, length), BF16),
            shape((cells, pairs, chunks, LANES, CHUNK), BF16),
            shape((cells, pairs, padded, LANES), BF16),
            shape((cells, pairs, 2, CHUNK, length), BF16),
            shape((cells, pairs, max(chunks - 1, 1), 2, CHUNK, length), BF16),
            shape((cells, pairs, chunks, 2, 1, length), F32),
            shape((cells, width, length), BF16),
            shape((cells, length, width), BF16),
            shape((cells, H, 1, length), F32),
            shape((cells, H, 1, length), F32),
        ),
        grid_spec=pltpu.PrefetchScalarGridSpec(
            num_scalar_prefetch=1,
            grid=(cells, pairs),
            in_specs=[full(*piece.shape) for piece in pieces]
            + [
                pl.BlockSpec((1, width + ONES, length), lambda c, p, s: (c, 0, 0)),
                pl.BlockSpec((1, padded, width), lambda c, p, s: (c, 0, 0)),
                pl.BlockSpec((1, 1, length), lambda c, p, s: (c, 0, 0)),
            ],
            out_specs=[
                full(width, 3 * width),
                full(EXTRA, width),
                pl.BlockSpec((1, 1, TRIPLE, length), lambda c, p, s: (c, p, 0, 0)),
                pl.BlockSpec((1, 1, chunks, LANES, CHUNK), lambda c, p, s: (c, p, 0, 0, 0)),
                pl.BlockSpec((1, 1, padded, LANES), lambda c, p, s: (c, p, 0, 0)),
                pl.BlockSpec((1, 1, 2, CHUNK, length), lambda c, p, s: (c, p, 0, 0, 0)),
                pl.BlockSpec(memory_space=pl.ANY),
                pl.BlockSpec((1, 1, chunks, 2, 1, length), lambda c, p, s: (c, p, 0, 0, 0, 0)),
                pl.BlockSpec((1, LANES, length), lambda c, p, s: (c, p, 0)),
                pl.BlockSpec((1, length, LANES), lambda c, p, s: (c, 0, p)),
                pl.BlockSpec((1, 2, 1, length), lambda c, p, s: (c, p, 0, 0)),
                pl.BlockSpec((1, 2, 1, length), lambda c, p, s: (c, p, 0, 0)),
            ],
            scratch_shapes=[
                pltpu.VMEM((pairs, LANES, 8), F32),
                pltpu.VMEM((2, LANES, length), BF16),
                pltpu.VMEM((CHUNK, LANES), BF16),
                pltpu.VMEM((2, HD + EXTRA, CHUNK), BF16),
                pltpu.VMEM((2, 1, length), F32),
                pltpu.VMEM((2, 1, length), F32),
                pltpu.VMEM((2, HD + EXTRA, length), F32),
                pltpu.VMEM((2, CHUNK, length), BF16),
            ],
        ),
        compiler_params=params(52),
        cost_estimate=cost(cells * 1e10, cells * 2.5e7),
        name="attend",
    )(scalars, *pieces, xt, xc, pos)


def row_mean(rows):
    return jnp.mean(rows, axis=-1, keepdims=True)


def normalize(rows):
    centred = rows - row_mean(rows)
    scale = lax.rsqrt(row_mean(centred * centred) + NORM_EPSILON)
    return centred * scale, scale


def norm_back(grad, normed, scale):
    return scale * (grad - row_mean(grad) - normed * row_mean(grad * normed))


def column_sum(rows):
    return jnp.sum(rows, axis=0, keepdims=True)


def middle_kernel(*refs, held, cells):
    scalars_ref, refs = refs[0], refs[1:]
    pieces, refs = refs[: len(held)], refs[len(held) :]
    (
        x_ref, o_ref, cot_ref, vec_ref,
        result_ref, dhid_ref, datt_ref, keep_ref, send_ref,
        w, go, gu, gd, gvec,
    ) = refs
    me = scalars_ref[cells]
    width = x_ref.shape[1]
    block = width // len(held)

    @pl.when(pl.program_id(0) == 0)
    def _():
        for offset, piece in zip(held, pieces):
            rows = pl.ds(pl.multiple_of((me ^ offset) * block, block), block)
            for which in range(3):
                w[which, rows, :] = piece[which * block : (which + 1) * block, :]
        go[...] = jnp.zeros_like(go)
        gu[...] = jnp.zeros_like(gu)
        gd[...] = jnp.zeros_like(gd)
        gvec[...] = jnp.zeros_like(gvec)

    def stages(rows):
        out_bias, gain_one, shift_one, up_bias, down_bias, gain_two, shift_two = (
            vec_ref[2 + i : 3 + i, :] for i in range(MIDDLE_VECTORS)
        )
        attended = o_ref[rows, :]
        product = dot(attended, w[0])
        yield
        norm_one, scale_one = normalize(x_ref[rows, :].astype(F32) + (product + out_bias))
        first_norm = norm_one * gain_one + shift_one
        first_low = first_norm.astype(BF16)
        product = dot(first_low, w[1])
        yield
        pre_act = product + up_bias
        below = 0.5 * (1.0 + lax.erf(pre_act * (0.5**0.5)))
        activated = (pre_act * below).astype(BF16)
        product = dot(activated, w[2])
        slope = below + pre_act * (jnp.exp(-0.5 * pre_act * pre_act) * 0.3989422804014327)
        yield
        norm_two, scale_two = normalize(first_norm + (product + down_bias))
        result_ref[rows, :] = (norm_two * gain_two + shift_two).astype(BF16)
        dy = cot_ref[rows, :].astype(F32)
        d_second = norm_back(dy * gain_two, norm_two, scale_two)
        d_ff = d_second.astype(BF16)
        product = dot(d_ff, w[2], 1, 1)
        gvec[4:5, :] += column_sum(d_ff.astype(F32))
        gvec[5:6, :] += column_sum(dy * norm_two)
        gvec[6:7, :] += column_sum(dy)
        yield
        d_pre = (product * slope).astype(BF16)
        product = dot(d_pre, w[1], 1, 1)
        gd[...] += dot(activated, d_ff, 0, 0)
        gvec[3:4, :] += column_sum(d_pre.astype(F32))
        yield
        d_first = d_second + product
        d_hidden = norm_back(d_first * gain_one, norm_one, scale_one)
        d_attn = d_hidden.astype(BF16)
        dhid_ref[rows, :] = d_attn
        product = dot(d_attn, w[0], 1, 1)
        gu[...] += dot(first_low, d_pre, 0, 0)
        gvec[0:1, :] += column_sum(d_attn.astype(F32))
        gvec[1:2, :] += column_sum(d_first * norm_one)
        gvec[2:3, :] += column_sum(d_first)
        yield
        datt_ref[rows, :] = product.astype(BF16)
        go[...] += dot(attended, d_attn, 0, 0)
        yield

    step = x_ref.shape[0] // SPLITS
    live = [stages(slice(i * step, (i + 1) * step)) for i in range(SPLITS)]
    for turn in range(STAGES + SPLITS - 1):
        for i, part in enumerate(live):
            if 0 <= turn - i < STAGES:
                next(part)

    @pl.when(pl.program_id(0) == pl.num_programs(0) - 1)
    def _():
        for offset in range(len(held)):
            target = (keep_ref, send_ref)[offset % 2].at[offset // 2]
            rows = pl.ds(pl.multiple_of((me ^ offset) * block, block), block)
            for which, grad in enumerate((go, gu, gd)):
                cols = slice(which * width, (which + 1) * width)
                target[0:block, cols] = grad[rows, :].astype(BF16)
            target[block:, :] = jnp.zeros((EXTRA, 3 * width), BF16)
            target[block:, 0:block] = gvec[:, rows].astype(BF16)


def middle(scalars, held, pieces, x, o, cot, vec, cells):
    rows, width = x.shape
    step = ROWS if rows % ROWS == 0 else rows
    block = pl.BlockSpec((step, width), lambda i, s: (i, 0))
    full = lambda *shape: pl.BlockSpec(shape, lambda i, s: (0,) * len(shape))
    low = jax.ShapeDtypeStruct((rows, width), BF16)
    half = (len(held) // 2, width // len(held) + EXTRA, 3 * width)
    return pl.pallas_call(
        functools.partial(middle_kernel, held=held, cells=cells),
        out_shape=(low, low, low, jax.ShapeDtypeStruct(half, BF16), jax.ShapeDtypeStruct(half, BF16)),
        grid_spec=pltpu.PrefetchScalarGridSpec(
            num_scalar_prefetch=1,
            grid=(rows // step,),
            in_specs=[full(*piece.shape) for piece in pieces] + [block, block, block, full(EXTRA, width)],
            out_specs=[block, block, block, full(*half), full(*half)],
            scratch_shapes=[
                pltpu.VMEM((3, width, width), BF16),
                pltpu.VMEM((width, width), F32),
                pltpu.VMEM((width, width), F32),
                pltpu.VMEM((width, width), F32),
                pltpu.VMEM((EXTRA, width), F32),
            ],
        ),
        compiler_params=params(50),
        cost_estimate=cost(rows * 5e6, rows * 8e3),
        name="middle",
    )(scalars, *pieces, x, o, cot, vec)


def back_kernel(
    scalars_ref, pos_ref, xt_ref, qkv_ref, kct_ref, vc_ref, e_ref, more_ref, top_ref, ot_ref, lse_ref,
    own_ref, datt_ref,
    dt_ref, keep_ref, send_ref,
    hot, oz, og, ds, joined, dqa, dkv, self_q, self_kv, delta, grad, term, spill,
    *, shards, cells, first_pair,
):
    pair, cell = pl.program_id(0), pl.program_id(1)
    known = scalars_ref[cell]
    me = scalars_ref[cells]
    width, length = xt_ref.shape[1] - ONES, xt_ref.shape[2]
    block = width // shards
    steps = (known + CHUNK - 1) // CHUNK
    place = pos_ref[0]
    hidden = place < 0

    @pl.when(pair == 0)
    def _():
        hot[cell, 0] = jnp.where(
            place == lax.broadcasted_iota(jnp.int32, (CHUNK, length), 0), 1.0, 0.0
        ).astype(BF16)

        def mark(chunk, carry):
            row = chunk * CHUNK + lax.broadcasted_iota(jnp.int32, (CHUNK, length), 0)
            hot[cell, chunk] = jnp.where(place == row, 1.0, 0.0).astype(BF16)
            return carry

        lax.fori_loop(1, steps, mark, 0)

    heads = [slice(side * HD, (side + 1) * HD) for side in range(2)]
    cuts = [slice(start, min(start + CUT, length)) for start in range(0, length, CUT)]
    queries = qkv_ref.at[0, 0, 0:LANES]

    @pl.when((pair == 0) & (cell == 0))
    def _():
        oz[...] = jnp.zeros_like(oz)

    og[...] = datt_ref[0].T

    def share(chunk, side):
        return jnp.exp(top_ref[0, 0, chunk, side] - lse_ref[0, side])

    def outset(side):
        rows = heads[side]
        grads = og[rows, :].astype(F32)
        query = queries[rows, :].astype(F32) * SCALE
        key = qkv_ref[0, 0, LANES + side * HD : LANES + (side + 1) * HD, :].astype(F32)
        value = qkv_ref[0, 0, 2 * LANES + side * HD : 2 * LANES + (side + 1) * HD, :].astype(F32)
        prob = jnp.exp(jnp.where(hidden, own_ref[0, side], MASK_FILL) - lse_ref[0, side])
        own_grad = jnp.sum(grads * value, axis=0, keepdims=True)
        back = (prob * (own_grad - delta[side])).astype(BF16).astype(F32)
        self_q[rows, :] = back * key
        self_kv[rows, :] = back * query
        self_kv[LANES + side * HD : LANES + (side + 1) * HD, :] = prob.astype(BF16).astype(F32) * grads

    def score_grads(chunk, side, exps, values, cut, scaled):
        part = dot(values, oz[side, :, cut]) - scaled[:, cut]
        ds[side, :, cut] = (exps[side, :, cut].astype(F32) * part).astype(BF16)

    def spread(chunk, side, part):
        scaled = share(chunk, side)
        oz[side, heads[side], :] = (og[heads[side], :].astype(F32) * scaled).astype(BF16)
        return delta[side] * scaled

    def close(q_part, kv_part):
        dt_ref[0, 0, 0:LANES, :] = ((q_part + self_q[...]) * SCALE).astype(BF16)
        dt_ref[0, 0, LANES:, :] = (kv_part + self_kv[...]).astype(BF16)
        term[...] = dot(xt_ref[0], dt_ref[0, 0], 1, 1)

    exps = e_ref.at[0, 0]
    values = vc_ref[0, 0, 0:CHUNK, :]
    for side in range(2):
        rows = heads[side]
        delta[side] = jnp.sum(
            og[rows, :].astype(F32) * ot_ref[0, rows, :].astype(F32), axis=0, keepdims=True
        )
    scaled = [spread(0, side, None) for side in range(2)]
    for cut in cuts:
        score_grads(0, 0, exps, values, cut, scaled[0])
    d_values = dot(exps[0], oz[0], 1, 1)
    outset(0)
    for cut in cuts:
        score_grads(0, 1, exps, values, cut, scaled[1])
    d_keys = dot(ds[0], queries[...], 1, 1)
    outset(1)
    d_values += dot(exps[1], oz[1], 1, 1)
    lanes = lax.broadcasted_iota(jnp.int32, (CHUNK, LANES), 1) < HD
    joined[:, LANES:] = d_values.astype(BF16)
    dqa[0:HD, :] = dot(kct_ref[0, 0, 0, 0:HD, :], ds[0])
    d_keys = jnp.where(lanes, d_keys, dot(ds[1], queries[...], 1, 1)) * SCALE
    dqa[HD:, :] = dot(kct_ref[0, 0, 0, HD:, :], ds[1])
    joined[:, 0:LANES] = d_keys.astype(BF16)
    dkv[...] = dot(joined[...], hot[cell, 0], 0, 0)
    close(dqa[...], dkv[...])

    def later_chunk(chunk, carry):
        pltpu.sync_copy(more_ref.at[cell, first_pair + pair, chunk - 1], spill)
        values = vc_ref[0, 0, pl.ds(pl.multiple_of(chunk * CHUNK, 16), CHUNK), :]
        d_values = jnp.zeros((CHUNK, LANES), F32)
        for side in range(2):
            scaled = spread(chunk, side, None)
            for cut in cuts:
                score_grads(chunk, side, spill, values, cut, scaled)
            d_values += dot(spill[side], oz[side], 1, 1)
            dqa[heads[side], :] += dot(kct_ref[0, 0, chunk, heads[side], :], ds[side])
        d_keys = jnp.where(lanes, dot(ds[0], queries[...], 1, 1), dot(ds[1], queries[...], 1, 1)) * SCALE
        joined[:, 0:LANES] = d_keys.astype(BF16)
        joined[:, LANES:] = d_values.astype(BF16)
        dkv[...] += dot(joined[...], hot[cell, chunk], 0, 0)
        return carry

    @pl.when(steps > 1)
    def _():
        lax.fori_loop(1, steps, later_chunk, 0)
        close(dqa[...], dkv[...])

    @pl.when(cell == 0)
    def _():
        grad[...] = term[...]

    @pl.when(cell > 0)
    def _():
        grad[...] += term[...]

    @pl.when(cell == cells - 1)
    def _():
        for offset in range(shards):
            owner = me ^ offset
            target = (keep_ref, send_ref)[offset % 2].at[offset // 2, 0]
            rows = pl.ds(pl.multiple_of(owner * block, block), block)
            target[0:block, :] = grad[rows, :].astype(BF16)
            ours = jnp.where(owner == first_pair + pair, 1.0, 0.0)
            target[block:, :] = (grad[width:, :] * ours).astype(BF16)


def attend_back(group, shards, scalars, pos, xt, qkv, kct, vc, e, more, top, ot, lse, own, datt):
    first, count = group
    cells, length = xt.shape[0], xt.shape[2]
    width = xt.shape[1] - ONES
    padded = vc.shape[2]
    chunks = padded // CHUNK
    half = (shards // 2, count, width // shards + EXTRA, TRIPLE)
    part = pl.BlockSpec((shards // 2, 1) + half[2:], lambda p, c, s: (0, p, 0, 0))
    shape = jax.ShapeDtypeStruct
    return pl.pallas_call(
        functools.partial(back_kernel, shards=shards, cells=cells, first_pair=first),
        out_shape=(shape((cells, count, TRIPLE, length), BF16), shape(half, BF16), shape(half, BF16)),
        grid_spec=pltpu.PrefetchScalarGridSpec(
            num_scalar_prefetch=1,
            grid=(count, cells),
            in_specs=[
                pl.BlockSpec((1, 1, length), lambda p, c, s: (c, 0, 0)),
                pl.BlockSpec((1, width + ONES, length), lambda p, c, s: (c, 0, 0)),
                pl.BlockSpec((1, 1, TRIPLE, length), lambda p, c, s: (c, first + p, 0, 0)),
                pl.BlockSpec((1, 1, chunks, LANES, CHUNK), lambda p, c, s: (c, first + p, 0, 0, 0)),
                pl.BlockSpec((1, 1, padded, LANES), lambda p, c, s: (c, first + p, 0, 0)),
                pl.BlockSpec((1, 1, 2, CHUNK, length), lambda p, c, s: (c, first + p, 0, 0, 0)),
                pl.BlockSpec(memory_space=pl.ANY),
                pl.BlockSpec((1, 1, chunks, 2, 1, length), lambda p, c, s: (c, first + p, 0, 0, 0, 0)),
                pl.BlockSpec((1, LANES, length), lambda p, c, s: (c, first + p, 0)),
                pl.BlockSpec((1, 2, 1, length), lambda p, c, s: (c, first + p, 0, 0)),
                pl.BlockSpec((1, 2, 1, length), lambda p, c, s: (c, first + p, 0, 0)),
                pl.BlockSpec((1, length, LANES), lambda p, c, s: (c, 0, first + p)),
            ],
            out_specs=[
                pl.BlockSpec((1, 1, TRIPLE, length), lambda p, c, s: (c, p, 0, 0)),
                part,
                part,
            ],
            scratch_shapes=[
                pltpu.VMEM((cells, chunks, CHUNK, length), BF16),
                pltpu.VMEM((2, LANES, length), BF16),
                pltpu.VMEM((LANES, length), BF16),
                pltpu.VMEM((2, CHUNK, length), BF16),
                pltpu.VMEM((CHUNK, 2 * LANES), BF16),
                pltpu.VMEM((LANES, length), F32),
                pltpu.VMEM((2 * LANES, length), F32),
                pltpu.VMEM((LANES, length), F32),
                pltpu.VMEM((2 * LANES, length), F32),
                pltpu.VMEM((2, 1, length), F32),
                pltpu.VMEM((width + ONES, TRIPLE), F32),
                pltpu.VMEM((width + ONES, TRIPLE), F32),
                pltpu.VMEM((2, CHUNK, length), BF16),
            ],
        ),
        compiler_params=params(51),
        cost_estimate=cost(cells * count * 6e9, cells * count * 7e6),
        name="attend_back",
    )(scalars, pos, xt, qkv, kct, vc, e, more, top, ot, lse, own, datt)


def input_kernel(w_ref, dhid_ref, *refs):
    parts, out_ref = refs[:-1], refs[-1]
    back, col = None, 0
    for part in parts:
        rows = part.shape[1]
        term = dot(w_ref[:, col : col + rows], part[0])
        back = term if back is None else back + term
        col += rows
    out_ref[0] = (back.T + dhid_ref[0].astype(F32)).astype(BF16)


def input_grad(w, dhid, parts):
    cells, length, width = dhid.shape
    parts = [part.reshape(cells, -1, length) for part in parts]
    block = pl.BlockSpec((1, length, width), lambda i: (i, 0, 0))
    return pl.pallas_call(
        input_kernel,
        out_shape=jax.ShapeDtypeStruct(dhid.shape, BF16),
        grid=(cells,),
        in_specs=[pl.BlockSpec(w.shape, lambda i: (0, 0)), block]
        + [pl.BlockSpec((1,) + part.shape[1:], lambda i: (i, 0, 0)) for part in parts],
        out_specs=block,
        compiler_params=params(28),
        cost_estimate=cost(cells * 2e9, cells * 8e6),
        name="input_grad",
    )(w, dhid, *parts)


def finish_kernel(*refs):
    terms, halves, outs = refs[:2], refs[2:-15], refs[-15:]
    block, width = outs[0].shape
    for which in range(3):
        cols = slice(which * width, (which + 1) * width)
        outs[3 + which][...] = terms[0][0:block, cols].astype(F32) + terms[1][0:block, cols].astype(F32)
    rows = terms[0][block:, 0:block].astype(F32) + terms[1][block:, 0:block].astype(F32)
    for row in range(MIDDLE_VECTORS):
        outs[8 + row][...] = rows[row : row + 1, :].reshape(block)

    def write(order):
        biases = [jnp.zeros((1, LANES), F32), jnp.zeros((1, LANES), F32)]
        pair = 0
        for group in range(0, len(halves), 2):
            for part in [halves[group + i] for i in order]:
                for p in range(part.shape[0]):
                    for which in range(3):
                        cols = slice(which * LANES, (which + 1) * LANES)
                        outs[which][:, pair * LANES : (pair + 1) * LANES] = part[p, 0:block, cols].astype(F32)
                    biases[0] += part[p, block : block + 1, 0:LANES].astype(F32)
                    biases[1] += part[p, block : block + 1, 2 * LANES :].astype(F32)
                    pair += 1
        outs[6][...] = biases[0].reshape(block)
        outs[7][...] = biases[1].reshape(block)

    low = lax.axis_index("dp") % 2 == 0

    @pl.when(low)
    def _():
        write((0, 1))

    @pl.when(jnp.logical_not(low))
    def _():
        write((1, 0))


def finish(parts, block, width):
    vmem = pl.BlockSpec(memory_space=pltpu.VMEM)
    return pl.pallas_call(
        finish_kernel,
        out_shape=(jax.ShapeDtypeStruct((block, width), F32),) * 6 + (jax.ShapeDtypeStruct((block,), F32),) * 9,
        in_specs=[vmem] * len(parts),
        out_specs=[vmem] * 15,
        compiler_params=params(16),
        name="finish",
    )(*parts)


def swap(values, axis, mask):
    size = lax.axis_size(axis)
    return lax.ppermute(values, axis, [(i, i ^ mask) for i in range(size)])


def masks(axis):
    found, mask = [], 1
    while mask < lax.axis_size(axis):
        found.append(mask)
        mask *= 2
    return found


def after(value, *others):
    return lax.optimization_barrier((value,) + others)[0]


def gather_pieces(own, beside):
    held = [own]
    for mask in reversed(masks("fsdp")):
        held = held + [swap(piece, "fsdp", mask) for piece in held]
        held = held[:1] + [after(piece, beside) for piece in held[1:]]
    return held


def plus(left, right):
    return left.astype(F32) + right.astype(F32)


class Reduction:
    def __init__(self, keep, send, half_dim=None):
        self.keep, self.send = keep, send
        self.half_dim = half_dim
        order = masks("dp") if half_dim is not None else reversed(masks("dp"))
        self.plan = [("fsdp", mask) for mask in masks("fsdp")] + [("dp", mask) for mask in order]
        self.low = (lax.axis_index("dp") % 2) == 0

    def pair(self):
        return self.keep, self.send

    def start(self, pair=None):
        if self.plan:
            self.keep, self.send = pair or self.pair()
            self.arrived = swap(self.send, *self.plan[0])

    def arrive(self):
        self.plan = self.plan[1:]
        if not self.plan:
            return
        total = plus(self.keep, self.arrived).astype(BF16)
        axis, mask = self.plan[0]
        if axis == "fsdp":
            self.keep, self.send = total[0::2], total[1::2]
        elif mask == 1 and self.half_dim is not None:
            first, second = jnp.split(total, 2, self.half_dim)
            self.keep = jnp.where(self.low, first, second)
            self.send = jnp.where(self.low, second, first)
        else:
            self.keep = self.send = total

    def finish(self):
        while self.plan:
            self.start()
            self.arrive()
        if self.half_dim is None:
            return self.keep[0], self.arrived[0]
        mine = plus(self.keep, self.arrived).astype(BF16)[0]
        if lax.axis_size("dp") == 1:
            return jnp.split(mine, 2, self.half_dim - 1)
        return mine, swap(mine, "dp", 1)


def body(*args):
    tokens, known_flags, cotangent = args[0], args[1], args[17]
    cells, length, width = tokens.shape
    shards = lax.axis_size("fsdp")
    block = width // shards
    held = offsets(shards)

    early, late, scalars = pack(known_flags, [args[i] for i in SQUARES], [args[i] for i in VECTORS])
    xc, xt, pos = gather_known(scalars, known_flags, tokens)
    early = gather_pieces(early, xt)
    late = after(late, *early[:2])
    late = [late] + [swap(late, "fsdp", offset) for offset in held[1:]]
    w, vec, qkv, kct, vc, e, more, top, ot, o, lse, own = attend(scalars, held, early, xt, xc, pos)
    flat = lambda a: a.reshape(cells * length, width)
    result, dhid, datt, keep, send = middle(
        scalars, held, late, flat(tokens), flat(o), flat(cotangent), vec, cells
    )
    cube = lambda a: a.reshape(cells, length, width)
    chains = [Reduction(keep, send)]

    def boundary(value):
        for chain in chains[:-1]:
            chain.arrive()
        newest = chains[-1]
        pairs = lax.optimization_barrier([chain.pair() for chain in chains])
        for chain, (chain.keep, chain.send) in zip(chains, pairs):
            pass
        newest.start()
        newest.arrive()
        value, pairs = lax.optimization_barrier((value, [chain.pair() for chain in chains]))
        for chain, pair in zip(chains, pairs):
            chain.start(pair)
        return value

    parts = []
    for group in GROUPS:
        dt, keep, send = attend_back(
            group, shards, boundary(scalars), pos, xt, qkv, kct, vc, e, more, top, ot, lse, own, cube(datt)
        )
        parts.append(dt)
        chains.append(Reduction(keep, send, 1))
    tokens_grad = input_grad(boundary(w), cube(dhid), parts)
    tokens_grad, arrived = lax.optimization_barrier((tokens_grad, [chain.arrived for chain in chains]))
    for chain, chain.arrived in zip(chains, arrived):
        chain.arrive()
    newest = chains[-1]
    newest.start()
    newest.arrive()
    chains[0].send = after(chains[0].send, newest.send)
    halves = [half for chain in chains for half in chain.finish()]
    summed = finish(halves, block, width)
    out = dict(zip(SQUARES + VECTORS, summed))
    return (cube(result), tokens_grad) + tuple(out[i] for i in range(2, 17))


def solution(mesh):
    cells = P(("dp", "fsdp"), None, None)
    specs = tuple(P("fsdp", None) if i in SQUARES else P("fsdp") for i in range(2, 17))
    return jax.shard_map(
        body,
        mesh=mesh,
        in_specs=(cells, P(("dp", "fsdp"), None)) + specs + (cells,),
        out_specs=(cells, cells) + specs,
        check_vma=False,
    )
```

```python
import functools

import jax
import jax.numpy as jnp
from jax import lax
from jax.experimental import pallas as pl
from jax.experimental.pallas import tpu as pltpu
from jax.sharding import PartitionSpec as P

H = 8
HD = 64
SCALE = HD ** (-0.5)
NORM_EPSILON = 1e-05
MASK_FILL = -1e30
SAFE_SCORE = 50.0

CHUNK = 672
ROWS = 480
SPLITS = 1
STAGES = 7
ONES = 16
EXTRA = 16
LANES = 128
CUT = 512
LOG2E = 1.4426950408889634
TRIPLE = 3 * LANES
GROUPS = ((0, 2), (2, 2))

F32 = jnp.float32
BF16 = jnp.bfloat16

SQUARES = (2, 4, 5, 7, 11, 13)
VECTORS = (3, 6, 8, 9, 10, 12, 14, 15, 16)
MIDDLE_VECTORS = 7


def dot(left, right, left_dim=1, right_dim=0):
    return lax.dot_general(
        left, right, (((left_dim,), (right_dim,)), ((), ())), preferred_element_type=F32
    )


def params(mebibytes):
    return pltpu.CompilerParams(vmem_limit_bytes=mebibytes << 20)


def cost(flops, moved):
    return pl.CostEstimate(flops=int(flops), bytes_accessed=int(moved), transcendentals=0)


def offsets(shards):
    held, mask = [0], shards // 2
    while mask:
        held = held + [offset ^ mask for offset in held]
        mask //= 2
    return held


def pack_kernel(*refs):
    flags_ref, squares, vectors = refs[0], refs[1:7], refs[7:16]
    early_ref, late_ref, scalars_ref = refs[16:]
    block = squares[0].shape[0]
    for i in range(3):
        early_ref[i * block : (i + 1) * block, :] = squares[i][...]
        late_ref[i * block : (i + 1) * block, :] = squares[3 + i][...]
    rows = [vector[...].astype(F32).reshape(1, -1) for vector in vectors]
    rows = jnp.concatenate(rows + [jnp.zeros((EXTRA - len(rows), block), F32)], axis=0)
    early_ref[3 * block :, :] = jnp.zeros((EXTRA, early_ref.shape[1]), BF16)
    early_ref[3 * block :, 0:block] = rows.astype(BF16)
    flagged = jnp.where(flags_ref[...] > 0, 1.0, 0.0)
    cells = flags_ref.shape[0]
    for cell in range(cells):
        scalars_ref[cell] = jnp.sum(flagged[cell : cell + 1, :]).astype(jnp.int32)
    scalars_ref[cells] = lax.axis_index("fsdp")


def pack(flags, squares, vectors):
    block, width = squares[0].shape
    cells = flags.shape[0]
    vmem = pl.BlockSpec(memory_space=pltpu.VMEM)
    return pl.pallas_call(
        pack_kernel,
        out_shape=(
            jax.ShapeDtypeStruct((3 * block + EXTRA, width), BF16),
            jax.ShapeDtypeStruct((3 * block, width), BF16),
            jax.ShapeDtypeStruct((cells + 1,), jnp.int32),
        ),
        in_specs=[vmem] * 16,
        out_specs=[vmem, vmem, pl.BlockSpec(memory_space=pltpu.SMEM)],
        compiler_params=params(60),
        name="pack",
    )(flags, *squares, *vectors)


def gather_kernel(scalars_ref, flags_ref, x_ref, xc_ref, xt_ref, pos_ref):
    known = scalars_ref[pl.program_id(0)]
    length, width = x_ref.shape[1], x_ref.shape[2]
    flagged = flags_ref[pl.ds(pl.program_id(0), 1), :] > 0
    before = lax.broadcasted_iota(jnp.int32, (length, length), 0)
    after = lax.broadcasted_iota(jnp.int32, (length, length), 1)
    upper = jnp.where(before <= after, 1.0, 0.0).astype(BF16)
    marks = jnp.broadcast_to(jnp.where(flagged, 1.0, 0.0), (16, length)).astype(BF16)
    place = dot(marks, upper)[0:1, :].astype(jnp.int32) - 1
    place = jnp.where(flagged, place, -1)
    pos_ref[0] = place

    for chunk in range(xc_ref.shape[1] // CHUNK):

        @pl.when((chunk == 0) | (chunk * CHUNK < known))
        def _():
            target = chunk * CHUNK + lax.broadcasted_iota(jnp.int32, (CHUNK, length), 0)
            target = jnp.where(known > 0, jnp.minimum(target, known - 1), -2)
            chosen = jnp.where(place == target, 1.0, 0.0).astype(BF16)
            xc_ref[0, chunk * CHUNK : (chunk + 1) * CHUNK, :] = dot(chosen, x_ref[0]).astype(BF16)

    xt_ref[0, 0:width, :] = x_ref[0].T
    xt_ref[0, width:, :] = jnp.ones((ONES, length), BF16)


def gather_known(scalars, flags, x):
    cells, length, width = x.shape
    padded = -(-length // CHUNK) * CHUNK
    one = lambda *shape: pl.BlockSpec((1,) + shape, lambda i, s: (i, 0, 0))
    return pl.pallas_call(
        gather_kernel,
        out_shape=(
            jax.ShapeDtypeStruct((cells, padded, width), BF16),
            jax.ShapeDtypeStruct((cells, width + ONES, length), BF16),
            jax.ShapeDtypeStruct((cells, 1, length), jnp.int32),
        ),
        grid_spec=pltpu.PrefetchScalarGridSpec(
            num_scalar_prefetch=1,
            grid=(cells,),
            in_specs=[pl.BlockSpec(flags.shape, lambda i, s: (0, 0)), one(length, width)],
            out_specs=[one(padded, width), one(width + ONES, length), one(1, length)],
        ),
        compiler_params=params(60),
        cost_estimate=cost(cells * 2e9, cells * 6e6),
        name="gather_known",
    )(scalars, flags, x)


def as_column(row):
    return jnp.broadcast_to(row, (LANES, LANES)).T[:, 0:1]


def attend_kernel(*refs, held, cells):
    scalars_ref, refs = refs[0], refs[1:]
    pieces, refs = refs[: len(held)], refs[len(held) :]
    (
        xt_ref, xc_ref, pos_ref,
        w_ref, vec_ref, qkv_ref, kvt_ref, e_ref, more_ref, stats_ref, o_ref,
        bias, qz, kc, vct, top, own, acc, spill,
    ) = refs
    cell, pair = pl.program_id(0), pl.program_id(1)
    known = scalars_ref[cell]
    me = scalars_ref[cells]
    width, length = w_ref.shape[0], xt_ref.shape[2]
    pairs = width // LANES
    block = width // len(held)

    @pl.when((cell == 0) & (pair == 0))
    def _():
        for offset, piece in zip(held, pieces):
            owner = me ^ offset
            rows = pl.ds(pl.multiple_of(owner * block, block), block)
            for which in range(3):
                for p in range(pairs):
                    col = p * TRIPLE + which * LANES
                    w_ref[rows, col : col + LANES] = piece[
                        which * block : (which + 1) * block, p * LANES : (p + 1) * LANES
                    ]
            vec_ref[:, rows] = piece[3 * block :, 0:block].astype(F32)
        qz[...] = jnp.zeros_like(qz)
        for p in range(pairs):
            cols = slice(p * LANES, (p + 1) * LANES)
            bias[p, :, 0:1] = as_column(vec_ref[0:1, cols])
            bias[p, :, 1:2] = as_column(vec_ref[1:2, cols])

    col = pl.multiple_of(pair * TRIPLE, LANES)
    part = lambda first, count: w_ref[:, pl.ds(col + first * LANES, count * LANES)]
    hidden = pos_ref[0] < 0
    steps = (known + CHUNK - 1) // CHUNK
    value_bias = vec_ref[1:2, pl.ds(pl.multiple_of(pair * LANES, LANES), LANES)]
    tokens = xt_ref[0, 0:width, :]
    heads = [slice(side * HD, (side + 1) * HD) for side in range(2)]
    cuts = [slice(start, min(start + CUT, length)) for start in range(0, length, CUT)]

    def project(chunk):
        rows = pl.ds(pl.multiple_of(chunk * CHUNK, 16), CHUNK)
        packed = dot(xc_ref[0, rows, :], part(1, 2))
        yield
        row = chunk * CHUNK + lax.broadcasted_iota(jnp.int32, (CHUNK, LANES), 0)
        keys = packed[:, 0:LANES]
        kc[...] = keys.astype(BF16)
        kvt_ref[0, 0, chunk, 0:LANES, :] = jnp.where(row < known, keys, 0.0).astype(BF16).T
        yield
        values = packed[:, LANES:] + value_bias
        values = jnp.where(row < known, values, 0.0).astype(BF16).T
        kvt_ref[0, 0, chunk, LANES:, :] = values
        counted = chunk * CHUNK + lax.broadcasted_iota(jnp.int32, (EXTRA, CHUNK), 1)
        counted = jnp.where(counted < known, 1.0, 0.0).astype(BF16)
        for side in range(2):
            vct[side, 0:HD, :] = values[heads[side], :]
            vct[side, HD:, :] = counted
        yield

    def begin(side, shifted):
        weight = jnp.ones((1, length), F32) if shifted else jnp.exp(own[side])
        weight = jnp.where(hidden, weight, 0.0).astype(BF16).astype(F32)
        top[side] = jnp.where(hidden, own[side], MASK_FILL) if shifted else jnp.zeros((1, length), F32)
        return weight

    def own_values(side):
        return qkv_ref[0, 0, 2 * LANES + side * HD : 2 * LANES + (side + 1) * HD, :].astype(F32)

    def measure(side):
        q = qkv_ref[0, 0, heads[side], :].astype(F32)
        k = qkv_ref[0, 0, LANES + side * HD : LANES + (side + 1) * HD, :].astype(F32)
        own[side] = jnp.sum(q * k, axis=0, keepdims=True) * SCALE
        longest_q = jnp.max(jnp.sum(q * q, axis=0, keepdims=True))
        longest_k = jnp.max(jnp.sum(k * k, axis=0, keepdims=True))
        return longest_q * longest_k < (SAFE_SCORE / SCALE) * (SAFE_SCORE / SCALE)

    def conclude(side):
        total = acc[side, HD : HD + 1, :]
        rows = slice(TRIPLE + side * HD, TRIPLE + (side + 1) * HD)
        qkv_ref[0, 0, rows, :] = (acc[side, 0:HD, :] * (1.0 / total)).astype(BF16)
        stats_ref[0, 0, side] = top[side] + jnp.log(total)
        stats_ref[0, 0, 2 + side] = own[side]

    first = project(0)
    next(first)
    turned = dot(part(0, 1), tokens, 0, 0)
    next(first)
    queries = (turned + bias[pair, :, 0:1]).astype(BF16)
    turned = dot(part(1, 2), tokens, 0, 0)
    qkv_ref[0, 0, 0:LANES, :] = queries
    for side in range(2):
        qz[side, heads[side], :] = queries[heads[side], :]
    next(first)
    qkv_ref[0, 0, LANES : 2 * LANES, :] = turned[0:LANES, :].astype(BF16)
    weights = []
    safe = None
    for side in range(2):
        for cut in cuts:
            scores = dot(kc[...], qz[side, :, cut])
            e_ref[0, 0, side, :, cut] = jnp.exp2(scores * (SCALE * LOG2E)).astype(BF16)
            if side == 0 and cut is cuts[0]:
                qkv_ref[0, 0, 2 * LANES : TRIPLE, :] = (turned[LANES:, :] + bias[pair, :, 1:2]).astype(BF16)
            if cut is cuts[1]:
                bounded = measure(side)
                safe = bounded if safe is None else safe & bounded
                weights.append(begin(side, False))
        total = dot(vct[side], e_ref[0, 0, side])
        acc[side, 0:HD, :] = total[0:HD, :] + weights[side] * own_values(side)
        acc[side, HD:, :] = total[HD:, :] + weights[side]
    for side in range(2):
        conclude(side)
        stats_ref[0, 0, 4 + side] = top[side]
    o_ref[0] = qkv_ref[0, 0, TRIPLE:, :].T

    def weigh(chunk, side, exps, shifted):
        scores = dot(kc[...], qz[side]) * SCALE
        if shifted:
            peak = jnp.maximum(top[side], jnp.max(scores, axis=0, keepdims=True))
            peak = jnp.where(known > 0, peak, top[side])
            scores = jnp.minimum(scores - peak, 0.0)
        probs = jnp.exp(scores).astype(BF16)
        exps[side] = probs
        if shifted:
            acc[side] = acc[side] * jnp.exp(top[side] - peak) + dot(vct[side], probs)
            top[side] = peak
        else:
            acc[side] += dot(vct[side], probs)
        stats_ref[0, 0, 4 + 2 * chunk + side] = top[side]

    @pl.when(jnp.logical_not(safe))
    def _():
        for side in range(2):
            weight = begin(side, True)
            acc[side, 0:HD, :] = weight * own_values(side)
            acc[side, HD:, :] = jnp.broadcast_to(weight, (EXTRA, length))
            weigh(0, side, e_ref.at[0, 0], True)

    def later_chunk(chunk, carry):
        for _ in project(chunk):
            pass

        @pl.when(safe)
        def _():
            for side in range(2):
                weigh(chunk, side, spill, False)

        @pl.when(jnp.logical_not(safe))
        def _():
            for side in range(2):
                weigh(chunk, side, spill, True)

        pltpu.sync_copy(spill, more_ref.at[cell, pair, chunk - 1])
        return carry

    lax.fori_loop(1, steps, later_chunk, 0)

    @pl.when(jnp.logical_not(safe) | (steps > 1))
    def _():
        for side in range(2):
            conclude(side)
        o_ref[0] = qkv_ref[0, 0, TRIPLE:, :].T


def attend(scalars, held, pieces, xt, xc, pos):
    cells, length = xt.shape[0], xt.shape[2]
    width = xt.shape[1] - ONES
    padded = xc.shape[1]
    pairs = width // LANES
    chunks = padded // CHUNK
    full = lambda *shape: pl.BlockSpec(shape, lambda c, p, s: (0,) * len(shape))
    shape = jax.ShapeDtypeStruct
    return pl.pallas_call(
        functools.partial(attend_kernel, held=held, cells=cells),
        out_shape=(
            shape((width, 3 * width), BF16),
            shape((EXTRA, width), F32),
            shape((cells, pairs, 4 * LANES, length), BF16),
            shape((cells, pairs, chunks, 2 * LANES, CHUNK), BF16),
            shape((cells, pairs, 2, CHUNK, length), BF16),
            shape((cells, pairs, max(chunks - 1, 1), 2, CHUNK, length), BF16),
            shape((cells, pairs, 4 + 2 * chunks, 1, length), F32),
            shape((cells, length, width), BF16),
        ),
        grid_spec=pltpu.PrefetchScalarGridSpec(
            num_scalar_prefetch=1,
            grid=(cells, pairs),
            in_specs=[full(*piece.shape) for piece in pieces]
            + [
                pl.BlockSpec((1, width + ONES, length), lambda c, p, s: (c, 0, 0)),
                pl.BlockSpec((1, padded, width), lambda c, p, s: (c, 0, 0)),
                pl.BlockSpec((1, 1, length), lambda c, p, s: (c, 0, 0)),
            ],
            out_specs=[
                full(width, 3 * width),
                full(EXTRA, width),
                pl.BlockSpec((1, 1, 4 * LANES, length), lambda c, p, s: (c, p, 0, 0)),
                pl.BlockSpec((1, 1, chunks, 2 * LANES, CHUNK), lambda c, p, s: (c, p, 0, 0, 0)),
                pl.BlockSpec((1, 1, 2, CHUNK, length), lambda c, p, s: (c, p, 0, 0, 0)),
                pl.BlockSpec(memory_space=pl.ANY),
                pl.BlockSpec((1, 1, 4 + 2 * chunks, 1, length), lambda c, p, s: (c, p, 0, 0, 0)),
                pl.BlockSpec((1, length, LANES), lambda c, p, s: (c, 0, p)),
            ],
            scratch_shapes=[
                pltpu.VMEM((pairs, LANES, 8), F32),
                pltpu.VMEM((2, LANES, length), BF16),
                pltpu.VMEM((CHUNK, LANES), BF16),
                pltpu.VMEM((2, HD + EXTRA, CHUNK), BF16),
                pltpu.VMEM((2, 1, length), F32),
                pltpu.VMEM((2, 1, length), F32),
                pltpu.VMEM((2, HD + EXTRA, length), F32),
                pltpu.VMEM((2, CHUNK, length), BF16),
            ],
        ),
        compiler_params=params(52),
        cost_estimate=cost(cells * 1e10, cells * 2.5e7),
        name="attend",
    )(scalars, *pieces, xt, xc, pos)


def row_mean(rows):
    return jnp.mean(rows, axis=-1, keepdims=True)


def normalize(rows):
    centred = rows - row_mean(rows)
    scale = lax.rsqrt(row_mean(centred * centred) + NORM_EPSILON)
    return centred * scale, scale


def norm_back(grad, normed, scale):
    return scale * (grad - row_mean(grad) - normed * row_mean(grad * normed))


def column_sum(rows):
    return jnp.sum(rows, axis=0, keepdims=True)


def middle_kernel(*refs, held, cells):
    scalars_ref, refs = refs[0], refs[1:]
    pieces, refs = refs[: len(held)], refs[len(held) :]
    (
        x_ref, o_ref, cot_ref, vec_ref,
        result_ref, dhid_ref, datt_ref, keep_ref, send_ref,
        w, go, gu, gd, gvec,
    ) = refs
    me = scalars_ref[cells]
    width = x_ref.shape[1]
    block = width // len(held)

    @pl.when(pl.program_id(0) == 0)
    def _():
        for offset, piece in zip(held, pieces):
            rows = pl.ds(pl.multiple_of((me ^ offset) * block, block), block)
            for which in range(3):
                w[which, rows, :] = piece[which * block : (which + 1) * block, :]
        go[...] = jnp.zeros_like(go)
        gu[...] = jnp.zeros_like(gu)
        gd[...] = jnp.zeros_like(gd)
        gvec[...] = jnp.zeros_like(gvec)

    def stages(rows):
        out_bias, gain_one, shift_one, up_bias, down_bias, gain_two, shift_two = (
            vec_ref[2 + i : 3 + i, :] for i in range(MIDDLE_VECTORS)
        )
        attended = o_ref[rows, :]
        product = dot(attended, w[0])
        yield
        norm_one, scale_one = normalize(x_ref[rows, :].astype(F32) + (product + out_bias))
        first_norm = norm_one * gain_one + shift_one
        first_low = first_norm.astype(BF16)
        product = dot(first_low, w[1])
        yield
        pre_act = product + up_bias
        below = 0.5 * (1.0 + lax.erf(pre_act * (0.5**0.5)))
        activated = (pre_act * below).astype(BF16)
        product = dot(activated, w[2])
        slope = below + pre_act * (jnp.exp(-0.5 * pre_act * pre_act) * 0.3989422804014327)
        yield
        norm_two, scale_two = normalize(first_norm + (product + down_bias))
        result_ref[rows, :] = (norm_two * gain_two + shift_two).astype(BF16)
        dy = cot_ref[rows, :].astype(F32)
        d_second = norm_back(dy * gain_two, norm_two, scale_two)
        d_ff = d_second.astype(BF16)
        product = dot(d_ff, w[2], 1, 1)
        gvec[4:5, :] += column_sum(d_ff.astype(F32))
        gvec[5:6, :] += column_sum(dy * norm_two)
        gvec[6:7, :] += column_sum(dy)
        yield
        d_pre = (product * slope).astype(BF16)
        product = dot(d_pre, w[1], 1, 1)
        gd[...] += dot(activated, d_ff, 0, 0)
        gvec[3:4, :] += column_sum(d_pre.astype(F32))
        yield
        d_first = d_second + product
        d_hidden = norm_back(d_first * gain_one, norm_one, scale_one)
        d_attn = d_hidden.astype(BF16)
        dhid_ref[rows, :] = d_attn
        product = dot(d_attn, w[0], 1, 1)
        gu[...] += dot(first_low, d_pre, 0, 0)
        gvec[0:1, :] += column_sum(d_attn.astype(F32))
        gvec[1:2, :] += column_sum(d_first * norm_one)
        gvec[2:3, :] += column_sum(d_first)
        yield
        datt_ref[rows, :] = product.astype(BF16)
        go[...] += dot(attended, d_attn, 0, 0)
        yield

    step = x_ref.shape[0] // SPLITS
    live = [stages(slice(i * step, (i + 1) * step)) for i in range(SPLITS)]
    for turn in range(STAGES + SPLITS - 1):
        for i, part in enumerate(live):
            if 0 <= turn - i < STAGES:
                next(part)

    @pl.when(pl.program_id(0) == pl.num_programs(0) - 1)
    def _():
        for offset in range(len(held)):
            target = (keep_ref, send_ref)[offset % 2].at[offset // 2]
            rows = pl.ds(pl.multiple_of((me ^ offset) * block, block), block)
            for which, grad in enumerate((go, gu, gd)):
                cols = slice(which * width, (which + 1) * width)
                target[0:block, cols] = grad[rows, :].astype(BF16)
            target[block:, :] = jnp.zeros((EXTRA, 3 * width), BF16)
            target[block:, 0:block] = gvec[:, rows].astype(BF16)


def middle(scalars, held, pieces, x, o, cot, vec, cells):
    rows, width = x.shape
    step = ROWS if rows % ROWS == 0 else rows
    block = pl.BlockSpec((step, width), lambda i, s: (i, 0))
    full = lambda *shape: pl.BlockSpec(shape, lambda i, s: (0,) * len(shape))
    low = jax.ShapeDtypeStruct((rows, width), BF16)
    half = (len(held) // 2, width // len(held) + EXTRA, 3 * width)
    return pl.pallas_call(
        functools.partial(middle_kernel, held=held, cells=cells),
        out_shape=(low, low, low, jax.ShapeDtypeStruct(half, BF16), jax.ShapeDtypeStruct(half, BF16)),
        grid_spec=pltpu.PrefetchScalarGridSpec(
            num_scalar_prefetch=1,
            grid=(rows // step,),
            in_specs=[full(*piece.shape) for piece in pieces] + [block, block, block, full(EXTRA, width)],
            out_specs=[block, block, block, full(*half), full(*half)],
            scratch_shapes=[
                pltpu.VMEM((3, width, width), BF16),
                pltpu.VMEM((width, width), F32),
                pltpu.VMEM((width, width), F32),
                pltpu.VMEM((width, width), F32),
                pltpu.VMEM((EXTRA, width), F32),
            ],
        ),
        compiler_params=params(50),
        cost_estimate=cost(rows * 5e6, rows * 8e3),
        name="middle",
    )(scalars, *pieces, x, o, cot, vec)


def back_kernel(
    scalars_ref, pos_ref, xt_ref, qkv_ref, kvt_ref, e_ref, more_ref, stats_ref, datt_ref,
    dt_ref, keep_ref, send_ref,
    hot, oz, og, ds, joined, dqa, dkv, self_q, self_kv, delta, grad, term, spill,
    *, shards, cells, first_pair,
):
    pair, cell = pl.program_id(0), pl.program_id(1)
    known = scalars_ref[cell]
    me = scalars_ref[cells]
    width, length = xt_ref.shape[1] - ONES, xt_ref.shape[2]
    block = width // shards
    steps = (known + CHUNK - 1) // CHUNK
    place = pos_ref[0]
    hidden = place < 0

    @pl.when(pair == 0)
    def _():
        hot[cell, 0] = jnp.where(
            place == lax.broadcasted_iota(jnp.int32, (CHUNK, length), 0), 1.0, 0.0
        ).astype(BF16)

        def mark(chunk, carry):
            row = chunk * CHUNK + lax.broadcasted_iota(jnp.int32, (CHUNK, length), 0)
            hot[cell, chunk] = jnp.where(place == row, 1.0, 0.0).astype(BF16)
            return carry

        lax.fori_loop(1, steps, mark, 0)

    heads = [slice(side * HD, (side + 1) * HD) for side in range(2)]
    cuts = [slice(start, min(start + CUT, length)) for start in range(0, length, CUT)]
    queries = qkv_ref.at[0, 0, 0:LANES]

    @pl.when((pair == 0) & (cell == 0))
    def _():
        oz[...] = jnp.zeros_like(oz)

    og[...] = datt_ref[0].T

    def share(chunk, side):
        return jnp.exp(stats_ref[0, 0, 4 + 2 * chunk + side] - stats_ref[0, 0, side])

    def outset(side):
        rows = heads[side]
        grads = og[rows, :].astype(F32)
        query = queries[rows, :].astype(F32) * SCALE
        key = qkv_ref[0, 0, LANES + side * HD : LANES + (side + 1) * HD, :].astype(F32)
        value = qkv_ref[0, 0, 2 * LANES + side * HD : 2 * LANES + (side + 1) * HD, :].astype(F32)
        prob = jnp.exp(jnp.where(hidden, stats_ref[0, 0, 2 + side], MASK_FILL) - stats_ref[0, 0, side])
        own_grad = jnp.sum(grads * value, axis=0, keepdims=True)
        back = (prob * (own_grad - delta[side])).astype(BF16).astype(F32)
        self_q[rows, :] = back * key
        self_kv[rows, :] = back * query
        self_kv[LANES + side * HD : LANES + (side + 1) * HD, :] = prob.astype(BF16).astype(F32) * grads

    def score_grads(chunk, side, exps, values, cut, scaled):
        part = dot(values, oz[side, :, cut]) - scaled[:, cut]
        ds[side, :, cut] = (exps[side, :, cut].astype(F32) * part).astype(BF16)

    def spread(chunk, side, part):
        scaled = share(chunk, side)
        oz[side, heads[side], :] = (og[heads[side], :].astype(F32) * scaled).astype(BF16)
        return delta[side] * scaled

    def close(q_part, kv_part):
        dt_ref[0, 0, 0:LANES, :] = ((q_part + self_q[...]) * SCALE).astype(BF16)
        dt_ref[0, 0, LANES:, :] = (kv_part + self_kv[...]).astype(BF16)
        term[...] = dot(xt_ref[0], dt_ref[0, 0], 1, 1)

    exps = e_ref.at[0, 0]
    values = kvt_ref[0, 0, 0, LANES:, :].T
    for side in range(2):
        rows = heads[side]
        delta[side] = jnp.sum(
            og[rows, :].astype(F32)
            * qkv_ref[0, 0, TRIPLE + side * HD : TRIPLE + (side + 1) * HD, :].astype(F32),
            axis=0,
            keepdims=True,
        )
    scaled = [spread(0, side, None) for side in range(2)]
    for cut in cuts:
        score_grads(0, 0, exps, values, cut, scaled[0])
    d_values = dot(exps[0], oz[0], 1, 1)
    outset(0)
    for cut in cuts:
        score_grads(0, 1, exps, values, cut, scaled[1])
    d_keys = dot(ds[0], queries[...], 1, 1)
    outset(1)
    d_values += dot(exps[1], oz[1], 1, 1)
    lanes = lax.broadcasted_iota(jnp.int32, (CHUNK, LANES), 1) < HD
    joined[:, LANES:] = d_values.astype(BF16)
    dqa[0:HD, :] = dot(kvt_ref[0, 0, 0, 0:HD, :], ds[0])
    d_keys = jnp.where(lanes, d_keys, dot(ds[1], queries[...], 1, 1)) * SCALE
    dqa[HD:, :] = dot(kvt_ref[0, 0, 0, HD:LANES, :], ds[1])
    joined[:, 0:LANES] = d_keys.astype(BF16)
    dkv[...] = dot(joined[...], hot[cell, 0], 0, 0)
    close(dqa[...], dkv[...])

    def later_chunk(chunk, carry):
        pltpu.sync_copy(more_ref.at[cell, first_pair + pair, chunk - 1], spill)
        values = kvt_ref[0, 0, chunk, LANES:, :].T
        d_values = jnp.zeros((CHUNK, LANES), F32)
        for side in range(2):
            scaled = spread(chunk, side, None)
            for cut in cuts:
                score_grads(chunk, side, spill, values, cut, scaled)
            d_values += dot(spill[side], oz[side], 1, 1)
            dqa[heads[side], :] += dot(kvt_ref[0, 0, chunk, heads[side], :], ds[side])
        d_keys = jnp.where(lanes, dot(ds[0], queries[...], 1, 1), dot(ds[1], queries[...], 1, 1)) * SCALE
        joined[:, 0:LANES] = d_keys.astype(BF16)
        joined[:, LANES:] = d_values.astype(BF16)
        dkv[...] += dot(joined[...], hot[cell, chunk], 0, 0)
        return carry

    @pl.when(steps > 1)
    def _():
        lax.fori_loop(1, steps, later_chunk, 0)
        close(dqa[...], dkv[...])

    @pl.when(cell == 0)
    def _():
        grad[...] = term[...]

    @pl.when(cell > 0)
    def _():
        grad[...] += term[...]

    @pl.when(cell == cells - 1)
    def _():
        for offset in range(shards):
            owner = me ^ offset
            target = (keep_ref, send_ref)[offset % 2].at[offset // 2, 0]
            rows = pl.ds(pl.multiple_of(owner * block, block), block)
            target[0:block, :] = grad[rows, :].astype(BF16)
            ours = jnp.where(owner == first_pair + pair, 1.0, 0.0)
            target[block:, :] = (grad[width:, :] * ours).astype(BF16)


def attend_back(group, shards, scalars, pos, xt, qkv, kvt, e, more, stats, datt):
    first, count = group
    cells, length = xt.shape[0], xt.shape[2]
    width = xt.shape[1] - ONES
    chunks = kvt.shape[2]
    half = (shards // 2, count, width // shards + EXTRA, TRIPLE)
    part = pl.BlockSpec((shards // 2, 1) + half[2:], lambda p, c, s: (0, p, 0, 0))
    shape = jax.ShapeDtypeStruct
    return pl.pallas_call(
        functools.partial(back_kernel, shards=shards, cells=cells, first_pair=first),
        out_shape=(shape((cells, count, TRIPLE, length), BF16), shape(half, BF16), shape(half, BF16)),
        grid_spec=pltpu.PrefetchScalarGridSpec(
            num_scalar_prefetch=1,
            grid=(count, cells),
            in_specs=[
                pl.BlockSpec((1, 1, length), lambda p, c, s: (c, 0, 0)),
                pl.BlockSpec((1, width + ONES, length), lambda p, c, s: (c, 0, 0)),
                pl.BlockSpec((1, 1, 4 * LANES, length), lambda p, c, s: (c, first + p, 0, 0)),
                pl.BlockSpec((1, 1, chunks, 2 * LANES, CHUNK), lambda p, c, s: (c, first + p, 0, 0, 0)),
                pl.BlockSpec((1, 1, 2, CHUNK, length), lambda p, c, s: (c, first + p, 0, 0, 0)),
                pl.BlockSpec(memory_space=pl.ANY),
                pl.BlockSpec((1, 1, 4 + 2 * chunks, 1, length), lambda p, c, s: (c, first + p, 0, 0, 0)),
                pl.BlockSpec((1, length, LANES), lambda p, c, s: (c, 0, first + p)),
            ],
            out_specs=[
                pl.BlockSpec((1, 1, TRIPLE, length), lambda p, c, s: (c, p, 0, 0)),
                part,
                part,
            ],
            scratch_shapes=[
                pltpu.VMEM((cells, chunks, CHUNK, length), BF16),
                pltpu.VMEM((2, LANES, length), BF16),
                pltpu.VMEM((LANES, length), BF16),
                pltpu.VMEM((2, CHUNK, length), BF16),
                pltpu.VMEM((CHUNK, 2 * LANES), BF16),
                pltpu.VMEM((LANES, length), F32),
                pltpu.VMEM((2 * LANES, length), F32),
                pltpu.VMEM((LANES, length), F32),
                pltpu.VMEM((2 * LANES, length), F32),
                pltpu.VMEM((2, 1, length), F32),
                pltpu.VMEM((width + ONES, TRIPLE), F32),
                pltpu.VMEM((width + ONES, TRIPLE), F32),
                pltpu.VMEM((2, CHUNK, length), BF16),
            ],
        ),
        compiler_params=params(51),
        cost_estimate=cost(cells * count * 6e9, cells * count * 7e6),
        name="attend_back",
    )(scalars, pos, xt, qkv, kvt, e, more, stats, datt)


def input_kernel(w_ref, dhid_ref, *refs):
    parts, out_ref = refs[:-1], refs[-1]
    back, col = None, 0
    for part in parts:
        rows = part.shape[1]
        term = dot(w_ref[:, col : col + rows], part[0])
        back = term if back is None else back + term
        col += rows
    out_ref[0] = (back.T + dhid_ref[0].astype(F32)).astype(BF16)


def input_grad(w, dhid, parts):
    cells, length, width = dhid.shape
    parts = [part.reshape(cells, -1, length) for part in parts]
    block = pl.BlockSpec((1, length, width), lambda i: (i, 0, 0))
    return pl.pallas_call(
        input_kernel,
        out_shape=jax.ShapeDtypeStruct(dhid.shape, BF16),
        grid=(cells,),
        in_specs=[pl.BlockSpec(w.shape, lambda i: (0, 0)), block]
        + [pl.BlockSpec((1,) + part.shape[1:], lambda i: (i, 0, 0)) for part in parts],
        out_specs=block,
        compiler_params=params(28),
        cost_estimate=cost(cells * 2e9, cells * 8e6),
        name="input_grad",
    )(w, dhid, *parts)


def finish_kernel(*refs):
    terms, halves, outs = refs[:2], refs[2:-15], refs[-15:]
    block, width = outs[0].shape
    for which in range(3):
        cols = slice(which * width, (which + 1) * width)
        outs[3 + which][...] = terms[0][0:block, cols].astype(F32) + terms[1][0:block, cols].astype(F32)
    rows = terms[0][block:, 0:block].astype(F32) + terms[1][block:, 0:block].astype(F32)
    for row in range(MIDDLE_VECTORS):
        outs[8 + row][...] = rows[row : row + 1, :].reshape(block)

    def write(order):
        biases = [jnp.zeros((1, LANES), F32), jnp.zeros((1, LANES), F32)]
        pair = 0
        for group in range(0, len(halves), 2):
            for part in [halves[group + i] for i in order]:
                for p in range(part.shape[0]):
                    for which in range(3):
                        cols = slice(which * LANES, (which + 1) * LANES)
                        outs[which][:, pair * LANES : (pair + 1) * LANES] = part[p, 0:block, cols].astype(F32)
                    biases[0] += part[p, block : block + 1, 0:LANES].astype(F32)
                    biases[1] += part[p, block : block + 1, 2 * LANES :].astype(F32)
                    pair += 1
        outs[6][...] = biases[0].reshape(block)
        outs[7][...] = biases[1].reshape(block)

    low = lax.axis_index("dp") % 2 == 0

    @pl.when(low)
    def _():
        write((0, 1))

    @pl.when(jnp.logical_not(low))
    def _():
        write((1, 0))


def finish(parts, block, width):
    vmem = pl.BlockSpec(memory_space=pltpu.VMEM)
    return pl.pallas_call(
        finish_kernel,
        out_shape=(jax.ShapeDtypeStruct((block, width), F32),) * 6 + (jax.ShapeDtypeStruct((block,), F32),) * 9,
        in_specs=[vmem] * len(parts),
        out_specs=[vmem] * 15,
        compiler_params=params(16),
        name="finish",
    )(*parts)


def swap(values, axis, mask):
    size = lax.axis_size(axis)
    return lax.ppermute(values, axis, [(i, i ^ mask) for i in range(size)])


def masks(axis):
    found, mask = [], 1
    while mask < lax.axis_size(axis):
        found.append(mask)
        mask *= 2
    return found


def after(value, *others):
    return lax.optimization_barrier((value,) + others)[0]


def gather_pieces(own, beside):
    held = [own]
    for mask in reversed(masks("fsdp")):
        held = held + [swap(piece, "fsdp", mask) for piece in held]
        held = held[:1] + [after(piece, beside) for piece in held[1:]]
    return held


def plus(left, right):
    return left.astype(F32) + right.astype(F32)


class Reduction:
    def __init__(self, keep, send, half_dim=None):
        self.keep, self.send = keep, send
        self.half_dim = half_dim
        order = masks("dp") if half_dim is not None else reversed(masks("dp"))
        self.plan = [("fsdp", mask) for mask in masks("fsdp")] + [("dp", mask) for mask in order]
        self.low = (lax.axis_index("dp") % 2) == 0

    def pair(self):
        return self.keep, self.send

    def start(self, pair=None):
        if self.plan:
            self.keep, self.send = pair or self.pair()
            self.arrived = swap(self.send, *self.plan[0])

    def arrive(self):
        self.plan = self.plan[1:]
        if not self.plan:
            return
        total = plus(self.keep, self.arrived).astype(BF16)
        axis, mask = self.plan[0]
        if axis == "fsdp":
            self.keep, self.send = total[0::2], total[1::2]
        elif mask == 1 and self.half_dim is not None:
            first, second = jnp.split(total, 2, self.half_dim)
            self.keep = jnp.where(self.low, first, second)
            self.send = jnp.where(self.low, second, first)
        else:
            self.keep = self.send = total

    def finish(self):
        while self.plan:
            self.start()
            self.arrive()
        if self.half_dim is None:
            return self.keep[0], self.arrived[0]
        mine = plus(self.keep, self.arrived).astype(BF16)[0]
        if lax.axis_size("dp") == 1:
            return jnp.split(mine, 2, self.half_dim - 1)
        return mine, swap(mine, "dp", 1)


def body(*args):
    tokens, known_flags, cotangent = args[0], args[1], args[17]
    cells, length, width = tokens.shape
    shards = lax.axis_size("fsdp")
    block = width // shards
    held = offsets(shards)

    early, late, scalars = pack(known_flags, [args[i] for i in SQUARES], [args[i] for i in VECTORS])
    xc, xt, pos = gather_known(scalars, known_flags, tokens)
    early = gather_pieces(early, xt)
    late = after(late, *early[:2])
    late = [late] + [swap(late, "fsdp", offset) for offset in held[1:]]
    w, vec, qkv, kvt, e, more, stats, o = attend(scalars, held, early, xt, xc, pos)
    flat = lambda a: a.reshape(cells * length, width)
    result, dhid, datt, keep, send = middle(
        scalars, held, late, flat(tokens), flat(o), flat(cotangent), vec, cells
    )
    cube = lambda a: a.reshape(cells, length, width)
    chains = [Reduction(keep, send)]

    def boundary(value):
        older, newest = chains[:-1], chains[-1]
        arrived = lax.optimization_barrier([chain.arrived for chain in older])
        for chain, chain.arrived in zip(older, arrived):
            chain.arrive()
        pairs = lax.optimization_barrier([chain.pair() for chain in chains])
        for chain, (chain.keep, chain.send) in zip(chains, pairs):
            pass
        newest.start()
        for chain in older:
            chain.start()
        newest.arrive()
        value, pair = lax.optimization_barrier((value, newest.pair()))
        newest.start(pair)
        return value

    parts = []
    for group in GROUPS:
        dt, keep, send = attend_back(
            group, shards, boundary(scalars), pos, xt, qkv, kvt, e, more, stats, cube(datt)
        )
        parts.append(dt)
        chains.append(Reduction(keep, send, 1))
    tokens_grad = input_grad(boundary(w), cube(dhid), parts)
    tokens_grad, arrived = lax.optimization_barrier((tokens_grad, [chain.arrived for chain in chains]))
    for chain, chain.arrived in zip(chains, arrived):
        chain.arrive()
    newest = chains[-1]
    newest.start()
    newest.arrive()
    chains[0].send = after(chains[0].send, newest.send)
    halves = [half for chain in chains for half in chain.finish()]
    summed = finish(halves, block, width)
    out = dict(zip(SQUARES + VECTORS, summed))
    return (cube(result), tokens_grad) + tuple(out[i] for i in range(2, 17))


def solution(mesh):
    cells = P(("dp", "fsdp"), None, None)
    specs = tuple(P("fsdp", None) if i in SQUARES else P("fsdp") for i in range(2, 17))
    return jax.shard_map(
        body,
        mesh=mesh,
        in_specs=(cells, P(("dp", "fsdp"), None)) + specs + (cells,),
        out_specs=(cells, cells) + specs,
        check_vma=False,
    )
```

```python
import functools

import jax
import jax.numpy as jnp
from jax import lax
from jax.experimental import pallas as pl
from jax.experimental.pallas import tpu as pltpu
from jax.sharding import PartitionSpec as P

H = 8
HD = 64
SCALE = HD ** (-0.5)
NORM_EPSILON = 1e-05
MASK_FILL = -1e30
SAFE_SCORE = 50.0

CHUNK = 672
ROWS = 480
SPLITS = 1
STAGES = 7
ONES = 16
EXTRA = 16
LANES = 128
CUT = 256
LOG2E = 1.4426950408889634
TRIPLE = 3 * LANES
GROUPS = ((0, 2), (2, 2))

F32 = jnp.float32
BF16 = jnp.bfloat16

SQUARES = (2, 4, 5, 7, 11, 13)
VECTORS = (3, 6, 8, 9, 10, 12, 14, 15, 16)
MIDDLE_VECTORS = 7


def dot(left, right, left_dim=1, right_dim=0):
    return lax.dot_general(
        left, right, (((left_dim,), (right_dim,)), ((), ())), preferred_element_type=F32
    )


def params(mebibytes):
    return pltpu.CompilerParams(vmem_limit_bytes=mebibytes << 20)


def cost(flops, moved):
    return pl.CostEstimate(flops=int(flops), bytes_accessed=int(moved), transcendentals=0)


def offsets(shards):
    held, mask = [0], shards // 2
    while mask:
        held = held + [offset ^ mask for offset in held]
        mask //= 2
    return held


def pack_kernel(*refs):
    flags_ref, squares, vectors = refs[0], refs[1:7], refs[7:16]
    early_ref, late_ref, scalars_ref = refs[16:]
    block = squares[0].shape[0]
    for i in range(3):
        early_ref[i * block : (i + 1) * block, :] = squares[i][...]
        late_ref[i * block : (i + 1) * block, :] = squares[3 + i][...]
    rows = [vector[...].astype(F32).reshape(1, -1) for vector in vectors]
    rows = jnp.concatenate(rows + [jnp.zeros((EXTRA - len(rows), block), F32)], axis=0)
    early_ref[3 * block :, :] = jnp.zeros((EXTRA, early_ref.shape[1]), BF16)
    early_ref[3 * block :, 0:block] = rows.astype(BF16)
    flagged = jnp.where(flags_ref[...] > 0, 1.0, 0.0)
    cells = flags_ref.shape[0]
    for cell in range(cells):
        scalars_ref[cell] = jnp.sum(flagged[cell : cell + 1, :]).astype(jnp.int32)
    scalars_ref[cells] = lax.axis_index("fsdp")


def pack(flags, squares, vectors):
    block, width = squares[0].shape
    cells = flags.shape[0]
    vmem = pl.BlockSpec(memory_space=pltpu.VMEM)
    return pl.pallas_call(
        pack_kernel,
        out_shape=(
            jax.ShapeDtypeStruct((3 * block + EXTRA, width), BF16),
            jax.ShapeDtypeStruct((3 * block, width), BF16),
            jax.ShapeDtypeStruct((cells + 1,), jnp.int32),
        ),
        in_specs=[vmem] * 16,
        out_specs=[vmem, vmem, pl.BlockSpec(memory_space=pltpu.SMEM)],
        compiler_params=params(60),
        name="pack",
    )(flags, *squares, *vectors)


def gather_kernel(scalars_ref, flags_ref, x_ref, xc_ref, xt_ref, pos_ref):
    known = scalars_ref[pl.program_id(0)]
    length, width = x_ref.shape[1], x_ref.shape[2]
    flagged = flags_ref[pl.ds(pl.program_id(0), 1), :] > 0
    before = lax.broadcasted_iota(jnp.int32, (length, length), 0)
    after = lax.broadcasted_iota(jnp.int32, (length, length), 1)
    upper = jnp.where(before <= after, 1.0, 0.0).astype(BF16)
    marks = jnp.broadcast_to(jnp.where(flagged, 1.0, 0.0), (16, length)).astype(BF16)
    place = dot(marks, upper)[0:1, :].astype(jnp.int32) - 1
    place = jnp.where(flagged, place, -1)
    pos_ref[0] = place

    for chunk in range(xc_ref.shape[1] // CHUNK):

        @pl.when((chunk == 0) | (chunk * CHUNK < known))
        def _():
            target = chunk * CHUNK + lax.broadcasted_iota(jnp.int32, (CHUNK, length), 0)
            target = jnp.where(known > 0, jnp.minimum(target, known - 1), -2)
            chosen = jnp.where(place == target, 1.0, 0.0).astype(BF16)
            xc_ref[0, chunk * CHUNK : (chunk + 1) * CHUNK, :] = dot(chosen, x_ref[0]).astype(BF16)

    xt_ref[0, 0:width, :] = x_ref[0].T
    xt_ref[0, width:, :] = jnp.ones((ONES, length), BF16)


def gather_known(scalars, flags, x):
    cells, length, width = x.shape
    padded = -(-length // CHUNK) * CHUNK
    one = lambda *shape: pl.BlockSpec((1,) + shape, lambda i, s: (i, 0, 0))
    return pl.pallas_call(
        gather_kernel,
        out_shape=(
            jax.ShapeDtypeStruct((cells, padded, width), BF16),
            jax.ShapeDtypeStruct((cells, width + ONES, length), BF16),
            jax.ShapeDtypeStruct((cells, 1, length), jnp.int32),
        ),
        grid_spec=pltpu.PrefetchScalarGridSpec(
            num_scalar_prefetch=1,
            grid=(cells,),
            in_specs=[pl.BlockSpec(flags.shape, lambda i, s: (0, 0)), one(length, width)],
            out_specs=[one(padded, width), one(width + ONES, length), one(1, length)],
        ),
        compiler_params=params(50),
        cost_estimate=cost(cells * 2e9, cells * 6e6),
        name="gather_known",
    )(scalars, flags, x)


def as_column(row):
    return jnp.broadcast_to(row, (LANES, LANES)).T[:, 0:1]


def attend_kernel(*refs, held, cells):
    scalars_ref, refs = refs[0], refs[1:]
    pieces, refs = refs[: len(held)], refs[len(held) :]
    (
        xt_ref, xc_ref, pos_ref,
        w_ref, vec_ref, qkv_ref, kvt_ref, e_ref, more_ref, stats_ref, o_ref,
        bias, qz, kc, vct, top, own, acc, spill,
    ) = refs
    cell, pair = pl.program_id(0), pl.program_id(1)
    known = scalars_ref[cell]
    me = scalars_ref[cells]
    width, length = w_ref.shape[0], xt_ref.shape[2]
    pairs = width // LANES
    block = width // len(held)

    @pl.when((cell == 0) & (pair == 0))
    def _():
        for offset, piece in zip(held, pieces):
            owner = me ^ offset
            rows = pl.ds(pl.multiple_of(owner * block, block), block)
            for which in range(3):
                for p in range(pairs):
                    col = p * TRIPLE + which * LANES
                    w_ref[rows, col : col + LANES] = piece[
                        which * block : (which + 1) * block, p * LANES : (p + 1) * LANES
                    ]
            vec_ref[:, rows] = piece[3 * block :, 0:block].astype(F32)
        qz[...] = jnp.zeros_like(qz)
        for p in range(pairs):
            cols = slice(p * LANES, (p + 1) * LANES)
            bias[p, :, 0:1] = as_column(vec_ref[0:1, cols])
            bias[p, :, 1:2] = as_column(vec_ref[1:2, cols])

    col = pl.multiple_of(pair * TRIPLE, LANES)
    part = lambda first, count: w_ref[:, pl.ds(col + first * LANES, count * LANES)]
    hidden = pos_ref[0] < 0
    steps = (known + CHUNK - 1) // CHUNK
    value_bias = vec_ref[1:2, pl.ds(pl.multiple_of(pair * LANES, LANES), LANES)]
    tokens = xt_ref[0, 0:width, :]
    heads = [slice(side * HD, (side + 1) * HD) for side in range(2)]
    cuts = [slice(start, min(start + CUT, length)) for start in range(0, length, CUT)]

    def project(chunk):
        rows = pl.ds(pl.multiple_of(chunk * CHUNK, 16), CHUNK)
        packed = dot(xc_ref[0, rows, :], part(1, 2))
        yield
        row = chunk * CHUNK + lax.broadcasted_iota(jnp.int32, (CHUNK, LANES), 0)
        keys = packed[:, 0:LANES]
        kc[...] = keys.astype(BF16)
        kvt_ref[0, 0, chunk, 0:LANES, :] = jnp.where(row < known, keys, 0.0).astype(BF16).T
        yield
        values = packed[:, LANES:] + value_bias
        values = jnp.where(row < known, values, 0.0).astype(BF16).T
        kvt_ref[0, 0, chunk, LANES:, :] = values
        counted = chunk * CHUNK + lax.broadcasted_iota(jnp.int32, (EXTRA, CHUNK), 1)
        counted = jnp.where(counted < known, 1.0, 0.0).astype(BF16)
        for side in range(2):
            vct[side, 0:HD, :] = values[heads[side], :]
            vct[side, HD:, :] = counted
        yield

    def begin(side, shifted):
        weight = jnp.ones((1, length), F32) if shifted else jnp.exp(own[side])
        weight = jnp.where(hidden, weight, 0.0).astype(BF16).astype(F32)
        top[side] = jnp.where(hidden, own[side], MASK_FILL) if shifted else jnp.zeros((1, length), F32)
        return weight

    def own_values(side):
        return qkv_ref[0, 0, 2 * LANES + side * HD : 2 * LANES + (side + 1) * HD, :].astype(F32)

    def measure(side):
        q = qkv_ref[0, 0, heads[side], :].astype(F32)
        k = qkv_ref[0, 0, LANES + side * HD : LANES + (side + 1) * HD, :].astype(F32)
        own[side] = jnp.sum(q * k, axis=0, keepdims=True) * SCALE
        longest_q = jnp.max(jnp.sum(q * q, axis=0, keepdims=True))
        longest_k = jnp.max(jnp.sum(k * k, axis=0, keepdims=True))
        return longest_q * longest_k < (SAFE_SCORE / SCALE) * (SAFE_SCORE / SCALE)

    def conclude(side):
        total = acc[side, HD : HD + 1, :]
        rows = slice(TRIPLE + side * HD, TRIPLE + (side + 1) * HD)
        qkv_ref[0, 0, rows, :] = (acc[side, 0:HD, :] * (1.0 / total)).astype(BF16)
        stats_ref[0, 0, side] = top[side] + jnp.log(total)
        stats_ref[0, 0, 2 + side] = own[side]

    first = project(0)
    next(first)
    turned = dot(part(0, 1), tokens, 0, 0)
    next(first)
    queries = (turned + bias[pair, :, 0:1]).astype(BF16)
    turned = dot(part(1, 2), tokens, 0, 0)
    qkv_ref[0, 0, 0:LANES, :] = queries
    for side in range(2):
        qz[side, heads[side], :] = queries[heads[side], :]
    next(first)
    qkv_ref[0, 0, LANES : 2 * LANES, :] = turned[0:LANES, :].astype(BF16)
    weights = []
    safe = None
    for side in range(2):
        for cut in cuts:
            scores = dot(kc[...], qz[side, :, cut])
            e_ref[0, 0, side, :, cut] = jnp.exp2(scores * (SCALE * LOG2E)).astype(BF16)
            if side == 0 and cut is cuts[0]:
                qkv_ref[0, 0, 2 * LANES : TRIPLE, :] = (turned[LANES:, :] + bias[pair, :, 1:2]).astype(BF16)
            if cut is cuts[1]:
                bounded = measure(side)
                safe = bounded if safe is None else safe & bounded
                weights.append(begin(side, False))
        total = dot(vct[side], e_ref[0, 0, side])
        acc[side, 0:HD, :] = total[0:HD, :] + weights[side] * own_values(side)
        acc[side, HD:, :] = total[HD:, :] + weights[side]
    for side in range(2):
        conclude(side)
        stats_ref[0, 0, 4 + side] = top[side]
    o_ref[0] = qkv_ref[0, 0, TRIPLE:, :].T

    def weigh(chunk, side, exps, shifted):
        scores = dot(kc[...], qz[side]) * SCALE
        if shifted:
            peak = jnp.maximum(top[side], jnp.max(scores, axis=0, keepdims=True))
            peak = jnp.where(known > 0, peak, top[side])
            scores = jnp.minimum(scores - peak, 0.0)
        probs = jnp.exp(scores).astype(BF16)
        exps[side] = probs
        if shifted:
            acc[side] = acc[side] * jnp.exp(top[side] - peak) + dot(vct[side], probs)
            top[side] = peak
        else:
            acc[side] += dot(vct[side], probs)
        stats_ref[0, 0, 4 + 2 * chunk + side] = top[side]

    @pl.when(jnp.logical_not(safe))
    def _():
        for side in range(2):
            weight = begin(side, True)
            acc[side, 0:HD, :] = weight * own_values(side)
            acc[side, HD:, :] = jnp.broadcast_to(weight, (EXTRA, length))
            weigh(0, side, e_ref.at[0, 0], True)

    def later_chunk(chunk, carry):
        for _ in project(chunk):
            pass

        @pl.when(safe)
        def _():
            for side in range(2):
                weigh(chunk, side, spill, False)

        @pl.when(jnp.logical_not(safe))
        def _():
            for side in range(2):
                weigh(chunk, side, spill, True)

        pltpu.sync_copy(spill, more_ref.at[cell, pair, chunk - 1])
        return carry

    lax.fori_loop(1, steps, later_chunk, 0)

    @pl.when(jnp.logical_not(safe) | (steps > 1))
    def _():
        for side in range(2):
            conclude(side)
        o_ref[0] = qkv_ref[0, 0, TRIPLE:, :].T


def attend(scalars, held, pieces, xt, xc, pos):
    cells, length = xt.shape[0], xt.shape[2]
    width = xt.shape[1] - ONES
    padded = xc.shape[1]
    pairs = width // LANES
    chunks = padded // CHUNK
    full = lambda *shape: pl.BlockSpec(shape, lambda c, p, s: (0,) * len(shape))
    shape = jax.ShapeDtypeStruct
    return pl.pallas_call(
        functools.partial(attend_kernel, held=held, cells=cells),
        out_shape=(
            shape((width, 3 * width), BF16),
            shape((EXTRA, width), F32),
            shape((cells, pairs, 4 * LANES, length), BF16),
            shape((cells, pairs, chunks, 2 * LANES, CHUNK), BF16),
            shape((cells, pairs, 2, CHUNK, length), BF16),
            shape((cells, pairs, max(chunks - 1, 1), 2, CHUNK, length), BF16),
            shape((cells, pairs, 4 + 2 * chunks, 1, length), F32),
            shape((cells, length, width), BF16),
        ),
        grid_spec=pltpu.PrefetchScalarGridSpec(
            num_scalar_prefetch=1,
            grid=(cells, pairs),
            in_specs=[full(*piece.shape) for piece in pieces]
            + [
                pl.BlockSpec((1, width + ONES, length), lambda c, p, s: (c, 0, 0)),
                pl.BlockSpec((1, padded, width), lambda c, p, s: (c, 0, 0)),
                pl.BlockSpec((1, 1, length), lambda c, p, s: (c, 0, 0)),
            ],
            out_specs=[
                full(width, 3 * width),
                full(EXTRA, width),
                pl.BlockSpec((1, 1, 4 * LANES, length), lambda c, p, s: (c, p, 0, 0)),
                pl.BlockSpec((1, 1, chunks, 2 * LANES, CHUNK), lambda c, p, s: (c, p, 0, 0, 0)),
                pl.BlockSpec((1, 1, 2, CHUNK, length), lambda c, p, s: (c, p, 0, 0, 0)),
                pl.BlockSpec(memory_space=pl.ANY),
                pl.BlockSpec((1, 1, 4 + 2 * chunks, 1, length), lambda c, p, s: (c, p, 0, 0, 0)),
                pl.BlockSpec((1, length, LANES), lambda c, p, s: (c, 0, p)),
            ],
            scratch_shapes=[
                pltpu.VMEM((pairs, LANES, 8), F32),
                pltpu.VMEM((2, LANES, length), BF16),
                pltpu.VMEM((CHUNK, LANES), BF16),
                pltpu.VMEM((2, HD + EXTRA, CHUNK), BF16),
                pltpu.VMEM((2, 1, length), F32),
                pltpu.VMEM((2, 1, length), F32),
                pltpu.VMEM((2, HD + EXTRA, length), F32),
                pltpu.VMEM((2, CHUNK, length), BF16),
            ],
        ),
        compiler_params=params(52),
        cost_estimate=cost(cells * 1e10, cells * 2.5e7),
        name="attend",
    )(scalars, *pieces, xt, xc, pos)


def row_mean(rows):
    return jnp.mean(rows, axis=-1, keepdims=True)


def normalize(rows):
    centred = rows - row_mean(rows)
    scale = lax.rsqrt(row_mean(centred * centred) + NORM_EPSILON)
    return centred * scale, scale


def norm_back(grad, normed, scale):
    return scale * (grad - row_mean(grad) - normed * row_mean(grad * normed))


def column_sum(rows):
    return jnp.sum(rows, axis=0, keepdims=True)


def middle_kernel(*refs, held, cells):
    scalars_ref, refs = refs[0], refs[1:]
    pieces, refs = refs[: len(held)], refs[len(held) :]
    (
        x_ref, o_ref, cot_ref, vec_ref,
        result_ref, dhid_ref, datt_ref, keep_ref, send_ref,
        w, go, gu, gd, gvec,
    ) = refs
    me = scalars_ref[cells]
    width = x_ref.shape[1]
    block = width // len(held)

    @pl.when(pl.program_id(0) == 0)
    def _():
        for offset, piece in zip(held, pieces):
            rows = pl.ds(pl.multiple_of((me ^ offset) * block, block), block)
            for which in range(3):
                w[which, rows, :] = piece[which * block : (which + 1) * block, :]
        go[...] = jnp.zeros_like(go)
        gu[...] = jnp.zeros_like(gu)
        gd[...] = jnp.zeros_like(gd)
        gvec[...] = jnp.zeros_like(gvec)

    def stages(rows):
        out_bias, gain_one, shift_one, up_bias, down_bias, gain_two, shift_two = (
            vec_ref[2 + i : 3 + i, :] for i in range(MIDDLE_VECTORS)
        )
        attended = o_ref[rows, :]
        product = dot(attended, w[0])
        yield
        norm_one, scale_one = normalize(x_ref[rows, :].astype(F32) + (product + out_bias))
        first_norm = norm_one * gain_one + shift_one
        first_low = first_norm.astype(BF16)
        product = dot(first_low, w[1])
        yield
        pre_act = product + up_bias
        below = 0.5 * (1.0 + lax.erf(pre_act * (0.5**0.5)))
        activated = (pre_act * below).astype(BF16)
        product = dot(activated, w[2])
        slope = below + pre_act * (jnp.exp(-0.5 * pre_act * pre_act) * 0.3989422804014327)
        yield
        norm_two, scale_two = normalize(first_norm + (product + down_bias))
        result_ref[rows, :] = (norm_two * gain_two + shift_two).astype(BF16)
        dy = cot_ref[rows, :].astype(F32)
        d_second = norm_back(dy * gain_two, norm_two, scale_two)
        d_ff = d_second.astype(BF16)
        product = dot(d_ff, w[2], 1, 1)
        gvec[4:5, :] += column_sum(d_ff.astype(F32))
        gvec[5:6, :] += column_sum(dy * norm_two)
        gvec[6:7, :] += column_sum(dy)
        yield
        d_pre = (product * slope).astype(BF16)
        product = dot(d_pre, w[1], 1, 1)
        gd[...] += dot(activated, d_ff, 0, 0)
        gvec[3:4, :] += column_sum(d_pre.astype(F32))
        yield
        d_first = d_second + product
        d_hidden = norm_back(d_first * gain_one, norm_one, scale_one)
        d_attn = d_hidden.astype(BF16)
        dhid_ref[rows, :] = d_attn
        product = dot(d_attn, w[0], 1, 1)
        gu[...] += dot(first_low, d_pre, 0, 0)
        gvec[0:1, :] += column_sum(d_attn.astype(F32))
        gvec[1:2, :] += column_sum(d_first * norm_one)
        gvec[2:3, :] += column_sum(d_first)
        yield
        datt_ref[rows, :] = product.astype(BF16)
        go[...] += dot(attended, d_attn, 0, 0)
        yield

    step = x_ref.shape[0] // SPLITS
    live = [stages(slice(i * step, (i + 1) * step)) for i in range(SPLITS)]
    for turn in range(STAGES + SPLITS - 1):
        for i, part in enumerate(live):
            if 0 <= turn - i < STAGES:
                next(part)

    @pl.when(pl.program_id(0) == pl.num_programs(0) - 1)
    def _():
        for offset in range(len(held)):
            target = (keep_ref, send_ref)[offset % 2].at[offset // 2]
            rows = pl.ds(pl.multiple_of((me ^ offset) * block, block), block)
            for which, grad in enumerate((go, gu, gd)):
                cols = slice(which * width, (which + 1) * width)
                target[0:block, cols] = grad[rows, :].astype(BF16)
            target[block:, :] = jnp.zeros((EXTRA, 3 * width), BF16)
            target[block:, 0:block] = gvec[:, rows].astype(BF16)


def middle(scalars, held, pieces, x, o, cot, vec, cells):
    rows, width = x.shape
    step = ROWS if rows % ROWS == 0 else rows
    block = pl.BlockSpec((step, width), lambda i, s: (i, 0))
    full = lambda *shape: pl.BlockSpec(shape, lambda i, s: (0,) * len(shape))
    low = jax.ShapeDtypeStruct((rows, width), BF16)
    half = (len(held) // 2, width // len(held) + EXTRA, 3 * width)
    return pl.pallas_call(
        functools.partial(middle_kernel, held=held, cells=cells),
        out_shape=(low, low, low, jax.ShapeDtypeStruct(half, BF16), jax.ShapeDtypeStruct(half, BF16)),
        grid_spec=pltpu.PrefetchScalarGridSpec(
            num_scalar_prefetch=1,
            grid=(rows // step,),
            in_specs=[full(*piece.shape) for piece in pieces] + [block, block, block, full(EXTRA, width)],
            out_specs=[block, block, block, full(*half), full(*half)],
            scratch_shapes=[
                pltpu.VMEM((3, width, width), BF16),
                pltpu.VMEM((width, width), F32),
                pltpu.VMEM((width, width), F32),
                pltpu.VMEM((width, width), F32),
                pltpu.VMEM((EXTRA, width), F32),
            ],
        ),
        compiler_params=params(50),
        cost_estimate=cost(rows * 5e6, rows * 8e3),
        name="middle",
    )(scalars, *pieces, x, o, cot, vec)


def back_kernel(
    scalars_ref, pos_ref, xt_ref, qkv_ref, kvt_ref, e_ref, more_ref, stats_ref, datt_ref,
    dt_ref, keep_ref, send_ref,
    hot, oz, og, ds, joined, dqa, dkv, self_q, self_kv, delta, grad, term, spill,
    *, shards, cells, first_pair,
):
    pair, cell = pl.program_id(0), pl.program_id(1)
    known = scalars_ref[cell]
    me = scalars_ref[cells]
    width, length = xt_ref.shape[1] - ONES, xt_ref.shape[2]
    block = width // shards
    steps = (known + CHUNK - 1) // CHUNK
    place = pos_ref[0]
    hidden = place < 0

    @pl.when(pair == 0)
    def _():
        hot[cell, 0] = jnp.where(
            place == lax.broadcasted_iota(jnp.int32, (CHUNK, length), 0), 1.0, 0.0
        ).astype(BF16)

        def mark(chunk, carry):
            row = chunk * CHUNK + lax.broadcasted_iota(jnp.int32, (CHUNK, length), 0)
            hot[cell, chunk] = jnp.where(place == row, 1.0, 0.0).astype(BF16)
            return carry

        lax.fori_loop(1, steps, mark, 0)

    heads = [slice(side * HD, (side + 1) * HD) for side in range(2)]
    cuts = [slice(start, min(start + CUT, length)) for start in range(0, length, CUT)]
    queries = qkv_ref.at[0, 0, 0:LANES]

    @pl.when((pair == 0) & (cell == 0))
    def _():
        oz[...] = jnp.zeros_like(oz)

    og[...] = datt_ref[0].T

    def share(chunk, side):
        return jnp.exp(stats_ref[0, 0, 4 + 2 * chunk + side] - stats_ref[0, 0, side])

    def outset(side):
        rows = heads[side]
        grads = og[rows, :].astype(F32)
        query = queries[rows, :].astype(F32) * SCALE
        key = qkv_ref[0, 0, LANES + side * HD : LANES + (side + 1) * HD, :].astype(F32)
        value = qkv_ref[0, 0, 2 * LANES + side * HD : 2 * LANES + (side + 1) * HD, :].astype(F32)
        prob = jnp.exp(jnp.where(hidden, stats_ref[0, 0, 2 + side], MASK_FILL) - stats_ref[0, 0, side])
        own_grad = jnp.sum(grads * value, axis=0, keepdims=True)
        back = (prob * (own_grad - delta[side])).astype(BF16).astype(F32)
        self_q[rows, :] = back * key
        self_kv[rows, :] = back * query
        self_kv[LANES + side * HD : LANES + (side + 1) * HD, :] = prob.astype(BF16).astype(F32) * grads

    def score_grads(chunk, side, exps, values, cut, scaled):
        part = dot(values, oz[side, :, cut]) - scaled[:, cut]
        ds[side, :, cut] = (exps[side, :, cut].astype(F32) * part).astype(BF16)

    def spread(chunk, side, part):
        scaled = share(chunk, side)
        oz[side, heads[side], :] = (og[heads[side], :].astype(F32) * scaled).astype(BF16)
        return delta[side] * scaled

    def close(q_part, kv_part):
        dt_ref[0, 0, 0:LANES, :] = ((q_part + self_q[...]) * SCALE).astype(BF16)
        dt_ref[0, 0, LANES:, :] = (kv_part + self_kv[...]).astype(BF16)
        term[...] = dot(xt_ref[0], dt_ref[0, 0], 1, 1)

    exps = e_ref.at[0, 0]
    values = kvt_ref[0, 0, 0, LANES:, :].T
    for side in range(2):
        rows = heads[side]
        delta[side] = jnp.sum(
            og[rows, :].astype(F32)
            * qkv_ref[0, 0, TRIPLE + side * HD : TRIPLE + (side + 1) * HD, :].astype(F32),
            axis=0,
            keepdims=True,
        )
    scaled = [spread(0, side, None) for side in range(2)]
    for cut in cuts:
        score_grads(0, 0, exps, values, cut, scaled[0])
    d_values = dot(exps[0], oz[0], 1, 1)
    outset(0)
    for cut in cuts:
        score_grads(0, 1, exps, values, cut, scaled[1])
    d_keys = dot(ds[0], queries[...], 1, 1)
    outset(1)
    d_values += dot(exps[1], oz[1], 1, 1)
    lanes = lax.broadcasted_iota(jnp.int32, (CHUNK, LANES), 1) < HD
    joined[:, LANES:] = d_values.astype(BF16)
    dqa[0:HD, :] = dot(kvt_ref[0, 0, 0, 0:HD, :], ds[0])
    d_keys = jnp.where(lanes, d_keys, dot(ds[1], queries[...], 1, 1)) * SCALE
    dqa[HD:, :] = dot(kvt_ref[0, 0, 0, HD:LANES, :], ds[1])
    joined[:, 0:LANES] = d_keys.astype(BF16)
    dkv[...] = dot(joined[...], hot[cell, 0], 0, 0)
    close(dqa[...], dkv[...])

    def later_chunk(chunk, carry):
        pltpu.sync_copy(more_ref.at[cell, first_pair + pair, chunk - 1], spill)
        values = kvt_ref[0, 0, chunk, LANES:, :].T
        d_values = jnp.zeros((CHUNK, LANES), F32)
        for side in range(2):
            scaled = spread(chunk, side, None)
            for cut in cuts:
                score_grads(chunk, side, spill, values, cut, scaled)
            d_values += dot(spill[side], oz[side], 1, 1)
            dqa[heads[side], :] += dot(kvt_ref[0, 0, chunk, heads[side], :], ds[side])
        d_keys = jnp.where(lanes, dot(ds[0], queries[...], 1, 1), dot(ds[1], queries[...], 1, 1)) * SCALE
        joined[:, 0:LANES] = d_keys.astype(BF16)
        joined[:, LANES:] = d_values.astype(BF16)
        dkv[...] += dot(joined[...], hot[cell, chunk], 0, 0)
        return carry

    @pl.when(steps > 1)
    def _():
        lax.fori_loop(1, steps, later_chunk, 0)
        close(dqa[...], dkv[...])

    @pl.when(cell == 0)
    def _():
        grad[...] = term[...]

    @pl.when(cell > 0)
    def _():
        grad[...] += term[...]

    @pl.when(cell == cells - 1)
    def _():
        for offset in range(shards):
            owner = me ^ offset
            target = (keep_ref, send_ref)[offset % 2].at[offset // 2, 0]
            rows = pl.ds(pl.multiple_of(owner * block, block), block)
            target[0:block, :] = grad[rows, :].astype(BF16)
            ours = jnp.where(owner == first_pair + pair, 1.0, 0.0)
            target[block:, :] = (grad[width:, :] * ours).astype(BF16)


def attend_back(group, shards, scalars, pos, xt, qkv, kvt, e, more, stats, datt):
    first, count = group
    cells, length = xt.shape[0], xt.shape[2]
    width = xt.shape[1] - ONES
    chunks = kvt.shape[2]
    half = (shards // 2, count, width // shards + EXTRA, TRIPLE)
    part = pl.BlockSpec((shards // 2, 1) + half[2:], lambda p, c, s: (0, p, 0, 0))
    shape = jax.ShapeDtypeStruct
    return pl.pallas_call(
        functools.partial(back_kernel, shards=shards, cells=cells, first_pair=first),
        out_shape=(shape((cells, count, TRIPLE, length), BF16), shape(half, BF16), shape(half, BF16)),
        grid_spec=pltpu.PrefetchScalarGridSpec(
            num_scalar_prefetch=1,
            grid=(count, cells),
            in_specs=[
                pl.BlockSpec((1, 1, length), lambda p, c, s: (c, 0, 0)),
                pl.BlockSpec((1, width + ONES, length), lambda p, c, s: (c, 0, 0)),
                pl.BlockSpec((1, 1, 4 * LANES, length), lambda p, c, s: (c, first + p, 0, 0)),
                pl.BlockSpec((1, 1, chunks, 2 * LANES, CHUNK), lambda p, c, s: (c, first + p, 0, 0, 0)),
                pl.BlockSpec((1, 1, 2, CHUNK, length), lambda p, c, s: (c, first + p, 0, 0, 0)),
                pl.BlockSpec(memory_space=pl.ANY),
                pl.BlockSpec((1, 1, 4 + 2 * chunks, 1, length), lambda p, c, s: (c, first + p, 0, 0, 0)),
                pl.BlockSpec((1, length, LANES), lambda p, c, s: (c, 0, first + p)),
            ],
            out_specs=[
                pl.BlockSpec((1, 1, TRIPLE, length), lambda p, c, s: (c, p, 0, 0)),
                part,
                part,
            ],
            scratch_shapes=[
                pltpu.VMEM((cells, chunks, CHUNK, length), BF16),
                pltpu.VMEM((2, LANES, length), BF16),
                pltpu.VMEM((LANES, length), BF16),
                pltpu.VMEM((2, CHUNK, length), BF16),
                pltpu.VMEM((CHUNK, 2 * LANES), BF16),
                pltpu.VMEM((LANES, length), F32),
                pltpu.VMEM((2 * LANES, length), F32),
                pltpu.VMEM((LANES, length), F32),
                pltpu.VMEM((2 * LANES, length), F32),
                pltpu.VMEM((2, 1, length), F32),
                pltpu.VMEM((width + ONES, TRIPLE), F32),
                pltpu.VMEM((width + ONES, TRIPLE), F32),
                pltpu.VMEM((2, CHUNK, length), BF16),
            ],
        ),
        compiler_params=params(52),
        cost_estimate=cost(cells * count * 6e9, cells * count * 7e6),
        name="attend_back",
    )(scalars, pos, xt, qkv, kvt, e, more, stats, datt)


def input_kernel(w_ref, dhid_ref, *refs):
    parts, out_ref = refs[:-1], refs[-1]
    back, col = None, 0
    for part in parts:
        rows = part.shape[1]
        term = dot(w_ref[:, col : col + rows], part[0])
        back = term if back is None else back + term
        col += rows
    out_ref[0] = (back.T + dhid_ref[0].astype(F32)).astype(BF16)


def input_grad(w, dhid, parts):
    cells, length, width = dhid.shape
    parts = [part.reshape(cells, -1, length) for part in parts]
    block = pl.BlockSpec((1, length, width), lambda i: (i, 0, 0))
    return pl.pallas_call(
        input_kernel,
        out_shape=jax.ShapeDtypeStruct(dhid.shape, BF16),
        grid=(cells,),
        in_specs=[pl.BlockSpec(w.shape, lambda i: (0, 0)), block]
        + [pl.BlockSpec((1,) + part.shape[1:], lambda i: (i, 0, 0)) for part in parts],
        out_specs=block,
        compiler_params=params(48),
        cost_estimate=cost(cells * 2e9, cells * 8e6),
        name="input_grad",
    )(w, dhid, *parts)


def finish_kernel(*refs):
    terms, halves, outs = refs[:2], refs[2:-15], refs[-15:]
    block, width = outs[0].shape
    for which in range(3):
        cols = slice(which * width, (which + 1) * width)
        outs[3 + which][...] = terms[0][0:block, cols].astype(F32) + terms[1][0:block, cols].astype(F32)
    rows = terms[0][block:, 0:block].astype(F32) + terms[1][block:, 0:block].astype(F32)
    for row in range(MIDDLE_VECTORS):
        outs[8 + row][...] = rows[row : row + 1, :].reshape(block)

    def write(order):
        biases = [jnp.zeros((1, LANES), F32), jnp.zeros((1, LANES), F32)]
        pair = 0
        for group in range(0, len(halves), 2):
            for part in [halves[group + i] for i in order]:
                for p in range(part.shape[0]):
                    for which in range(3):
                        cols = slice(which * LANES, (which + 1) * LANES)
                        outs[which][:, pair * LANES : (pair + 1) * LANES] = part[p, 0:block, cols].astype(F32)
                    biases[0] += part[p, block : block + 1, 0:LANES].astype(F32)
                    biases[1] += part[p, block : block + 1, 2 * LANES :].astype(F32)
                    pair += 1
        outs[6][...] = biases[0].reshape(block)
        outs[7][...] = biases[1].reshape(block)

    low = lax.axis_index("dp") % 2 == 0

    @pl.when(low)
    def _():
        write((0, 1))

    @pl.when(jnp.logical_not(low))
    def _():
        write((1, 0))


def finish(parts, block, width):
    vmem = pl.BlockSpec(memory_space=pltpu.VMEM)
    return pl.pallas_call(
        finish_kernel,
        out_shape=(jax.ShapeDtypeStruct((block, width), F32),) * 6 + (jax.ShapeDtypeStruct((block,), F32),) * 9,
        in_specs=[vmem] * len(parts),
        out_specs=[vmem] * 15,
        compiler_params=params(16),
        name="finish",
    )(*parts)


def swap(values, axis, mask):
    size = lax.axis_size(axis)
    return lax.ppermute(values, axis, [(i, i ^ mask) for i in range(size)])


def masks(axis):
    found, mask = [], 1
    while mask < lax.axis_size(axis):
        found.append(mask)
        mask *= 2
    return found


def after(value, *others):
    return lax.optimization_barrier((value,) + others)[0]


def gather_pieces(own, beside):
    held = [own]
    for mask in reversed(masks("fsdp")):
        held = held + [swap(piece, "fsdp", mask) for piece in held]
        held = held[:1] + [after(piece, beside) for piece in held[1:]]
    return held


def plus(left, right):
    return left.astype(F32) + right.astype(F32)


class Reduction:
    def __init__(self, keep, send, half_dim=None):
        self.keep, self.send = keep, send
        self.half_dim = half_dim
        order = masks("dp") if half_dim is not None else reversed(masks("dp"))
        self.plan = [("fsdp", mask) for mask in masks("fsdp")] + [("dp", mask) for mask in order]
        self.low = (lax.axis_index("dp") % 2) == 0

    def pair(self):
        return self.keep, self.send

    def start(self, pair=None):
        if self.plan:
            self.keep, self.send = pair or self.pair()
            self.arrived = swap(self.send, *self.plan[0])

    def arrive(self):
        self.plan = self.plan[1:]
        if not self.plan:
            return
        total = plus(self.keep, self.arrived).astype(BF16)
        axis, mask = self.plan[0]
        if axis == "fsdp":
            self.keep, self.send = total[0::2], total[1::2]
        elif mask == 1 and self.half_dim is not None:
            first, second = jnp.split(total, 2, self.half_dim)
            self.keep = jnp.where(self.low, first, second)
            self.send = jnp.where(self.low, second, first)
        else:
            self.keep = self.send = total

    def finish(self):
        while self.plan:
            self.start()
            self.arrive()
        if self.half_dim is None:
            return self.keep[0], self.arrived[0]
        mine = plus(self.keep, self.arrived).astype(BF16)[0]
        if lax.axis_size("dp") == 1:
            return jnp.split(mine, 2, self.half_dim - 1)
        return mine, swap(mine, "dp", 1)


def body(*args):
    tokens, known_flags, cotangent = args[0], args[1], args[17]
    cells, length, width = tokens.shape
    shards = lax.axis_size("fsdp")
    block = width // shards
    held = offsets(shards)

    early, late, scalars = pack(known_flags, [args[i] for i in SQUARES], [args[i] for i in VECTORS])
    xc, xt, pos = gather_known(scalars, known_flags, tokens)
    early = gather_pieces(early, xt)
    late = after(late, *early[:2])
    late = [late] + [swap(late, "fsdp", offset) for offset in held[1:]]
    w, vec, qkv, kvt, e, more, stats, o = attend(scalars, held, early, xt, xc, pos)
    flat = lambda a: a.reshape(cells * length, width)
    result, dhid, datt, keep, send = middle(
        scalars, held, late, flat(tokens), flat(o), flat(cotangent), vec, cells
    )
    cube = lambda a: a.reshape(cells, length, width)
    chains = [Reduction(keep, send)]

    def boundary(value):
        older, newest = chains[:-1], chains[-1]
        arrived = lax.optimization_barrier([chain.arrived for chain in older])
        for chain, chain.arrived in zip(older, arrived):
            chain.arrive()
        pairs = lax.optimization_barrier([chain.pair() for chain in chains])
        for chain, (chain.keep, chain.send) in zip(chains, pairs):
            pass
        newest.start()
        for chain in older:
            chain.start()
        newest.arrive()
        value, pair = lax.optimization_barrier((value, newest.pair()))
        newest.start(pair)
        return value

    parts = []
    for group in GROUPS:
        dt, keep, send = attend_back(
            group, shards, boundary(scalars), pos, xt, qkv, kvt, e, more, stats, cube(datt)
        )
        parts.append(dt)
        chains.append(Reduction(keep, send, 1))
    tokens_grad = input_grad(boundary(w), cube(dhid), parts)
    tokens_grad, arrived = lax.optimization_barrier((tokens_grad, [chain.arrived for chain in chains]))
    for chain, chain.arrived in zip(chains, arrived):
        chain.arrive()
    newest = chains[-1]
    newest.start()
    newest.arrive()
    chains[0].send = after(chains[0].send, newest.send)
    halves = [half for chain in chains for half in chain.finish()]
    summed = finish(halves, block, width)
    out = dict(zip(SQUARES + VECTORS, summed))
    return (cube(result), tokens_grad) + tuple(out[i] for i in range(2, 17))


def solution(mesh):
    cells = P(("dp", "fsdp"), None, None)
    specs = tuple(P("fsdp", None) if i in SQUARES else P("fsdp") for i in range(2, 17))
    return jax.shard_map(
        body,
        mesh=mesh,
        in_specs=(cells, P(("dp", "fsdp"), None)) + specs + (cells,),
        out_specs=(cells, cells) + specs,
        check_vma=False,
    )
```

```python
import functools

import jax
import jax.numpy as jnp
from jax import lax
from jax.experimental import pallas as pl
from jax.experimental.pallas import tpu as pltpu
from jax.sharding import PartitionSpec as P

H = 8
HD = 64
SCALE = HD ** (-0.5)
NORM_EPSILON = 1e-05
MASK_FILL = -1e30
SAFE_SCORE = 50.0

CHUNK = 672
ROWS = 480
SPLITS = 1
STAGES = 7
ONES = 16
EXTRA = 16
LANES = 128
CUT = 256
LOG2E = 1.4426950408889634
TRIPLE = 3 * LANES
GROUPS = ((0, 2), (2, 2))

F32 = jnp.float32
BF16 = jnp.bfloat16

SQUARES = (2, 4, 5, 7, 11, 13)
VECTORS = (3, 6, 8, 9, 10, 12, 14, 15, 16)
MIDDLE_VECTORS = 7


def dot(left, right, left_dim=1, right_dim=0):
    return lax.dot_general(
        left, right, (((left_dim,), (right_dim,)), ((), ())), preferred_element_type=F32
    )


def params(mebibytes):
    return pltpu.CompilerParams(vmem_limit_bytes=mebibytes << 20)


def cost(flops, moved):
    return pl.CostEstimate(flops=int(flops), bytes_accessed=int(moved), transcendentals=0)


def offsets(shards):
    held, mask = [0], shards // 2
    while mask:
        held = held + [offset ^ mask for offset in held]
        mask //= 2
    return held


def pack_kernel(*refs):
    flags_ref, squares, vectors = refs[0], refs[1:7], refs[7:16]
    early_ref, late_ref, scalars_ref = refs[16:]
    block = squares[0].shape[0]
    for i in range(3):
        early_ref[i * block : (i + 1) * block, :] = squares[i][...]
        late_ref[i * block : (i + 1) * block, :] = squares[3 + i][...]
    rows = [vector[...].astype(F32).reshape(1, -1) for vector in vectors]
    rows = jnp.concatenate(rows + [jnp.zeros((EXTRA - len(rows), block), F32)], axis=0)
    early_ref[3 * block :, :] = jnp.zeros((EXTRA, early_ref.shape[1]), BF16)
    early_ref[3 * block :, 0:block] = rows.astype(BF16)
    flagged = jnp.where(flags_ref[...] > 0, 1.0, 0.0)
    cells = flags_ref.shape[0]
    for cell in range(cells):
        scalars_ref[cell] = jnp.sum(flagged[cell : cell + 1, :]).astype(jnp.int32)
    scalars_ref[cells] = lax.axis_index("fsdp")


def pack(flags, squares, vectors):
    block, width = squares[0].shape
    cells = flags.shape[0]
    vmem = pl.BlockSpec(memory_space=pltpu.VMEM)
    return pl.pallas_call(
        pack_kernel,
        out_shape=(
            jax.ShapeDtypeStruct((3 * block + EXTRA, width), BF16),
            jax.ShapeDtypeStruct((3 * block, width), BF16),
            jax.ShapeDtypeStruct((cells + 1,), jnp.int32),
        ),
        in_specs=[vmem] * 16,
        out_specs=[vmem, vmem, pl.BlockSpec(memory_space=pltpu.SMEM)],
        compiler_params=params(60),
        name="pack",
    )(flags, *squares, *vectors)


def gather_kernel(scalars_ref, flags_ref, x_ref, xc_ref, xt_ref, pos_ref):
    known = scalars_ref[pl.program_id(0)]
    length, width = x_ref.shape[1], x_ref.shape[2]
    flagged = flags_ref[pl.ds(pl.program_id(0), 1), :] > 0
    before = lax.broadcasted_iota(jnp.int32, (length, length), 0)
    after = lax.broadcasted_iota(jnp.int32, (length, length), 1)
    upper = jnp.where(before <= after, 1.0, 0.0).astype(BF16)
    marks = jnp.broadcast_to(jnp.where(flagged, 1.0, 0.0), (16, length)).astype(BF16)
    place = dot(marks, upper)[0:1, :].astype(jnp.int32) - 1
    place = jnp.where(flagged, place, -1)
    pos_ref[0] = place

    for chunk in range(xc_ref.shape[1] // CHUNK):

        @pl.when((chunk == 0) | (chunk * CHUNK < known))
        def _():
            target = chunk * CHUNK + lax.broadcasted_iota(jnp.int32, (CHUNK, length), 0)
            target = jnp.where(known > 0, jnp.minimum(target, known - 1), -2)
            chosen = jnp.where(place == target, 1.0, 0.0).astype(BF16)
            xc_ref[0, chunk * CHUNK : (chunk + 1) * CHUNK, :] = dot(chosen, x_ref[0]).astype(BF16)

    xt_ref[0, 0:width, :] = x_ref[0].T
    xt_ref[0, width:, :] = jnp.ones((ONES, length), BF16)


def gather_known(scalars, flags, x):
    cells, length, width = x.shape
    padded = -(-length // CHUNK) * CHUNK
    one = lambda *shape: pl.BlockSpec((1,) + shape, lambda i, s: (i, 0, 0))
    return pl.pallas_call(
        gather_kernel,
        out_shape=(
            jax.ShapeDtypeStruct((cells, padded, width), BF16),
            jax.ShapeDtypeStruct((cells, width + ONES, length), BF16),
            jax.ShapeDtypeStruct((cells, 1, length), jnp.int32),
        ),
        grid_spec=pltpu.PrefetchScalarGridSpec(
            num_scalar_prefetch=1,
            grid=(cells,),
            in_specs=[pl.BlockSpec(flags.shape, lambda i, s: (0, 0)), one(length, width)],
            out_specs=[one(padded, width), one(width + ONES, length), one(1, length)],
        ),
        compiler_params=params(50),
        cost_estimate=cost(cells * 2e9, cells * 6e6),
        name="gather_known",
    )(scalars, flags, x)


def as_column(row):
    return jnp.broadcast_to(row, (LANES, LANES)).T[:, 0:1]


def attend_kernel(*refs, held, cells):
    scalars_ref, refs = refs[0], refs[1:]
    pieces, refs = refs[: len(held)], refs[len(held) :]
    (
        xt_ref, xc_ref, pos_ref,
        w_ref, vec_ref, qkv_ref, kvt_ref, e_ref, more_ref, stats_ref, o_ref,
        bias, qz, kc, vct, top, own, acc, spill,
    ) = refs
    cell, pair = pl.program_id(0), pl.program_id(1)
    known = scalars_ref[cell]
    me = scalars_ref[cells]
    width, length = w_ref.shape[0], xt_ref.shape[2]
    pairs = width // LANES
    block = width // len(held)

    @pl.when((cell == 0) & (pair == 0))
    def _():
        for offset, piece in zip(held, pieces):
            owner = me ^ offset
            rows = pl.ds(pl.multiple_of(owner * block, block), block)
            for which in range(3):
                for p in range(pairs):
                    col = p * TRIPLE + which * LANES
                    w_ref[rows, col : col + LANES] = piece[
                        which * block : (which + 1) * block, p * LANES : (p + 1) * LANES
                    ]
            vec_ref[:, rows] = piece[3 * block :, 0:block].astype(F32)
        qz[...] = jnp.zeros_like(qz)
        for p in range(pairs):
            cols = slice(p * LANES, (p + 1) * LANES)
            bias[p, :, 0:1] = as_column(vec_ref[0:1, cols])
            bias[p, :, 1:2] = as_column(vec_ref[1:2, cols])

    col = pl.multiple_of(pair * TRIPLE, LANES)
    part = lambda first, count: w_ref[:, pl.ds(col + first * LANES, count * LANES)]
    hidden = pos_ref[0] < 0
    steps = (known + CHUNK - 1) // CHUNK
    value_bias = vec_ref[1:2, pl.ds(pl.multiple_of(pair * LANES, LANES), LANES)]
    tokens = xt_ref[0, 0:width, :]
    heads = [slice(side * HD, (side + 1) * HD) for side in range(2)]
    cuts = [slice(start, min(start + CUT, length)) for start in range(0, length, CUT)]

    def project(chunk):
        rows = pl.ds(pl.multiple_of(chunk * CHUNK, 16), CHUNK)
        packed = dot(xc_ref[0, rows, :], part(1, 2))
        yield
        row = chunk * CHUNK + lax.broadcasted_iota(jnp.int32, (CHUNK, LANES), 0)
        keys = packed[:, 0:LANES]
        kc[...] = keys.astype(BF16)
        kvt_ref[0, 0, chunk, 0:LANES, :] = jnp.where(row < known, keys, 0.0).astype(BF16).T
        yield
        values = packed[:, LANES:] + value_bias
        values = jnp.where(row < known, values, 0.0).astype(BF16).T
        kvt_ref[0, 0, chunk, LANES:, :] = values
        counted = chunk * CHUNK + lax.broadcasted_iota(jnp.int32, (EXTRA, CHUNK), 1)
        counted = jnp.where(counted < known, 1.0, 0.0).astype(BF16)
        for side in range(2):
            vct[side, 0:HD, :] = values[heads[side], :]
            vct[side, HD:, :] = counted
        yield

    def begin(side, shifted):
        weight = jnp.ones((1, length), F32) if shifted else jnp.exp(own[side])
        weight = jnp.where(hidden, weight, 0.0).astype(BF16).astype(F32)
        top[side] = jnp.where(hidden, own[side], MASK_FILL) if shifted else jnp.zeros((1, length), F32)
        return weight

    def own_values(side):
        return qkv_ref[0, 0, 2 * LANES + side * HD : 2 * LANES + (side + 1) * HD, :].astype(F32)

    def measure(side):
        q = qkv_ref[0, 0, heads[side], :].astype(F32)
        k = qkv_ref[0, 0, LANES + side * HD : LANES + (side + 1) * HD, :].astype(F32)
        own[side] = jnp.sum(q * k, axis=0, keepdims=True) * SCALE
        longest_q = jnp.max(jnp.sum(q * q, axis=0, keepdims=True))
        longest_k = jnp.max(jnp.sum(k * k, axis=0, keepdims=True))
        return longest_q * longest_k < (SAFE_SCORE / SCALE) * (SAFE_SCORE / SCALE)

    def conclude(side):
        total = acc[side, HD : HD + 1, :]
        rows = slice(TRIPLE + side * HD, TRIPLE + (side + 1) * HD)
        qkv_ref[0, 0, rows, :] = (acc[side, 0:HD, :] * (1.0 / total)).astype(BF16)
        stats_ref[0, 0, side] = top[side] + jnp.log(total)
        stats_ref[0, 0, 2 + side] = own[side]

    first = project(0)
    next(first)
    turned = dot(part(0, 1), tokens, 0, 0)
    next(first)
    queries = (turned + bias[pair, :, 0:1]).astype(BF16)
    turned = dot(part(1, 2), tokens, 0, 0)
    qkv_ref[0, 0, 0:LANES, :] = queries
    for side in range(2):
        qz[side, heads[side], :] = queries[heads[side], :]
    next(first)
    qkv_ref[0, 0, LANES : 2 * LANES, :] = turned[0:LANES, :].astype(BF16)
    weights = []
    safe = None
    for side in range(2):
        for cut in cuts:
            scores = dot(kc[...], qz[side, :, cut])
            e_ref[0, 0, side, :, cut] = jnp.exp2(scores * (SCALE * LOG2E)).astype(BF16)
            if side == 0 and cut is cuts[0]:
                qkv_ref[0, 0, 2 * LANES : TRIPLE, :] = (turned[LANES:, :] + bias[pair, :, 1:2]).astype(BF16)
            if cut is cuts[1]:
                bounded = measure(side)
                safe = bounded if safe is None else safe & bounded
                weights.append(begin(side, False))
        total = dot(vct[side], e_ref[0, 0, side])
        acc[side, 0:HD, :] = total[0:HD, :] + weights[side] * own_values(side)
        acc[side, HD:, :] = total[HD:, :] + weights[side]
    for side in range(2):
        conclude(side)
        stats_ref[0, 0, 4 + side] = top[side]
    o_ref[0] = qkv_ref[0, 0, TRIPLE:, :].T

    def weigh(chunk, side, exps, shifted):
        scores = dot(kc[...], qz[side]) * SCALE
        if shifted:
            peak = jnp.maximum(top[side], jnp.max(scores, axis=0, keepdims=True))
            peak = jnp.where(known > 0, peak, top[side])
            scores = jnp.minimum(scores - peak, 0.0)
        probs = jnp.exp(scores).astype(BF16)
        exps[side] = probs
        if shifted:
            acc[side] = acc[side] * jnp.exp(top[side] - peak) + dot(vct[side], probs)
            top[side] = peak
        else:
            acc[side] += dot(vct[side], probs)
        stats_ref[0, 0, 4 + 2 * chunk + side] = top[side]

    @pl.when(jnp.logical_not(safe))
    def _():
        for side in range(2):
            weight = begin(side, True)
            acc[side, 0:HD, :] = weight * own_values(side)
            acc[side, HD:, :] = jnp.broadcast_to(weight, (EXTRA, length))
            weigh(0, side, e_ref.at[0, 0], True)

    def later_chunk(chunk, carry):
        for _ in project(chunk):
            pass

        @pl.when(safe)
        def _():
            for side in range(2):
                weigh(chunk, side, spill, False)

        @pl.when(jnp.logical_not(safe))
        def _():
            for side in range(2):
                weigh(chunk, side, spill, True)

        pltpu.sync_copy(spill, more_ref.at[cell, pair, chunk - 1])
        return carry

    lax.fori_loop(1, steps, later_chunk, 0)

    @pl.when(jnp.logical_not(safe) | (steps > 1))
    def _():
        for side in range(2):
            conclude(side)
        o_ref[0] = qkv_ref[0, 0, TRIPLE:, :].T


def attend(scalars, held, pieces, xt, xc, pos):
    cells, length = xt.shape[0], xt.shape[2]
    width = xt.shape[1] - ONES
    padded = xc.shape[1]
    pairs = width // LANES
    chunks = padded // CHUNK
    full = lambda *shape: pl.BlockSpec(shape, lambda c, p, s: (0,) * len(shape))
    shape = jax.ShapeDtypeStruct
    return pl.pallas_call(
        functools.partial(attend_kernel, held=held, cells=cells),
        out_shape=(
            shape((width, 3 * width), BF16),
            shape((EXTRA, width), F32),
            shape((cells, pairs, 4 * LANES, length), BF16),
            shape((cells, pairs, chunks, 2 * LANES, CHUNK), BF16),
            shape((cells, pairs, 2, CHUNK, length), BF16),
            shape((cells, pairs, max(chunks - 1, 1), 2, CHUNK, length), BF16),
            shape((cells, pairs, 4 + 2 * chunks, 1, length), F32),
            shape((cells, length, width), BF16),
        ),
        grid_spec=pltpu.PrefetchScalarGridSpec(
            num_scalar_prefetch=1,
            grid=(cells, pairs),
            in_specs=[full(*piece.shape) for piece in pieces]
            + [
                pl.BlockSpec((1, width + ONES, length), lambda c, p, s: (c, 0, 0)),
                pl.BlockSpec((1, padded, width), lambda c, p, s: (c, 0, 0)),
                pl.BlockSpec((1, 1, length), lambda c, p, s: (c, 0, 0)),
            ],
            out_specs=[
                full(width, 3 * width),
                full(EXTRA, width),
                pl.BlockSpec((1, 1, 4 * LANES, length), lambda c, p, s: (c, p, 0, 0)),
                pl.BlockSpec((1, 1, chunks, 2 * LANES, CHUNK), lambda c, p, s: (c, p, 0, 0, 0)),
                pl.BlockSpec((1, 1, 2, CHUNK, length), lambda c, p, s: (c, p, 0, 0, 0)),
                pl.BlockSpec(memory_space=pl.ANY),
                pl.BlockSpec((1, 1, 4 + 2 * chunks, 1, length), lambda c, p, s: (c, p, 0, 0, 0)),
                pl.BlockSpec((1, length, LANES), lambda c, p, s: (c, 0, p)),
            ],
            scratch_shapes=[
                pltpu.VMEM((pairs, LANES, 8), F32),
                pltpu.VMEM((2, LANES, length), BF16),
                pltpu.VMEM((CHUNK, LANES), BF16),
                pltpu.VMEM((2, HD + EXTRA, CHUNK), BF16),
                pltpu.VMEM((2, 1, length), F32),
                pltpu.VMEM((2, 1, length), F32),
                pltpu.VMEM((2, HD + EXTRA, length), F32),
                pltpu.VMEM((2, CHUNK, length), BF16),
            ],
        ),
        compiler_params=params(52),
        cost_estimate=cost(cells * 1e10, cells * 2.5e7),
        name="attend",
    )(scalars, *pieces, xt, xc, pos)


def row_mean(rows):
    return jnp.mean(rows, axis=-1, keepdims=True)


def normalize(rows):
    centred = rows - row_mean(rows)
    scale = lax.rsqrt(row_mean(centred * centred) + NORM_EPSILON)
    return centred * scale, scale


def norm_back(grad, normed, scale):
    return scale * (grad - row_mean(grad) - normed * row_mean(grad * normed))


def column_sum(rows):
    return jnp.sum(rows, axis=0, keepdims=True)


def middle_kernel(*refs, held, cells):
    scalars_ref, refs = refs[0], refs[1:]
    pieces, refs = refs[: len(held)], refs[len(held) :]
    (
        x_ref, o_ref, cot_ref, vec_ref,
        result_ref, dhid_ref, datt_ref, keep_ref, send_ref,
        w, go, gu, gd, gvec,
    ) = refs
    me = scalars_ref[cells]
    width = x_ref.shape[1]
    block = width // len(held)

    @pl.when(pl.program_id(0) == 0)
    def _():
        for offset, piece in zip(held, pieces):
            rows = pl.ds(pl.multiple_of((me ^ offset) * block, block), block)
            for which in range(3):
                w[which, rows, :] = piece[which * block : (which + 1) * block, :]
        go[...] = jnp.zeros_like(go)
        gu[...] = jnp.zeros_like(gu)
        gd[...] = jnp.zeros_like(gd)
        gvec[...] = jnp.zeros_like(gvec)

    def stages(rows):
        out_bias, gain_one, shift_one, up_bias, down_bias, gain_two, shift_two = (
            vec_ref[2 + i : 3 + i, :] for i in range(MIDDLE_VECTORS)
        )
        attended = o_ref[rows, :]
        product = dot(attended, w[0])
        yield
        norm_one, scale_one = normalize(x_ref[rows, :].astype(F32) + (product + out_bias))
        first_norm = norm_one * gain_one + shift_one
        first_low = first_norm.astype(BF16)
        product = dot(first_low, w[1])
        yield
        pre_act = product + up_bias
        below = 0.5 * (1.0 + lax.erf(pre_act * (0.5**0.5)))
        activated = (pre_act * below).astype(BF16)
        product = dot(activated, w[2])
        slope = below + pre_act * (jnp.exp2(pre_act * pre_act * (-0.5 * LOG2E)) * 0.3989422804014327)
        yield
        norm_two, scale_two = normalize(first_norm + (product + down_bias))
        result_ref[rows, :] = (norm_two * gain_two + shift_two).astype(BF16)
        dy = cot_ref[rows, :].astype(F32)
        d_second = norm_back(dy * gain_two, norm_two, scale_two)
        d_ff = d_second.astype(BF16)
        product = dot(d_ff, w[2], 1, 1)
        gvec[4:5, :] += column_sum(d_ff.astype(F32))
        gvec[5:6, :] += column_sum(dy * norm_two)
        gvec[6:7, :] += column_sum(dy)
        yield
        d_pre = (product * slope).astype(BF16)
        product = dot(d_pre, w[1], 1, 1)
        gd[...] += dot(activated, d_ff, 0, 0)
        gvec[3:4, :] += column_sum(d_pre.astype(F32))
        yield
        d_first = d_second + product
        d_hidden = norm_back(d_first * gain_one, norm_one, scale_one)
        d_attn = d_hidden.astype(BF16)
        dhid_ref[rows, :] = d_attn
        product = dot(d_attn, w[0], 1, 1)
        gu[...] += dot(first_low, d_pre, 0, 0)
        gvec[0:1, :] += column_sum(d_attn.astype(F32))
        gvec[1:2, :] += column_sum(d_first * norm_one)
        gvec[2:3, :] += column_sum(d_first)
        yield
        datt_ref[rows, :] = product.astype(BF16)
        go[...] += dot(attended, d_attn, 0, 0)
        yield

    step = x_ref.shape[0] // SPLITS
    live = [stages(slice(i * step, (i + 1) * step)) for i in range(SPLITS)]
    for turn in range(STAGES + SPLITS - 1):
        for i, part in enumerate(live):
            if 0 <= turn - i < STAGES:
                next(part)

    @pl.when(pl.program_id(0) == pl.num_programs(0) - 1)
    def _():
        for offset in range(len(held)):
            target = (keep_ref, send_ref)[offset % 2].at[offset // 2]
            rows = pl.ds(pl.multiple_of((me ^ offset) * block, block), block)
            for which, grad in enumerate((go, gu, gd)):
                cols = slice(which * width, (which + 1) * width)
                target[0:block, cols] = grad[rows, :].astype(BF16)
            target[block:, :] = jnp.zeros((EXTRA, 3 * width), BF16)
            target[block:, 0:block] = gvec[:, rows].astype(BF16)


def middle(scalars, held, pieces, x, o, cot, vec, cells):
    rows, width = x.shape
    step = ROWS if rows % ROWS == 0 else rows
    block = pl.BlockSpec((step, width), lambda i, s: (i, 0))
    full = lambda *shape: pl.BlockSpec(shape, lambda i, s: (0,) * len(shape))
    low = jax.ShapeDtypeStruct((rows, width), BF16)
    half = (len(held) // 2, width // len(held) + EXTRA, 3 * width)
    return pl.pallas_call(
        functools.partial(middle_kernel, held=held, cells=cells),
        out_shape=(low, low, low, jax.ShapeDtypeStruct(half, BF16), jax.ShapeDtypeStruct(half, BF16)),
        grid_spec=pltpu.PrefetchScalarGridSpec(
            num_scalar_prefetch=1,
            grid=(rows // step,),
            in_specs=[full(*piece.shape) for piece in pieces] + [block, block, block, full(EXTRA, width)],
            out_specs=[block, block, block, full(*half), full(*half)],
            scratch_shapes=[
                pltpu.VMEM((3, width, width), BF16),
                pltpu.VMEM((width, width), F32),
                pltpu.VMEM((width, width), F32),
                pltpu.VMEM((width, width), F32),
                pltpu.VMEM((EXTRA, width), F32),
            ],
        ),
        compiler_params=params(50),
        cost_estimate=cost(rows * 5e6, rows * 8e3),
        name="middle",
    )(scalars, *pieces, x, o, cot, vec)


def back_kernel(
    scalars_ref, pos_ref, xt_ref, qkv_ref, kvt_ref, e_ref, more_ref, stats_ref, datt_ref,
    dt_ref, keep_ref, send_ref,
    hot, oz, og, ds, joined, dqa, dkv, self_q, self_kv, delta, grad, term, spill,
    *, shards, cells, first_pair,
):
    pair, cell = pl.program_id(0), pl.program_id(1)
    known = scalars_ref[cell]
    me = scalars_ref[cells]
    width, length = xt_ref.shape[1] - ONES, xt_ref.shape[2]
    block = width // shards
    steps = (known + CHUNK - 1) // CHUNK
    place = pos_ref[0]
    hidden = place < 0

    @pl.when(pair == 0)
    def _():
        hot[cell, 0] = jnp.where(
            place == lax.broadcasted_iota(jnp.int32, (CHUNK, length), 0), 1.0, 0.0
        ).astype(BF16)

        def mark(chunk, carry):
            row = chunk * CHUNK + lax.broadcasted_iota(jnp.int32, (CHUNK, length), 0)
            hot[cell, chunk] = jnp.where(place == row, 1.0, 0.0).astype(BF16)
            return carry

        lax.fori_loop(1, steps, mark, 0)

    heads = [slice(side * HD, (side + 1) * HD) for side in range(2)]
    cuts = [slice(start, min(start + CUT, length)) for start in range(0, length, CUT)]
    queries = qkv_ref.at[0, 0, 0:LANES]

    @pl.when((pair == 0) & (cell == 0))
    def _():
        oz[...] = jnp.zeros_like(oz)

    og[...] = datt_ref[0].T

    def share(chunk, side):
        return jnp.exp(stats_ref[0, 0, 4 + 2 * chunk + side] - stats_ref[0, 0, side])

    def outset(side):
        rows = heads[side]
        grads = og[rows, :].astype(F32)
        query = queries[rows, :].astype(F32) * SCALE
        key = qkv_ref[0, 0, LANES + side * HD : LANES + (side + 1) * HD, :].astype(F32)
        value = qkv_ref[0, 0, 2 * LANES + side * HD : 2 * LANES + (side + 1) * HD, :].astype(F32)
        prob = jnp.exp(jnp.where(hidden, stats_ref[0, 0, 2 + side], MASK_FILL) - stats_ref[0, 0, side])
        own_grad = jnp.sum(grads * value, axis=0, keepdims=True)
        back = (prob * (own_grad - delta[side])).astype(BF16).astype(F32)
        self_q[rows, :] = back * key
        self_kv[rows, :] = back * query
        self_kv[LANES + side * HD : LANES + (side + 1) * HD, :] = prob.astype(BF16).astype(F32) * grads

    def score_grads(chunk, side, exps, values, cut, scaled):
        part = dot(values, oz[side, :, cut]) - scaled[:, cut]
        ds[side, :, cut] = (exps[side, :, cut].astype(F32) * part).astype(BF16)

    def spread(chunk, side, part):
        scaled = share(chunk, side)
        oz[side, heads[side], :] = (og[heads[side], :].astype(F32) * scaled).astype(BF16)
        return delta[side] * scaled

    def close(q_part, kv_part):
        dt_ref[0, 0, 0:LANES, :] = ((q_part + self_q[...]) * SCALE).astype(BF16)
        dt_ref[0, 0, LANES:, :] = (kv_part + self_kv[...]).astype(BF16)
        term[...] = dot(xt_ref[0], dt_ref[0, 0], 1, 1)

    exps = e_ref.at[0, 0]
    values = kvt_ref[0, 0, 0, LANES:, :].T
    for side in range(2):
        rows = heads[side]
        delta[side] = jnp.sum(
            og[rows, :].astype(F32)
            * qkv_ref[0, 0, TRIPLE + side * HD : TRIPLE + (side + 1) * HD, :].astype(F32),
            axis=0,
            keepdims=True,
        )
    scaled = [spread(0, side, None) for side in range(2)]
    for cut in cuts:
        score_grads(0, 0, exps, values, cut, scaled[0])
    d_values = dot(exps[0], oz[0], 1, 1)
    outset(0)
    for cut in cuts:
        score_grads(0, 1, exps, values, cut, scaled[1])
    d_keys = dot(ds[0], queries[...], 1, 1)
    outset(1)
    d_values += dot(exps[1], oz[1], 1, 1)
    lanes = lax.broadcasted_iota(jnp.int32, (CHUNK, LANES), 1) < HD
    joined[:, LANES:] = d_values.astype(BF16)
    dqa[0:HD, :] = dot(kvt_ref[0, 0, 0, 0:HD, :], ds[0])
    d_keys = jnp.where(lanes, d_keys, dot(ds[1], queries[...], 1, 1)) * SCALE
    dqa[HD:, :] = dot(kvt_ref[0, 0, 0, HD:LANES, :], ds[1])
    joined[:, 0:LANES] = d_keys.astype(BF16)
    dkv[...] = dot(joined[...], hot[cell, 0], 0, 0)
    close(dqa[...], dkv[...])

    def later_chunk(chunk, carry):
        pltpu.sync_copy(more_ref.at[cell, first_pair + pair, chunk - 1], spill)
        values = kvt_ref[0, 0, chunk, LANES:, :].T
        d_values = jnp.zeros((CHUNK, LANES), F32)
        for side in range(2):
            scaled = spread(chunk, side, None)
            for cut in cuts:
                score_grads(chunk, side, spill, values, cut, scaled)
            d_values += dot(spill[side], oz[side], 1, 1)
            dqa[heads[side], :] += dot(kvt_ref[0, 0, chunk, heads[side], :], ds[side])
        d_keys = jnp.where(lanes, dot(ds[0], queries[...], 1, 1), dot(ds[1], queries[...], 1, 1)) * SCALE
        joined[:, 0:LANES] = d_keys.astype(BF16)
        joined[:, LANES:] = d_values.astype(BF16)
        dkv[...] += dot(joined[...], hot[cell, chunk], 0, 0)
        return carry

    @pl.when(steps > 1)
    def _():
        lax.fori_loop(1, steps, later_chunk, 0)
        close(dqa[...], dkv[...])

    @pl.when(cell == 0)
    def _():
        grad[...] = term[...]

    @pl.when(cell > 0)
    def _():
        grad[...] += term[...]

    @pl.when(cell == cells - 1)
    def _():
        for offset in range(shards):
            owner = me ^ offset
            target = (keep_ref, send_ref)[offset % 2].at[offset // 2, 0]
            rows = pl.ds(pl.multiple_of(owner * block, block), block)
            target[0:block, :] = grad[rows, :].astype(BF16)
            ours = jnp.where(owner == first_pair + pair, 1.0, 0.0)
            target[block:, :] = (grad[width:, :] * ours).astype(BF16)


def attend_back(group, shards, scalars, pos, xt, qkv, kvt, e, more, stats, datt):
    first, count = group
    cells, length = xt.shape[0], xt.shape[2]
    width = xt.shape[1] - ONES
    chunks = kvt.shape[2]
    half = (shards // 2, count, width // shards + EXTRA, TRIPLE)
    part = pl.BlockSpec((shards // 2, 1) + half[2:], lambda p, c, s: (0, p, 0, 0))
    shape = jax.ShapeDtypeStruct
    return pl.pallas_call(
        functools.partial(back_kernel, shards=shards, cells=cells, first_pair=first),
        out_shape=(shape((cells, count, TRIPLE, length), BF16), shape(half, BF16), shape(half, BF16)),
        grid_spec=pltpu.PrefetchScalarGridSpec(
            num_scalar_prefetch=1,
            grid=(count, cells),
            in_specs=[
                pl.BlockSpec((1, 1, length), lambda p, c, s: (c, 0, 0)),
                pl.BlockSpec((1, width + ONES, length), lambda p, c, s: (c, 0, 0)),
                pl.BlockSpec((1, 1, 4 * LANES, length), lambda p, c, s: (c, first + p, 0, 0)),
                pl.BlockSpec((1, 1, chunks, 2 * LANES, CHUNK), lambda p, c, s: (c, first + p, 0, 0, 0)),
                pl.BlockSpec((1, 1, 2, CHUNK, length), lambda p, c, s: (c, first + p, 0, 0, 0)),
                pl.BlockSpec(memory_space=pl.ANY),
                pl.BlockSpec((1, 1, 4 + 2 * chunks, 1, length), lambda p, c, s: (c, first + p, 0, 0, 0)),
                pl.BlockSpec((1, length, LANES), lambda p, c, s: (c, 0, first + p)),
            ],
            out_specs=[
                pl.BlockSpec((1, 1, TRIPLE, length), lambda p, c, s: (c, p, 0, 0)),
                part,
                part,
            ],
            scratch_shapes=[
                pltpu.VMEM((cells, chunks, CHUNK, length), BF16),
                pltpu.VMEM((2, LANES, length), BF16),
                pltpu.VMEM((LANES, length), BF16),
                pltpu.VMEM((2, CHUNK, length), BF16),
                pltpu.VMEM((CHUNK, 2 * LANES), BF16),
                pltpu.VMEM((LANES, length), F32),
                pltpu.VMEM((2 * LANES, length), F32),
                pltpu.VMEM((LANES, length), F32),
                pltpu.VMEM((2 * LANES, length), F32),
                pltpu.VMEM((2, 1, length), F32),
                pltpu.VMEM((width + ONES, TRIPLE), F32),
                pltpu.VMEM((width + ONES, TRIPLE), F32),
                pltpu.VMEM((2, CHUNK, length), BF16),
            ],
        ),
        compiler_params=params(52),
        cost_estimate=cost(cells * count * 6e9, cells * count * 7e6),
        name="attend_back",
    )(scalars, pos, xt, qkv, kvt, e, more, stats, datt)


def input_kernel(w_ref, dhid_ref, *refs):
    parts, out_ref = refs[:-1], refs[-1]
    back, col = None, 0
    for part in parts:
        rows = part.shape[1]
        term = dot(w_ref[:, col : col + rows], part[0])
        back = term if back is None else back + term
        col += rows
    out_ref[0] = (back.T + dhid_ref[0].astype(F32)).astype(BF16)


def input_grad(w, dhid, parts):
    cells, length, width = dhid.shape
    parts = [part.reshape(cells, -1, length) for part in parts]
    block = pl.BlockSpec((1, length, width), lambda i: (i, 0, 0))
    return pl.pallas_call(
        input_kernel,
        out_shape=jax.ShapeDtypeStruct(dhid.shape, BF16),
        grid=(cells,),
        in_specs=[pl.BlockSpec(w.shape, lambda i: (0, 0)), block]
        + [pl.BlockSpec((1,) + part.shape[1:], lambda i: (i, 0, 0)) for part in parts],
        out_specs=block,
        compiler_params=params(48),
        cost_estimate=cost(cells * 2e9, cells * 8e6),
        name="input_grad",
    )(w, dhid, *parts)


def finish_kernel(*refs):
    terms, halves, outs = refs[:2], refs[2:-15], refs[-15:]
    block, width = outs[0].shape
    for which in range(3):
        cols = slice(which * width, (which + 1) * width)
        outs[3 + which][...] = terms[0][0:block, cols].astype(F32) + terms[1][0:block, cols].astype(F32)
    rows = terms[0][block:, 0:block].astype(F32) + terms[1][block:, 0:block].astype(F32)
    for row in range(MIDDLE_VECTORS):
        outs[8 + row][...] = rows[row : row + 1, :].reshape(block)

    def write(order):
        biases = [jnp.zeros((1, LANES), F32), jnp.zeros((1, LANES), F32)]
        pair = 0
        for group in range(0, len(halves), 2):
            for part in [halves[group + i] for i in order]:
                for p in range(part.shape[0]):
                    for which in range(3):
                        cols = slice(which * LANES, (which + 1) * LANES)
                        outs[which][:, pair * LANES : (pair + 1) * LANES] = part[p, 0:block, cols].astype(F32)
                    biases[0] += part[p, block : block + 1, 0:LANES].astype(F32)
                    biases[1] += part[p, block : block + 1, 2 * LANES :].astype(F32)
                    pair += 1
        outs[6][...] = biases[0].reshape(block)
        outs[7][...] = biases[1].reshape(block)

    low = lax.axis_index("dp") % 2 == 0

    @pl.when(low)
    def _():
        write((0, 1))

    @pl.when(jnp.logical_not(low))
    def _():
        write((1, 0))


def finish(parts, block, width):
    vmem = pl.BlockSpec(memory_space=pltpu.VMEM)
    return pl.pallas_call(
        finish_kernel,
        out_shape=(jax.ShapeDtypeStruct((block, width), F32),) * 6 + (jax.ShapeDtypeStruct((block,), F32),) * 9,
        in_specs=[vmem] * len(parts),
        out_specs=[vmem] * 15,
        compiler_params=params(16),
        name="finish",
    )(*parts)


def swap(values, axis, mask):
    size = lax.axis_size(axis)
    return lax.ppermute(values, axis, [(i, i ^ mask) for i in range(size)])


def masks(axis):
    found, mask = [], 1
    while mask < lax.axis_size(axis):
        found.append(mask)
        mask *= 2
    return found


def after(value, *others):
    return lax.optimization_barrier((value,) + others)[0]


def gather_pieces(own, beside):
    held = [own]
    for mask in reversed(masks("fsdp")):
        held = held + [swap(piece, "fsdp", mask) for piece in held]
        held = held[:1] + [after(piece, beside) for piece in held[1:]]
    return held


def plus(left, right):
    return left.astype(F32) + right.astype(F32)


class Reduction:
    def __init__(self, keep, send, half_dim=None):
        self.keep, self.send = keep, send
        self.half_dim = half_dim
        order = masks("dp") if half_dim is not None else reversed(masks("dp"))
        self.plan = [("fsdp", mask) for mask in masks("fsdp")] + [("dp", mask) for mask in order]
        self.low = (lax.axis_index("dp") % 2) == 0

    def pair(self):
        return self.keep, self.send

    def start(self, pair=None):
        if self.plan:
            self.keep, self.send = pair or self.pair()
            self.arrived = swap(self.send, *self.plan[0])

    def arrive(self):
        self.plan = self.plan[1:]
        if not self.plan:
            return
        total = plus(self.keep, self.arrived).astype(BF16)
        axis, mask = self.plan[0]
        if axis == "fsdp":
            self.keep, self.send = total[0::2], total[1::2]
        elif mask == 1 and self.half_dim is not None:
            first, second = jnp.split(total, 2, self.half_dim)
            self.keep = jnp.where(self.low, first, second)
            self.send = jnp.where(self.low, second, first)
        else:
            self.keep = self.send = total

    def finish(self):
        while self.plan:
            self.start()
            self.arrive()
        if self.half_dim is None:
            return self.keep[0], self.arrived[0]
        mine = plus(self.keep, self.arrived).astype(BF16)[0]
        if lax.axis_size("dp") == 1:
            return jnp.split(mine, 2, self.half_dim - 1)
        return mine, swap(mine, "dp", 1)


def body(*args):
    tokens, known_flags, cotangent = args[0], args[1], args[17]
    cells, length, width = tokens.shape
    shards = lax.axis_size("fsdp")
    block = width // shards
    held = offsets(shards)

    early, late, scalars = pack(known_flags, [args[i] for i in SQUARES], [args[i] for i in VECTORS])
    xc, xt, pos = gather_known(scalars, known_flags, tokens)
    early = gather_pieces(early, xt)
    late = after(late, *early[:2])
    late = [late] + [swap(late, "fsdp", offset) for offset in held[1:]]
    w, vec, qkv, kvt, e, more, stats, o = attend(scalars, held, early, xt, xc, pos)
    flat = lambda a: a.reshape(cells * length, width)
    result, dhid, datt, keep, send = middle(
        scalars, held, late, flat(tokens), flat(o), flat(cotangent), vec, cells
    )
    cube = lambda a: a.reshape(cells, length, width)
    chains = [Reduction(keep, send)]

    def boundary(value):
        older, newest = chains[:-1], chains[-1]
        arrived = lax.optimization_barrier([chain.arrived for chain in older])
        for chain, chain.arrived in zip(older, arrived):
            chain.arrive()
        pairs = lax.optimization_barrier([chain.pair() for chain in chains])
        for chain, (chain.keep, chain.send) in zip(chains, pairs):
            pass
        newest.start()
        for chain in older:
            chain.start()
        newest.arrive()
        value, pair = lax.optimization_barrier((value, newest.pair()))
        newest.start(pair)
        return value

    parts = []
    for group in GROUPS:
        dt, keep, send = attend_back(
            group, shards, boundary(scalars), pos, xt, qkv, kvt, e, more, stats, cube(datt)
        )
        parts.append(dt)
        chains.append(Reduction(keep, send, 1))
    tokens_grad = input_grad(boundary(w), cube(dhid), parts)
    tokens_grad, arrived = lax.optimization_barrier((tokens_grad, [chain.arrived for chain in chains]))
    for chain, chain.arrived in zip(chains, arrived):
        chain.arrive()
    newest = chains[-1]
    newest.start()
    newest.arrive()
    chains[0].send = after(chains[0].send, newest.send)
    halves = [half for chain in chains for half in chain.finish()]
    summed = finish(halves, block, width)
    out = dict(zip(SQUARES + VECTORS, summed))
    return (cube(result), tokens_grad) + tuple(out[i] for i in range(2, 17))


def solution(mesh):
    cells = P(("dp", "fsdp"), None, None)
    specs = tuple(P("fsdp", None) if i in SQUARES else P("fsdp") for i in range(2, 17))
    return jax.shard_map(
        body,
        mesh=mesh,
        in_specs=(cells, P(("dp", "fsdp"), None)) + specs + (cells,),
        out_specs=(cells, cells) + specs,
        check_vma=False,
    )
```
